256 devices in a mesh: comp: 4 (over x), tile: 32 (over y, z), lev: 2 (over core).
Axes of the slice: x: 4, y: 4, z: 8, core: 2. Of those that a mesh axis runs over, the one named last changes fastest.
Arguments:
- atm_state: float32 [2, 48, 256, 2304], P(None, None, ('comp', 'tile'), 'lev'), may hold values from -6 to 6
- atm_diffusion: float32 [48], replicated, may hold values from 0.04 to 0.2
- atm_surface_coef: float32 [2, 256, 2304], P(None, ('comp', 'tile'), 'lev'), may hold values from 0.03 to 0.3
- ocn_state: float32 [2, 24, 512, 3584], P(None, None, ('comp', 'tile'), 'lev'), may hold values from -6 to 6
- ocn_diffusion: float32 [24], replicated, may hold values from 0.03 to 0.2
- sea_mask: int32 [512, 3584], P(('comp', 'tile'), 'lev'), may hold values 0 or 1
- atm_pair_cols: int32 [2, 128, 128, 512], P('lev', ('comp', 'tile')), may hold values from 0 to 2303, as said below
- a2o_weights: float32 [2, 128, 128, 512], P('lev', ('comp', 'tile')), as said below
- ocn_pair_cells: int32 [2, 128, 128, 512], P('lev', ('comp', 'tile')), may hold values from 0 to 7167, as said below
- o2a_weights: float32 [2, 128, 128, 512], P('lev', ('comp', 'tile')), as said below
Outputs:
- atm_next: float32 [2, 48, 256, 2304], P(None, None, ('comp', 'tile'), 'lev')
- ocean_next: float32 [2, 24, 512, 3584], P(None, None, ('comp', 'tile'), 'lev')
The draws below stay inside these ranges and needn't reach their ends.
Inputs may be any that keep to these rules, and one draw needn't show every extreme that they name: `atm_pair_cols`: entry [l, s, d, k] is a local column i * 1152 + j of the atmosphere block at lev index l and comp+tile index s. Every (l, s, d) has 1 to 512 live entries in its first slots; all other slots are padding with index 0. In every draw some ocean block receives 512 live entries from every atmosphere block at its lev index, and some atmosphere block sends 512 to every ocean block. `ocn_pair_cells`: entry [l, d, s, k] is the local ocean cell r * 1792 + c of block (l, d) for the margin that atm_pair_cols holds at [l, s, d, k]; padding slots hold 0. `a2o_weights`: entry [l, s, d, k] belongs to the margin of atm_pair_cols[l, s, d, k]; exactly 0 on padding slots. `o2a_weights`: entry [l, d, s, k] belongs to the margin of ocn_pair_cells[l, d, s, k]; exactly 0 on padding slots.
All inputs are finite; a program needn't handle non-finite values. No bound on the sum of `sea_mask` on one device may be relied on, other than what follows from the above.
Results may differ from the reference program's by a relative error of at most 0.00002.
Values sent between devices are 32-bit elements; how exact they have to be, the bound alone decides.
No kernel may reach another device: no remote copies, remote signals or barrier semaphores. Data moves between devices by JAX's collectives and lax.ppermute only.
A program may use at most 128 MiB of HBM per device.

```python
import math
import jax
import jax.numpy as jnp

ACOL_DEV = 2
ALONG = 2304
LA = 48
OROW_DEV = 4
OLON = 3584
LO = 24
SLOT = 512
ASTEPS = 4
OSTEPS = 2
GROUP = 128
AWIDE = 256
OLAT = 512
ATM_COLS = 2304
OCN_CELLS = 7168
N_LEV = 2


def live_slots(key):
    counts = jax.random.randint(jax.random.fold_in(key, 11), (N_LEV, GROUP, GROUP), 1, SLOT + 1)
    full_dst = jax.random.randint(jax.random.fold_in(key, 12), (N_LEV, 1, 1), 0, GROUP)
    full_src = jax.random.randint(jax.random.fold_in(key, 13), (N_LEV, 1, 1), 0, GROUP)
    src_ids = jnp.arange(GROUP, dtype=jnp.int32)[None, :, None]
    dst_ids = jnp.arange(GROUP, dtype=jnp.int32)[None, None, :]
    counts = jnp.where((dst_ids == full_dst) | (src_ids == full_src), SLOT, counts)
    slot_ids = jnp.arange(SLOT, dtype=jnp.int32)[None, None, None, :]
    return (slot_ids < counts[..., None]).astype(jnp.int32)


def draw_atm_pair_cols(key, part):
    live_mask = live_slots(key)
    return jax.random.randint(jax.random.fold_in(key, 21), live_mask.shape, 0, ATM_COLS) * live_mask


def draw_ocn_pair_cells(key, part):
    live_mask = live_slots(key)
    drawn_cells = jax.random.randint(jax.random.fold_in(key, 22), live_mask.shape, 0, OCN_CELLS) * live_mask
    return jnp.transpose(drawn_cells, (0, 2, 1, 3))


def draw_a2o_weights(key, part):
    live_mask = live_slots(key)
    drawn_weights = jax.random.uniform(jax.random.fold_in(key, 23), live_mask.shape, jnp.float32, 0.05, 0.6)
    return drawn_weights * live_mask.astype(jnp.float32)


def draw_o2a_weights(key, part):
    live_mask = live_slots(key)
    drawn_weights = jax.random.uniform(jax.random.fold_in(key, 24), live_mask.shape, jnp.float32, 0.02, 0.2)
    return jnp.transpose(drawn_weights * live_mask.astype(jnp.float32), (0, 2, 1, 3))


def set_ends(values, own_key, least, high):
    index_at = [jax.random.randint(jax.random.fold_in(own_key, axis), (), 0, length) for axis, length in enumerate(values.shape)]
    main_axis = values.shape.index(max(values.shape))
    beside = index_at[:main_axis] + [(index_at[main_axis] + 1) % values.shape[main_axis]] + index_at[main_axis + 1:]
    return values.at[tuple(index_at)].set(least).at[tuple(beside)].set(high)


def level_of(key, shape, split, smallest, high):
    level = 1.0
    for dim, parts in split:
        heights = jax.random.uniform(jax.random.fold_in(jax.random.fold_in(key, 6), dim), (parts,), jnp.float32, smallest / len(split), high / len(split))
        level = level * jnp.repeat(jnp.exp(heights), shape[dim] // parts).reshape((-1,) + (1,) * (len(shape) - 1 - dim))
    return level


def centred(rng, shape, deviation, most, shards=(), kind=jnp.bfloat16):
    gain = level_of(rng, shape, shards, -0.22, 0.18) if shards else 1.0
    values = jax.random.normal(rng, shape, jnp.float32) * deviation * gain
    return jnp.minimum(jnp.maximum(values, -most), most).astype(kind)


def setup_inputs(seed: int = 0) -> dict:
    splits = jax.random.split(jax.random.key(seed), 11)
    atm_state = centred(splits[0], (2, LA, AWIDE, ALONG), 1.0, 6.0, ((2, 128), (3, 2)), jnp.float32)
    atm_diffusion = jnp.clip(jnp.exp(jax.random.uniform(splits[1], (LA,), jnp.float32, math.log(0.04), math.log(0.2))), 0.04, 0.2)
    atm_surface_coef = jnp.clip(jnp.exp(math.log(0.3) - 2.3025852 * jax.random.uniform(splits[2], (2, AWIDE, ALONG), jnp.float32) ** level_of(splits[2], (2, AWIDE, ALONG), ((1, 128), (2, 2)), -0.2, 0.2)), 0.03, 0.3)
    ocn_state = centred(splits[3], (2, LO, OLAT, OLON), 1.0, 6.0, ((2, 128), (3, 2)), jnp.float32)
    ocn_diffusion = jnp.clip(jnp.exp(jax.random.uniform(splits[4], (LO,), jnp.float32, math.log(0.03), math.log(0.2))), 0.03, 0.2)
    sea_mask = set_ends((jax.random.randint(splits[5], (OLAT, OLON), 0, 10) < 7).astype(jnp.int32), jax.random.fold_in(splits[5], 1), 0, 1)
    atm_pair_cols = draw_atm_pair_cols(jax.random.fold_in(splits[10], 71), 0)
    a2o_weights = draw_a2o_weights(jax.random.fold_in(splits[10], 71), 0)
    ocn_pair_cells = draw_ocn_pair_cells(jax.random.fold_in(splits[10], 71), 0)
    o2a_weights = draw_o2a_weights(jax.random.fold_in(splits[10], 71), 0)
    return dict(atm_state=atm_state, atm_diffusion=atm_diffusion, atm_surface_coef=atm_surface_coef, ocn_state=ocn_state, ocn_diffusion=ocn_diffusion, sea_mask=sea_mask, atm_pair_cols=atm_pair_cols, a2o_weights=a2o_weights, ocn_pair_cells=ocn_pair_cells, o2a_weights=o2a_weights)


VERT_MIX = 0.1
OCEAN_MIX = 0.15
HEAT_GAIN = 2.0
SALT_GAIN = 1.0
MOIST_RATIO = 0.8


def level_mix(middle):
    upper_level = jnp.concatenate([middle[:, 1:], middle[:, -1:]], axis=1)
    lower_level = jnp.concatenate([middle[:, :1], middle[:, :-1]], axis=1)
    return upper_level + lower_level - 2.0 * middle


def lateral_mix(padded):
    middle = padded[:, :, 1:-1, 1:-1]
    lateral = padded[:, :, 2:, 1:-1] + padded[:, :, :-2, 1:-1] + padded[:, :, 1:-1, 2:] + padded[:, :, 1:-1, :-2] - 4.0 * middle
    return middle, lateral


def atm_step(padded, surface, diffusion):
    middle, lateral = lateral_mix(padded)
    result = middle + diffusion[None, :, None, None] * lateral + VERT_MIX * level_mix(middle)
    result = result.at[0, 0].add(surface[1, 0] * (surface[0, 0] - middle[0, 0]))
    result = result.at[1, 0].add(surface[2, 0] * (MOIST_RATIO * surface[0, 0] - middle[1, 0]))
    return result


def ocean_step(padded, diffusion, forcing, sea_frac):
    middle, lateral = lateral_mix(padded)
    result = middle + diffusion[None, :, None, None] * lateral + OCEAN_MIX * level_mix(middle)
    result = result.at[0, 0].add(HEAT_GAIN * forcing[0])
    result = result.at[1, 0].add(-SALT_GAIN * forcing[1])
    return result * sea_frac[None, None]


def wrap_pad(field):
    return jnp.pad(field, ((0, 0), (0, 0), (1, 1), (1, 1)), mode="wrap")


def reference(atm_state, atm_diffusion, atm_surface_coef, ocn_state, ocn_diffusion, sea_mask, atm_pair_cols, a2o_weights, ocn_pair_cells, o2a_weights):
    along_half = ALONG // N_LEV
    ocean_half = OLON // N_LEV
    row_ids = jnp.arange(OLAT, dtype=jnp.int32)
    inner_rows = ((row_ids > 0) & (row_ids < OLAT - 1)).astype(jnp.float32)
    sea_frac = sea_mask.astype(jnp.float32) * inner_rows[:, None]
    ocean_now = ocn_state * sea_frac[None, None]
    lev_ids = jnp.arange(N_LEV, dtype=jnp.int32)[:, None, None, None]
    src_ids = jnp.arange(GROUP, dtype=jnp.int32)[None, :, None, None]
    dst_ids = jnp.arange(GROUP, dtype=jnp.int32)[None, None, :, None]
    cell_index = jnp.transpose(ocn_pair_cells, (0, 2, 1, 3))
    back_weights = jnp.transpose(o2a_weights, (0, 2, 1, 3))
    atm_flat = (src_ids * ACOL_DEV + atm_pair_cols // along_half) * ALONG + lev_ids * along_half + atm_pair_cols % along_half
    ocn_flat = (dst_ids * OROW_DEV + cell_index // ocean_half) * OLON + lev_ids * ocean_half + cell_index % ocean_half
    atm_flat = atm_flat.reshape(-1).astype(jnp.int32)
    ocn_flat = ocn_flat.reshape(-1).astype(jnp.int32)
    top_temp = ocean_now[0, 0].reshape(-1)
    sea_temp = jnp.zeros((AWIDE * ALONG,), jnp.float32).at[atm_flat].add(back_weights.reshape(-1) * top_temp[ocn_flat]).reshape(AWIDE, ALONG)
    heat_flux = atm_surface_coef[0] * (atm_state[0, 0] - sea_temp)
    fresh_flux = atm_surface_coef[1] * (atm_state[1, 0] - MOIST_RATIO * sea_temp)
    fluxes = jnp.stack([heat_flux, fresh_flux]).reshape(2, -1)
    weighted = a2o_weights.reshape(1, -1) * fluxes[:, atm_flat]
    forcing = jnp.zeros((2, OLAT * OLON), jnp.float32).at[:, ocn_flat].add(weighted).reshape(2, OLAT, OLON)
    surface = jnp.stack([sea_temp, atm_surface_coef[0], atm_surface_coef[1]])[:, None]
    atm_now = atm_state
    for step_index in range(ASTEPS):
        atm_now = atm_step(wrap_pad(atm_now), surface, atm_diffusion)
    for step_index in range(OSTEPS):
        ocean_now = ocean_step(wrap_pad(ocean_now), ocn_diffusion, forcing, sea_frac)
    return atm_now, ocean_now
```

```python
import functools
import jax
import jax.numpy as jnp
from jax import lax
from jax.experimental import pallas as pl
from jax.experimental.pallas import tpu as pltpu
from jax.sharding import PartitionSpec as P

F32, BF16 = jnp.float32, jnp.bfloat16

def parts_of(v, count):
    out = []
    for i in range(count):
        p = v.astype(BF16)
        out.append(p)
        v = v - p.astype(F32)
    return out

def spread(row, rows):
    return jnp.broadcast_to(row.astype(F32), (rows, row.shape[1])).astype(BF16)

def one_hot(row, size):
    b = spread(row, 16)
    base = lax.broadcasted_iota(jnp.int32, b.shape, 0).astype(F32)
    one, zero = jnp.ones(b.shape, BF16), jnp.zeros(b.shape, BF16)
    return jnp.concatenate([jnp.where(b == (base + 16.0 * j).astype(BF16), one, zero) for j in range(size // 16)], axis=0)

def g1_kernel(splits, H, L, table_ref, cell_ref, w_ref, out_ref, t_ref):
    t_ref[...] = jnp.concatenate(parts_of(table_ref[...], splits), axis=1)
    sh = L.bit_length() - 1
    def group(g, c):
        base = pl.multiple_of(g * 8, 8)
        idx = cell_ref[pl.ds(base, 8), :]
        w = w_ref[pl.ds(base, 8), :]
        hi, lo = idx >> sh, idx & (L - 1)
        for r in range(8):
            oh = one_hot(hi[r:r+1], H)
            rhs = jnp.concatenate([oh] * splits, axis=0)
            o = jnp.dot(t_ref[...], rhs, preferred_element_type=F32)
            rows = lax.broadcasted_iota(jnp.int32, o.shape, 0)
            pick = jnp.where(rows == lo[r:r+1], o, 0.0)
            res = jnp.sum(pick, axis=0, keepdims=True) * w[r:r+1]
            for q in range(4):
                out_ref[base + r, q:q+1, :] = res[:, q*128:(q+1)*128]
        return c
    lax.fori_loop(0, cell_ref.shape[0] // 8, group, 0)

def g1(table_t, cells, w, splits=3):
    L, H = table_t.shape
    n = cells.shape[0]
    return pl.pallas_call(functools.partial(g1_kernel, splits, H, L),
        out_shape=jax.ShapeDtypeStruct((n, 4, 128), F32),
        in_specs=[pl.BlockSpec(memory_space=pltpu.VMEM)]*3,
        out_specs=pl.BlockSpec(memory_space=pltpu.VMEM),
        scratch_shapes=[pltpu.VMEM((L, H*splits), BF16)], name="g1")(table_t, cells, w)

def scatter_loop(splits, H, L, F, val_ref, idx_ref, unroll=8):
    sh = L.bit_length() - 1
    def group(g, acc):
        base = pl.multiple_of(g * 8, 8)
        idx = idx_ref[pl.ds(base, 8), :]
        hi, lo = idx >> sh, idx & (L - 1)
        for r in range(8):
            ohl = one_hot(lo[r:r+1], L)
            b = spread(hi[r:r+1], 16)
            rows = lax.broadcasted_iota(jnp.int32, b.shape, 0).astype(F32)
            ms = [b == (rows + 16.0*j).astype(BF16) for j in range(H // 16)]
            a = []
            for f in range(F):
                v = jnp.concatenate([val_ref[base + r, 4*f+q:4*f+q+1, :] for q in range(4)], axis=1)
                v = jnp.broadcast_to(v, (16, v.shape[1]))
                for p in parts_of(v, splits):
                    a += [jnp.where(m, p, jnp.zeros_like(p)) for m in ms]
            a = jnp.concatenate(a, axis=0)
            acc = acc + lax.dot_general(a, ohl, (((1,), (1,)), ((), ())), preferred_element_type=F32)
        return acc
    return lax.fori_loop(0, idx_ref.shape[0] // 8, group, jnp.zeros((F*splits*H, L), F32))

def s_kernel(splits, H, L, F, val_ref, idx_ref, out_ref):
    acc = scatter_loop(splits, H, L, F, val_ref, idx_ref)
    for f in range(F):
        out_ref[f] = sum(acc[(f*splits+i)*H:(f*splits+i+1)*H] for i in range(splits))

def scat(vals, idx, H, L, F, splits=3):
    n = idx.shape[0]
    return pl.pallas_call(functools.partial(s_kernel, splits, H, L, F),
        out_shape=jax.ShapeDtypeStruct((F, H, L), F32),
        in_specs=[pl.BlockSpec(memory_space=pltpu.VMEM)]*2,
        out_specs=pl.BlockSpec(memory_space=pltpu.VMEM), name=f"s{F}_{H}_{L}_{splits}")(vals, idx)

def g2_kernel(splits, H, L, F, table_ref, idx_ref, w_ref, out_ref, t_ref):
    t_ref[...] = jnp.concatenate([jnp.concatenate(parts_of(table_ref[f], splits), axis=1) for f in range(F)], axis=0)
    sh = L.bit_length() - 1
    def group(g, c):
        base = pl.multiple_of(g * 8, 8)
        idx = idx_ref[pl.ds(base, 8), :]
        w = w_ref[pl.ds(base, 8), :]
        hi, lo = idx >> sh, idx & (L - 1)
        for r in range(8):
            oh = one_hot(hi[r:r+1], H)
            rhs = jnp.concatenate([oh] * splits, axis=0)
            o = jnp.dot(t_ref[...], rhs, preferred_element_type=F32)
            rows = lax.broadcasted_iota(jnp.int32, (L, 512), 0)
            m = rows == lo[r:r+1]
            for f in range(F):
                res = jnp.sum(jnp.where(m, o[f*L:(f+1)*L], 0.0), axis=0, keepdims=True) * w[r:r+1]
                for q in range(4):
                    out_ref[base + r, 4*f+q:4*f+q+1, :] = res[:, q*128:(q+1)*128]
        return c
    lax.fori_loop(0, idx_ref.shape[0] // 8, group, 0)

def g2(table_t, idx, w, splits=3):
    F, L, H = table_t.shape
    n = idx.shape[0]
    return pl.pallas_call(functools.partial(g2_kernel, splits, H, L, F),
        out_shape=jax.ShapeDtypeStruct((n, 4*F, 128), F32),
        in_specs=[pl.BlockSpec(memory_space=pltpu.VMEM)]*3,
        out_specs=pl.BlockSpec(memory_space=pltpu.VMEM),
        scratch_shapes=[pltpu.VMEM((F*L, H*splits), BF16)], name=f"g2_{F}_{H}_{L}_{splits}")(table_t, idx, w)


ASTEPS = 4
OSTEPS = 2


VERT_MIX = 0.1
OCEAN_MIX = 0.15
HEAT_GAIN = 2.0
SALT_GAIN = 1.0
MOIST_RATIO = 0.8


def in_blocks(value, dim, count):
    dims = value.shape
    pieces = value.reshape(*dims[:dim], count, dims[dim] // count, *dims[dim + 1 :])
    return jnp.moveaxis(pieces, dim, 0)


def laid_out(pieces, dim):
    pieces = jnp.moveaxis(pieces, 0, dim)
    dims = pieces.shape
    return pieces.reshape(*dims[:dim], dims[dim] * dims[dim + 1], *dims[dim + 2 :])


def one_exchange(value, axis, axes, splits, concats):
    sizes = [lax.axis_size(a) for a in axes]
    pieces = in_blocks(value, splits[0], sizes[0])
    pieces = jnp.moveaxis(in_blocks(pieces, splits[1] + 1, sizes[1]), 0, 1)
    inside = pieces.shape[2:]
    pieces = pieces.reshape(-1, *inside)
    pieces = lax.all_to_all(pieces, axis, split_axis=0, concat_axis=0, tiled=True)
    pieces = laid_out(pieces.reshape(*sizes, *inside), concats[0] + 1)
    return laid_out(pieces, concats[1])


def padded_2(value, sides, width):
    edges = {}
    for axis, dim in sides:
        count, length = (lax.axis_size(axis), value.shape[dim])
        up = [(i, (i + 1) % count) for i in range(count)]
        last = lax.slice_in_dim(value, length - width, length, axis=dim)
        first = lax.slice_in_dim(value, 0, width, axis=dim)
        edges[dim] = (
            lax.ppermute(last, axis, up),
            lax.ppermute(first, axis, [(b, a) for a, b in up]),
        )
    done = []
    for _, dim in sides:
        low, high = edges[dim]
        around = [(width, width) if d in done else (0, 0) for d in range(value.ndim)]
        value = jnp.concatenate([jnp.pad(low, around), value, jnp.pad(high, around)], axis=dim)
        done.append(dim)
    return value


def level_mix(middle):
    upper_level = jnp.concatenate([middle[:, 1:], middle[:, -1:]], axis=1)
    lower_level = jnp.concatenate([middle[:, :1], middle[:, :-1]], axis=1)
    return upper_level + lower_level - 2.0 * middle


def lateral_mix(padded):
    middle = padded[:, :, 1:-1, 1:-1]
    lateral = (
        padded[:, :, 2:, 1:-1]
        + padded[:, :, :-2, 1:-1]
        + padded[:, :, 1:-1, 2:]
        + padded[:, :, 1:-1, :-2]
        - 4.0 * middle
    )
    return (middle, lateral)


def atm_step(padded, surface, diffusion):
    middle, lateral = lateral_mix(padded)
    result = middle + diffusion[None, :, None, None] * lateral + VERT_MIX * level_mix(middle)
    result = result.at[0, 0].add(surface[1, 0] * (surface[0, 0] - middle[0, 0]))
    result = result.at[1, 0].add(surface[2, 0] * (MOIST_RATIO * surface[0, 0] - middle[1, 0]))
    return result


def ocean_step(padded, diffusion, forcing, sea_frac):
    middle, lateral = lateral_mix(padded)
    result = middle + diffusion[None, :, None, None] * lateral + OCEAN_MIX * level_mix(middle)
    result = result.at[0, 0].add(HEAT_GAIN * forcing[0])
    result = result.at[1, 0].add(-SALT_GAIN * forcing[1])
    return result * sea_frac[None, None]


def shards(
    atm_state,
    atm_diffusion,
    atm_surface_coef,
    ocn_state,
    ocn_diffusion,
    sea_mask,
    atm_pair_cols,
    a2o_weights,
    ocn_pair_cells,
    o2a_weights,
):
    group_size = lax.axis_size(("comp", "tile"))
    comp_size = lax.axis_size("comp")
    tile_size = lax.axis_size("tile")
    my_block = lax.axis_index(("comp", "tile"))
    atm_rows = atm_state.shape[2]
    atm_cols = atm_state.shape[3]
    ocn_rows = ocn_state.shape[2]
    ocn_cols = ocn_state.shape[3]
    slot_count = atm_pair_cols.shape[3]
    row_ids = my_block * ocn_rows + jnp.arange(ocn_rows, dtype=jnp.int32)
    inner_rows = ((row_ids > 0) & (row_ids < ocn_rows * group_size - 1)).astype(jnp.float32)
    sea_frac = sea_mask.astype(jnp.float32) * inner_rows[:, None]
    ocean_now = ocn_state * sea_frac[None, None]
    col_index = atm_pair_cols[0, 0]
    cell_index = ocn_pair_cells[0, 0]
    table = jnp.pad(ocean_now[0, 0].reshape(-1, 128), ((0, 8), (0, 0))).T
    outgoing = g1(table, cell_index, o2a_weights[0, 0])
    incoming = lax.all_to_all(outgoing, ("comp", "tile"), split_axis=0, concat_axis=0, tiled=True)
    sea_temp = scat(incoming, col_index, 48, 64, 1)[0, :36].reshape(atm_rows, atm_cols)
    heat_flux = atm_surface_coef[0] * (atm_state[0, 0] - sea_temp)
    fresh_flux = atm_surface_coef[1] * (atm_state[1, 0] - MOIST_RATIO * sea_temp)
    fluxes = jnp.stack([heat_flux, fresh_flux]).reshape(2, 36, 64)
    flux_table = jnp.swapaxes(jnp.pad(fluxes, ((0, 0), (0, 12), (0, 0))), 1, 2)
    outgoing_flux = g2(flux_table, col_index, a2o_weights[0, 0])
    incoming_flux = lax.all_to_all(outgoing_flux, ("comp", "tile"), split_axis=0, concat_axis=0, tiled=True)
    forcing = scat(incoming_flux, cell_index, 32, 256, 2)[:, :28].reshape(2, ocn_rows, ocn_cols)
    surface = jnp.stack([sea_temp, atm_surface_coef[0], atm_surface_coef[1]])[:, None]
    atm_now = atm_state
    for step_index in range(ASTEPS):
        padded = padded_2(atm_now, ((("comp", "tile"), 2), ("lev", 3)), 1)
        atm_now = atm_step(padded, surface, atm_diffusion)
    for step_index in range(OSTEPS):
        padded_ocean = padded_2(ocean_now, ((("comp", "tile"), 2), ("lev", 3)), 1)
        ocean_now = ocean_step(padded_ocean, ocn_diffusion, forcing, sea_frac)
    return (atm_now, ocean_now)


def solution(mesh):
    placed = (
        P(None, None, ("comp", "tile"), "lev"),
        P(),
        P(None, ("comp", "tile"), "lev"),
        P(None, None, ("comp", "tile"), "lev"),
        P(),
        P(("comp", "tile"), "lev"),
        P("lev", ("comp", "tile"), None, None),
        P("lev", ("comp", "tile"), None, None),
        P("lev", ("comp", "tile"), None, None),
        P("lev", ("comp", "tile"), None, None),
    )
    return jax.shard_map(
        shards,
        mesh=mesh,
        in_specs=placed,
        out_specs=(P(None, None, ("comp", "tile"), "lev"), P(None, None, ("comp", "tile"), "lev")),
        check_vma=False,
    )
```

```python
import functools

import jax
import jax.numpy as jnp
from jax import lax
from jax.experimental import pallas as pl
from jax.experimental.pallas import tpu as pltpu
from jax.sharding import PartitionSpec as P

ASTEPS = 4
OSTEPS = 2
VERT_MIX = 0.1
OCEAN_MIX = 0.15
HEAT_GAIN = 2.0
SALT_GAIN = 1.0
MOIST_RATIO = 0.8
LANES = 128
GROUP = ("comp", "tile")
F32, BF16 = jnp.float32, jnp.bfloat16


SPLITS = 3


def parts_of(v):
    out = []
    for _ in range(SPLITS):
        p = v.astype(BF16)
        out.append(p)
        v = v - p.astype(F32)
    return out


def spread(row):
    return jnp.broadcast_to(row.astype(F32), (16, row.shape[1])).astype(BF16)


def hits(row, size):
    b = spread(row)
    base = lax.broadcasted_iota(jnp.int32, b.shape, 0).astype(F32)
    return [b == (base + 16.0 * j).astype(BF16) for j in range(size // 16)]


def one_hot(row, size):
    masks = hits(row, size)
    one, zero = jnp.ones(masks[0].shape, BF16), jnp.zeros(masks[0].shape, BF16)
    return jnp.concatenate([jnp.where(m, one, zero) for m in masks], axis=0)


def gather_loop(t_ref, index_ref, w_ref, out_ref, split, H, L, F):
    def group(g, c):
        base = pl.multiple_of(g * 8, 8)
        hi, lo = split(index_ref[pl.ds(base, 8), :])
        w = w_ref[pl.ds(base, 8), :]
        for r in range(8):
            hot = jnp.concatenate([one_hot(hi[r : r + 1], H)] * SPLITS, axis=0)
            o = jnp.dot(t_ref[...], hot, preferred_element_type=F32)
            rows = lax.broadcasted_iota(jnp.int32, (L, o.shape[1]), 0)
            mine = rows == lo[r : r + 1]
            for f in range(F):
                picked = jnp.where(mine, o[f * L : (f + 1) * L], 0.0)
                value = jnp.sum(picked, axis=0, keepdims=True) * w[r : r + 1]
                for q in range(4):
                    out_ref[base + r, 4 * f + q : 4 * f + q + 1, :] = value[:, q * 128 : (q + 1) * 128]
        return c
    lax.fori_loop(0, index_ref.shape[0] // 8, group, 0)


def scatter_loop(val_ref, index_ref, H, L, F):
    shift = L.bit_length() - 1
    def group(g, acc):
        base = pl.multiple_of(g * 8, 8)
        index = index_ref[pl.ds(base, 8), :]
        hi, lo = index >> shift, index & (L - 1)
        for r in range(8):
            masks = hits(hi[r : r + 1], H)
            a = []
            for f in range(F):
                v = jnp.concatenate([val_ref[base + r, 4 * f + q : 4 * f + q + 1, :] for q in range(4)], axis=1)
                for p in parts_of(jnp.broadcast_to(v, (16, v.shape[1]))):
                    a += [jnp.where(m, p, jnp.zeros_like(p)) for m in masks]
            a = jnp.concatenate(a, axis=0)
            acc = acc + lax.dot_general(a, one_hot(lo[r : r + 1], L), (((1,), (1,)), ((), ())), preferred_element_type=F32)
        return acc
    acc = lax.fori_loop(0, index_ref.shape[0] // 8, group, jnp.zeros((F * SPLITS * H, L), F32))
    return [sum(acc[(f * SPLITS + i) * H : (f * SPLITS + i + 1) * H] for i in range(SPLITS)) for f in range(F)]


def temp_kernel(table_ref, cell_ref, w_ref, out_ref, t_ref):
    t_ref[...] = jnp.concatenate(parts_of(table_ref[...].T), axis=1)
    gather_loop(t_ref, cell_ref, w_ref, out_ref, lambda i: (i >> 7, i & 127), 64, 128, 1)


def flux_kernel(val_ref, col_ref, state_ref, coef_ref, temp_ref, t_ref):
    temp, = scatter_loop(val_ref, col_ref, 32, 128, 1)
    temp_ref[...] = temp
    tables = []
    for f in range(2):
        flux = coef_ref[f] * (state_ref[f] - (1.0, MOIST_RATIO)[f] * temp)
        halves = jnp.concatenate([flux[:24, :64], flux[:24, 64:]], axis=0)
        tables.append(jnp.concatenate(parts_of(halves.T), axis=1))
    t_ref[...] = jnp.concatenate(tables, axis=0)


def half_split(i):
    return (i >> 7) + 24 * ((i >> 6) & 1), i & 63


def send_kernel(t_ref, col_ref, w_ref, out_ref):
    gather_loop(t_ref, col_ref, w_ref, out_ref, half_split, 48, 64, 2)


def forcing_kernel(val_ref, cell_ref, out_ref):
    sums = scatter_loop(val_ref, cell_ref, 32, 256, 2)
    out_ref[0] = HEAT_GAIN * sums[0][:28]
    out_ref[1] = -SALT_GAIN * sums[1][:28]


VM = pl.BlockSpec(memory_space=pltpu.VMEM)


def tile_steps(tile, before, after, other, diffusion, vertical):
    above = jnp.concatenate([tile[1:], tile[-1:]], axis=0)
    below = jnp.concatenate([tile[:1], tile[:-1]], axis=0)
    lateral = other + after + before - 4.0 * tile
    return tile + diffusion * lateral + vertical * (above + below - 2.0 * tile)


def stepped_row(get, get_up, get_down, f, tiles, left, right, diffusion, vertical, finish):
    lane = lax.broadcasted_iota(jnp.int32, left.shape, 1)
    values = [get(f, j) for j in range(tiles)]
    to_right = [pltpu.roll(v, 1, 1) for v in values]
    to_left = [pltpu.roll(v, LANES - 1, 1) for v in values]
    ends = []
    for j in range(tiles):
        before = jnp.where(lane == 0, left if j == 0 else to_right[j - 1], to_right[j])
        after = jnp.where(lane == LANES - 1, right if j == tiles - 1 else to_left[j + 1], to_left[j])
        other = get_down(f, j) + get_up(f, j)
        fresh = tile_steps(values[j], before, after, other, diffusion, vertical)
        fresh = finish(f, j, fresh, values[j])
        if j in (0, tiles - 1):
            ends.append(fresh)
    return ends


def edges_of(rows):
    lane = lax.broadcasted_iota(jnp.int32, rows[0][0].shape, 1)
    out = jnp.zeros(rows[0][0].shape, F32)
    for i, (first, last) in enumerate(rows):
        out = jnp.where(lane == 2 * i, pltpu.roll(first, 2 * i, 1) if i else first, out)
        out = jnp.where(lane == 2 * i + 1, pltpu.roll(last, 2 * i + 2, 1), out)
    return out


def edge(edges, i):
    return jnp.broadcast_to(edges[:, i : i + 1], edges.shape)


def atm_kernel(row0, row1, up, down, edges_ref, diff_ref, coef_ref, temp_ref, out0, out1, out_edges):
    tiles = row0.shape[1]
    edges, diffusion = edges_ref[...], diff_ref[...]
    top = lax.broadcasted_iota(jnp.int32, (8, LANES), 0) == 0
    rows = [up, row0, row1, down]
    ends = []
    for r, out in enumerate((out0, out1)):
        def finish(f, j, fresh, old, r=r, out=out):
            at = r * tiles + j
            gain = (1.0, MOIST_RATIO)[f] * temp_ref[at : at + 1, :]
            gain = coef_ref[f, at : at + 1, :] * (gain - old[:1])
            fresh = jnp.concatenate([fresh[:8] + jnp.where(top, gain, 0.0), fresh[8:]], axis=0)
            out[f, j] = fresh
            return fresh
        for f in range(2):
            i = 2 * r + f
            ends.append(stepped_row(*(lambda f, j, ref=ref: ref[f, j] for ref in (rows[r + 1], rows[r], rows[r + 2])), f, tiles, edge(edges, 2 * i + 1), edge(edges, 2 * i), diffusion, VERT_MIX, finish))
    out_edges[...] = edges_of(ends)


def atm_stepped(row0, row1, up, down, edges, diffusion, coef, temp):
    row = jax.ShapeDtypeStruct(row0.shape, F32)
    return pl.pallas_call(
        atm_kernel,
        out_shape=(row, row, jax.ShapeDtypeStruct(edges.shape, F32)),
        in_specs=[VM] * 8,
        out_specs=(VM,) * 3,
        cost_estimate=pl.CostEstimate(flops=12 * 4 * row0.size, bytes_accessed=24 * row0.size, transcendentals=0),
        name="atm_step",
    )(row0, row1, up, down, edges, diffusion, coef, temp)


def ocn_kernel(own, up, down, edges_ref, diff_ref, frac_ref, out, out_edges):
    count, _, tiles = own.shape[:3]
    edges, diffusion = edges_ref[...], diff_ref[...]
    rows = [up] + [own.at[r] for r in range(count)] + [down]
    ends = []
    for r in range(count):
        def finish(f, j, fresh, old, r=r):
            fresh = fresh * frac_ref[r * tiles + j : r * tiles + j + 1, :]
            out[r, f, j] = fresh
            return fresh
        for f in range(2):
            i = 2 * r + f
            ends.append(stepped_row(*(lambda f, j, ref=ref: ref[f, j] for ref in (rows[r + 1], rows[r], rows[r + 2])), f, tiles, edge(edges, 2 * i + 1), edge(edges, 2 * i), diffusion, OCEAN_MIX, finish))
    out_edges[...] = edges_of(ends)


def ocn_stepped(own, up, down, edges, diffusion, frac):
    return pl.pallas_call(
        ocn_kernel,
        out_shape=(jax.ShapeDtypeStruct(own.shape, F32), jax.ShapeDtypeStruct(edges.shape, F32)),
        in_specs=[VM] * 6,
        out_specs=(VM,) * 2,
        cost_estimate=pl.CostEstimate(flops=12 * own.size, bytes_accessed=12 * own.size, transcendentals=0),
        name="ocn_step",
    )(own, up, down, edges, diffusion, frac)


def call(kernel, name, flops, out_shape, *args, scratch=()):
    return pl.pallas_call(
        kernel,
        out_shape=out_shape,
        in_specs=[VM] * len(args),
        out_specs=jax.tree.map(lambda _: VM, out_shape),
        scratch_shapes=list(scratch),
        cost_estimate=pl.CostEstimate(flops=flops, bytes_accessed=1 << 20, transcendentals=0),
        name=name,
    )(*args)


def by_rows(field):
    fields, levels, rows, cols = field.shape
    return field.reshape(fields, levels, rows, cols // LANES, LANES).transpose(2, 0, 3, 1, 4)


def from_rows(tiles):
    rows, fields, count, levels, lanes = tiles.shape
    return tiles.transpose(1, 3, 0, 2, 4).reshape(fields, levels, rows, count * lanes)


def row_halos(first, last):
    count = lax.axis_size(GROUP)
    up = [(i, (i + 1) % count) for i in range(count)]
    return lax.ppermute(last, GROUP, up), lax.ppermute(first, GROUP, [(b, a) for a, b in up])


def partner(edges):
    count = lax.axis_size("lev")
    return lax.ppermute(edges, "lev", [(i, (i + 1) % count) for i in range(count)])


def first_edges(field):
    ends = jnp.stack([field[..., 0], field[..., -1]], axis=-1)
    ends = ends.transpose(1, 2, 0, 3).reshape(field.shape[1], -1)
    return jnp.pad(ends, ((0, 0), (0, LANES - ends.shape[1])))


def shards(
    atm_state,
    atm_diffusion,
    atm_surface_coef,
    ocn_state,
    ocn_diffusion,
    sea_mask,
    atm_pair_cols,
    a2o_weights,
    ocn_pair_cells,
    o2a_weights,
):
    group_size = lax.axis_size(GROUP)
    my_block = lax.axis_index(GROUP)
    atm_levels, atm_rows, atm_cols = atm_state.shape[1:]
    ocn_levels, ocn_rows, ocn_cols = ocn_state.shape[1:]
    slots = atm_pair_cols.shape[3]
    shape = lambda *s: jax.ShapeDtypeStruct(s, F32)

    row_ids = my_block * ocn_rows + jnp.arange(ocn_rows, dtype=jnp.int32)
    inner_rows = ((row_ids > 0) & (row_ids < ocn_rows * group_size - 1)).astype(F32)
    sea_frac = sea_mask.astype(F32) * inner_rows[:, None]
    ocean_start = ocn_state * sea_frac[None, None]
    cols, cells = atm_pair_cols[0, 0], ocn_pair_cells[0, 0]

    table = jnp.pad((ocn_state[0, 0] * sea_frac).reshape(-1, LANES), ((0, 8), (0, 0)))
    outgoing = call(temp_kernel, "temp_gather", 1 << 33, shape(group_size, slots // LANES, LANES), table, cells, o2a_weights[0, 0], scratch=[pltpu.VMEM((128, SPLITS * 64), BF16)])
    incoming = lax.all_to_all(outgoing, GROUP, split_axis=0, concat_axis=0, tiled=True)

    atm = by_rows(atm_state)
    row0, row1 = atm[0], atm[1]
    atm_diff = jnp.broadcast_to(atm_diffusion[:, None], (atm_levels, LANES))
    edges = first_edges(atm_state)
    ocean = by_rows(ocean_start)
    ocn_diff = jnp.broadcast_to(ocn_diffusion[:, None], (ocn_levels, LANES))
    frac_tiles = sea_frac.reshape(-1, LANES)
    ocn_edges = first_edges(ocean_start)

    up, down = row_halos(row0, row1)
    beside = partner(edges)
    ocean, ocn_edges = ocn_stepped(ocean, *row_halos(ocean[0], ocean[-1]), partner(ocn_edges), ocn_diff, frac_tiles)

    pad = ((0, 0), (0, 32 - atm_rows * atm_cols // LANES), (0, 0))
    coef = jnp.pad(atm_surface_coef.reshape(2, -1, LANES), pad)
    surface = jnp.pad(atm_state[:, 0].reshape(2, -1, LANES), pad)
    temp, flux_table = call(flux_kernel, "temp_scatter", 1 << 33, (shape(32, LANES), jax.ShapeDtypeStruct((128, SPLITS * 48), BF16)), incoming, cols, surface, coef)
    outgoing = call(send_kernel, "flux_gather", 1 << 33, shape(group_size, 2 * slots // LANES, LANES), flux_table, cols, a2o_weights[0, 0])
    incoming = lax.all_to_all(outgoing, GROUP, split_axis=0, concat_axis=0, tiled=True)

    for step in range(ASTEPS):
        row0, row1, edges = atm_stepped(row0, row1, up, down, beside, atm_diff, coef, temp)
        if step < ASTEPS - 1:
            up, down = row_halos(row0, row1)
            beside = partner(edges)
    atm_next = from_rows(jnp.stack([row0, row1]))

    ocean, _ = ocn_stepped(ocean, *row_halos(ocean[0], ocean[-1]), partner(ocn_edges), ocn_diff, frac_tiles)
    ocean = from_rows(ocean)

    forcing = call(forcing_kernel, "forcing_scatter", 1 << 33, shape(2, 28, 256), incoming, cells).reshape(2, ocn_rows, ocn_cols)
    gained = forcing * sea_frac
    above, below = row_halos(gained[:, :1], gained[:, -1:])
    ends = partner(jnp.stack([gained[:, :, 0], gained[:, :, -1]]))
    tall = jnp.concatenate([above, gained, below], axis=1)
    wide = jnp.concatenate([ends[1][:, :, None], gained, ends[0][:, :, None]], axis=2)
    lateral = tall[:, 2:] + tall[:, :-2] + wide[:, :, 2:] + wide[:, :, :-2] - 4.0 * gained
    second = gained + ocn_diffusion[0] * lateral - OCEAN_MIX * gained + forcing
    added = jnp.stack([second, OCEAN_MIX * gained], axis=1) * sea_frac
    return (atm_next, ocean.at[:, :2].add(added))


def solution(mesh):
    across = P(None, None, GROUP, "lev")
    pairs = P("lev", GROUP, None, None)
    placed = (across, P(), P(None, GROUP, "lev"), across, P(), P(GROUP, "lev"), pairs, pairs, pairs, pairs)
    return jax.shard_map(shards, mesh=mesh, in_specs=placed, out_specs=(across, across), check_vma=False)
```

```python
import jax
import jax.numpy as jnp
from jax import lax
from jax.experimental import pallas as pl
from jax.experimental.pallas import tpu as pltpu
from jax.sharding import PartitionSpec as P

ASTEPS = 4
OSTEPS = 2
VERT_MIX = 0.1
OCEAN_MIX = 0.15
HEAT_GAIN = 2.0
SALT_GAIN = 1.0
MOIST_RATIO = 0.8
LANES = 128
GROUP = ("comp", "tile")
F32, BF16 = jnp.float32, jnp.bfloat16


SPLITS = 3


def parts_of(v):
    out = []
    for _ in range(SPLITS):
        p = v.astype(BF16)
        out.append(p)
        v = v - p.astype(F32)
    return out


def spread(row):
    return jnp.broadcast_to(row.astype(F32), (16, row.shape[1])).astype(BF16)


def hits(row, size):
    b = spread(row)
    base = lax.broadcasted_iota(jnp.int32, b.shape, 0).astype(F32)
    return [b == (base + 16.0 * j).astype(BF16) for j in range(size // 16)]


def one_hot(row, size):
    masks = hits(row, size)
    one, zero = jnp.ones(masks[0].shape, BF16), jnp.zeros(masks[0].shape, BF16)
    return jnp.concatenate([jnp.where(m, one, zero) for m in masks], axis=0)


def gather_loop(t_ref, index_ref, w_ref, out_ref, split, H, L, F):
    def group(g, c):
        base = pl.multiple_of(g * 8, 8)
        hi, lo = split(index_ref[pl.ds(base, 8), :])
        w = w_ref[pl.ds(base, 8), :]
        for r in range(8):
            hot = jnp.concatenate([one_hot(hi[r : r + 1], H)] * SPLITS, axis=0)
            o = jnp.dot(t_ref[...], hot, preferred_element_type=F32)
            rows = lax.broadcasted_iota(jnp.int32, (L, o.shape[1]), 0)
            mine = rows == lo[r : r + 1]
            for f in range(F):
                picked = jnp.where(mine, o[f * L : (f + 1) * L], 0.0)
                value = jnp.sum(picked, axis=0, keepdims=True) * w[r : r + 1]
                for q in range(4):
                    out_ref[base + r, 4 * f + q : 4 * f + q + 1, :] = value[:, q * 128 : (q + 1) * 128]
        return c
    lax.fori_loop(0, index_ref.shape[0] // 8, group, 0)


def scatter_loop(val_ref, index_ref, H, L, F, place_of=lambda h: h):
    shift = L.bit_length() - 1
    def group(g, acc):
        base = pl.multiple_of(g * 8, 8)
        index = index_ref[pl.ds(base, 8), :]
        hi, lo = place_of(index >> shift), index & (L - 1)
        for r in range(8):
            masks = hits(hi[r : r + 1], H)
            a = []
            for f in range(F):
                v = jnp.concatenate([val_ref[base + r, 4 * f + q : 4 * f + q + 1, :] for q in range(4)], axis=1)
                for p in parts_of(jnp.broadcast_to(v, (16, v.shape[1]))):
                    a += [jnp.where(m, p, jnp.zeros_like(p)) for m in masks]
            a = jnp.concatenate(a, axis=0)
            acc = acc + lax.dot_general(a, one_hot(lo[r : r + 1], L), (((1,), (1,)), ((), ())), preferred_element_type=F32)
        return acc
    acc = lax.fori_loop(0, index_ref.shape[0] // 8, group, jnp.zeros((F * SPLITS * H, L), F32))
    return [sum(acc[(f * SPLITS + i) * H : (f * SPLITS + i + 1) * H] for i in range(SPLITS)) for f in range(F)]


def temp_kernel(table_ref, cell_ref, w_ref, out_ref, t_ref):
    t_ref[...] = jnp.concatenate(parts_of(table_ref[...].T), axis=1)
    gather_loop(t_ref, cell_ref, w_ref, out_ref, lambda i: (i >> 7, i & 127), 64, 128, 1)


AT, AL, AR = 9, 48, 2
OT, OL, OR = 14, 24, 4
ASIZE, OSIZE = 2 * AT * AL, 2 * OT * OL


def flux_kernel(val_ref, col_ref, state_ref, coef_ref, temp_ref, t_ref, flux_ref):
    temp, = scatter_loop(val_ref, col_ref, 32, 128, 1)
    temp = temp[: AR * AT]
    temp_ref[...] = temp
    flux_ref[...] = jnp.zeros_like(flux_ref)
    tables = []
    for f in range(2):
        flux_ref[: AR * AT, :] = coef_ref[f] * (state_ref[f] - (1.0, MOIST_RATIO)[f] * temp)
        flux = flux_ref[...]
        halves = jnp.concatenate([flux[:, :64], flux[:, 64:]], axis=0)
        tables.append(jnp.concatenate(parts_of(halves.T), axis=1))
    t_ref[...] = jnp.concatenate(tables, axis=0)


def half_split(i):
    return (i >> 7) + 24 * ((i >> 6) & 1), i & 63


def send_kernel(t_ref, col_ref, w_ref, out_ref):
    gather_loop(t_ref, col_ref, w_ref, out_ref, half_split, 48, 64, 2)


def shifted_levels(ref, base, levels, tile):
    side = lax.broadcasted_iota(jnp.int32, (8, LANES), 0)
    first, last = tile[:8], tile[-8:]
    above = jnp.concatenate([ref[base + 1 : base + levels - 7, :], jnp.where(side == 7, last, pltpu.roll(last, 7, 0))], axis=0)
    below = jnp.concatenate([jnp.where(side == 0, first, pltpu.roll(first, 1, 0)), ref[base + 7 : base + levels - 1, :]], axis=0)
    return above, below


def step_row(own, up, down, tiles, levels, left, right, own_gain, side_gain, vertical, finish):
    lane = lax.broadcasted_iota(jnp.int32, (levels, LANES), 1)
    load = lambda place, j: place[0][place[1] + j * levels : place[1] + (j + 1) * levels, :]
    ends = []
    tile = load(own, 0)
    low_side = left
    for j in range(tiles):
        if j < tiles - 1:
            ahead = load(own, j + 1)
            high_side = pltpu.roll(ahead, LANES - 1, 1)
        else:
            ahead, high_side = None, right
        to_right = pltpu.roll(tile, 1, 1)
        before = jnp.where(lane == 0, low_side, to_right)
        after = jnp.where(lane == LANES - 1, high_side, pltpu.roll(tile, LANES - 1, 1))
        above, below = shifted_levels(own[0], own[1] + j * levels, levels, tile)
        around = (load(up, j) + load(down, j)) + (before + after)
        fresh = own_gain * tile + side_gain * around + vertical * (above + below)
        fresh = finish(j, fresh, tile)
        if j in (0, tiles - 1):
            ends.append(fresh)
        tile, low_side = ahead, to_right
    return ends


def edges_of(rows):
    lane = lax.broadcasted_iota(jnp.int32, rows[0][0].shape, 1)
    out = jnp.zeros(rows[0][0].shape, F32)
    for i, (first, last) in enumerate(rows):
        out = jnp.where(lane == 2 * i, pltpu.roll(first, 2 * i, 1) if i else first, out)
        out = jnp.where(lane == 2 * i + 1, pltpu.roll(last, 2 * i + 2, 1), out)
    return out


def edge(edges, i):
    return jnp.broadcast_to(edges[:, i : i + 1], edges.shape)


def prep_kernel(atm_ref, ocn_ref, mask_ref, inner_ref, coef_ref, adiff_ref, odiff_ref, low, high, edges, ocean, frac, table, surface, coef, adiff, odiff):
    adiff[...] = jnp.broadcast_to(adiff_ref[...], (LANES, AL)).T
    odiff[...] = jnp.broadcast_to(odiff_ref[...], (LANES, OL)).T
    ends = []
    for r, out in enumerate((low, high)):
        for f in range(2):
            pair = []
            for j in range(AT):
                tile = atm_ref[f, :, r, j * LANES : (j + 1) * LANES]
                out[(f * AT + j) * AL : (f * AT + j + 1) * AL, :] = tile
                at = r * AT + j
                surface[f, at : at + 1, :] = tile[:1]
                coef[f, at : at + 1, :] = coef_ref[f, r : r + 1, j * LANES : (j + 1) * LANES]
                if j in (0, AT - 1):
                    pair.append(tile)
            ends.append(pair)
    edges[:AL, :] = edges_of(ends)
    table[...] = jnp.zeros_like(table)
    ends = []
    for r in range(OR):
        for j in range(OT):
            at = r * OT + j
            frac[at : at + 1, :] = mask_ref[r : r + 1, j * LANES : (j + 1) * LANES].astype(F32) * inner_ref[r : r + 1, :]
        for f in range(2):
            pair = []
            for j in range(OT):
                at = r * OT + j
                tile = ocn_ref[f, :, r, j * LANES : (j + 1) * LANES] * frac[at : at + 1, :]
                line = ((r * 2 + f) * OT + j) * OL
                ocean[line : line + OL, :] = tile
                if r in (0, OR - 1):
                    line = ASIZE + (f * OT + j) * OL
                    (high if r else low)[line : line + OL, :] = tile
                if f == 0:
                    table[at : at + 1, :] = tile[:1]
                if j in (0, OT - 1):
                    pair.append(tile)
            ends.append(pair)
    edges[AL:, :] = edges_of(ends)


def atm_kernel(share, low, high, up, down, edges_ref, diff_ref, coef_ref, temp_ref, *rest):
    if share:
        ocean, ocn_edges, out_low, out_high, out_edges = rest
    else:
        out_low, out_high, out_edges = rest
    edges, side_gain = edges_ref[:AL, :], diff_ref[...]
    own_gain = (1.0 - 2.0 * VERT_MIX) - 4.0 * side_gain
    top = lax.broadcasted_iota(jnp.int32, (8, LANES), 0) == 0
    rows = [up, low, high, down]
    ends = []
    for r, out in enumerate((out_low, out_high)):
        for f in range(2):
            def finish(j, fresh, old, f=f, r=r, out=out):
                at = r * AT + j
                gain = (1.0, MOIST_RATIO)[f] * temp_ref[at : at + 1, :]
                gain = coef_ref[f, at : at + 1, :] * (gain - old[:1])
                fresh = jnp.concatenate([fresh[:8] + jnp.where(top, gain, 0.0), fresh[8:]], axis=0)
                out[(f * AT + j) * AL : (f * AT + j + 1) * AL, :] = fresh
                return fresh
            i, base = 2 * r + f, f * AT * AL
            ends.append(step_row(*((rows[k], base) for k in (r + 1, r, r + 2)), AT, AL, edge(edges, 2 * i + 1), edge(edges, 2 * i), own_gain, side_gain, VERT_MIX, finish))
    out_edges[:AL, :] = edges_of(ends)
    if share:
        out_low[ASIZE:, :] = ocean[:OSIZE, :]
        out_high[ASIZE:, :] = ocean[(OR - 1) * OSIZE :, :]
        out_edges[AL:, :] = ocn_edges[...]


def ocn_kernel(own, up, down, edges_ref, diff_ref, frac_ref, out, *out_edges):
    edges, side_gain = edges_ref[AL:, :], diff_ref[...]
    own_gain = (1.0 - 2.0 * OCEAN_MIX) - 4.0 * side_gain
    ends = []
    for r in range(OR):
        for f in range(2):
            def finish(j, fresh, old, f=f, r=r):
                fresh = fresh * frac_ref[r * OT + j : r * OT + j + 1, :]
                line = ((r * 2 + f) * OT + j) * OL
                out[line : line + OL, :] = fresh
                return fresh
            i = 2 * r + f
            part = lambda k: (own, (k * 2 + f) * OT * OL)
            above = part(r - 1) if r else (up, ASIZE + f * OT * OL)
            below = part(r + 1) if r < OR - 1 else (down, ASIZE + f * OT * OL)
            ends.append(step_row(part(r), above, below, OT, OL, edge(edges, 2 * i + 1), edge(edges, 2 * i), own_gain, side_gain, OCEAN_MIX, finish))
    if out_edges:
        out_edges[0][...] = edges_of(ends)


def forcing_kernel(val_ref, cell_ref, frac_ref, out_ref, gain_ref, low, high):
    for f, total in enumerate(scatter_loop(val_ref, cell_ref, 32, 256, 2)):
        total = (HEAT_GAIN, -SALT_GAIN)[f] * total[: OR * OT // 2]
        for side in range(2):
            out_ref[f, pl.ds(side, OR * OT // 2, stride=2), :] = total[:, side * LANES : (side + 1) * LANES]
        gain_ref[f] = out_ref[f] * frac_ref[...]
        low[f] = gain_ref[f, :OT, :]
        high[f] = gain_ref[f, (OR - 1) * OT :, :]


def last_kernel(base_ref, top_ref, forcing_ref, gain_ref, up, down, beside, frac_ref, diff_ref, out_ref, tall, low_side, high_side, result, sem):
    count = OR * OT
    lane = lax.broadcasted_iota(jnp.int32, (count, LANES), 1)
    line = lax.broadcasted_iota(jnp.int32, (count, LANES), 0)
    starts = (line == 0) | (line == OT) | (line == 2 * OT) | (line == 3 * OT)
    stops = (line == OT - 1) | (line == 2 * OT - 1) | (line == 3 * OT - 1) | (line == 4 * OT - 1)
    frac = frac_ref[...]
    low_side[...] = jnp.zeros_like(low_side)
    high_side[...] = jnp.zeros_like(high_side)
    for f in range(2):
        forcing, gained = forcing_ref[f], gain_ref[f]
        tall[OT : 5 * OT, :] = gained
        tall[:OT, :] = up[f]
        tall[5 * OT :, :] = down[f]
        partner = beside[f]
        to_right, to_left = pltpu.roll(partner, 1, 1), pltpu.roll(partner, LANES - 1, 1)
        for r in range(OR):
            first, last = r * OT, (r + 1) * OT - 1
            low_side[first : first + 1, :] = to_right[last : last + 1]
            high_side[last : last + 1, :] = to_left[first : first + 1]
        to_right, to_left = pltpu.roll(gained, 1, 1), pltpu.roll(gained, LANES - 1, 1)
        before = jnp.where(lane == 0, jnp.where(starts, low_side[...], pltpu.roll(to_right, 1, 0)), to_right)
        after = jnp.where(lane == LANES - 1, jnp.where(stops, high_side[...], pltpu.roll(to_left, count - 1, 0)), to_left)
        lateral = tall[: 4 * OT, :] + tall[2 * OT :, :] + before + after - 4.0 * gained
        second = (gained + diff_ref[:1, :] * lateral - OCEAN_MIX * gained + forcing) * frac
        third = OCEAN_MIX * gained * frac
        for r in range(OR):
            for j in range(OT):
                at, cols = r * OT + j, pl.ds(j * LANES, LANES)
                result[f, 0, r : r + 1, cols] = top_ref[f, 0, r : r + 1, cols] + second[at : at + 1]
                result[f, 1, r : r + 1, cols] = top_ref[f, 1, r : r + 1, cols] + third[at : at + 1]
    copy = pltpu.make_async_copy(result, out_ref.at[:, pl.ds(0, 2)], sem)
    copy.start()
    copy.wait()


VM = pl.BlockSpec(memory_space=pltpu.VMEM)
ANY = pl.BlockSpec(memory_space=pl.ANY)


def call(kernel, name, micros, out_shape, *args, scratch=(), **more):
    specs = {"in_specs": [VM] * len(args), "out_specs": jax.tree.map(lambda _: VM, out_shape), **more}
    return pl.pallas_call(
        kernel,
        out_shape=out_shape,
        scratch_shapes=list(scratch),
        cost_estimate=pl.CostEstimate(flops=int(micros * 1.1e9), bytes_accessed=int(micros * 3e6), transcendentals=0),
        name=name,
        **specs,
    )(*args)


def from_rows(tiles):
    rows, fields, count, levels, lanes = tiles.shape
    return tiles.transpose(1, 3, 0, 2, 4).reshape(fields, levels, rows, count * lanes)


def row_halos(first, last):
    count = lax.axis_size(GROUP)
    up = [(i, (i + 1) % count) for i in range(count)]
    return lax.ppermute(last, GROUP, up), lax.ppermute(first, GROUP, [(b, a) for a, b in up])


def partner(edges):
    count = lax.axis_size("lev")
    return lax.ppermute(edges, "lev", [(i, (i + 1) % count) for i in range(count)])


def exchange(values):
    return lax.all_to_all(values, GROUP, split_axis=0, concat_axis=0, tiled=True)


def shards(
    atm_state,
    atm_diffusion,
    atm_surface_coef,
    ocn_state,
    ocn_diffusion,
    sea_mask,
    atm_pair_cols,
    a2o_weights,
    ocn_pair_cells,
    o2a_weights,
):
    group_size = lax.axis_size(GROUP)
    shape = lambda *s: jax.ShapeDtypeStruct(s, F32)
    row_ids = lax.axis_index(GROUP) * OR + lax.broadcasted_iota(jnp.int32, (OR, LANES), 0)
    inner = ((row_ids > 0) & (row_ids < OR * group_size - 1)).astype(F32)
    cols, cells = atm_pair_cols[0, 0], ocn_pair_cells[0, 0]
    both = shape(ASIZE + OSIZE, LANES)

    low, high, edges, ocean, frac, table, surface, coef, atm_diff, ocn_diff = call(
        prep_kernel,
        "prep",
        3,
        (both, both, shape(AL + OL, LANES), shape(OR * OSIZE, LANES), shape(OR * OT, LANES), shape(64, LANES), shape(2, AR * AT, LANES), shape(2, AR * AT, LANES), shape(AL, LANES), shape(OL, LANES)),
        atm_state,
        ocn_state,
        sea_mask,
        inner,
        atm_surface_coef,
        atm_diffusion[None],
        ocn_diffusion[None],
    )
    up, down = row_halos(low, high)
    beside = partner(edges)

    outgoing = call(temp_kernel, "temp_gather", 9, shape(group_size, 4, LANES), table, cells, o2a_weights[0, 0], scratch=[pltpu.VMEM((128, SPLITS * 64), BF16)])
    incoming = exchange(outgoing)
    ocean, ocn_edges = call(ocn_kernel, "ocn_step", 3, (shape(OR * OSIZE, LANES), shape(OL, LANES)), ocean, up, down, beside, ocn_diff, frac)
    incoming, ocean, ocn_edges = lax.optimization_barrier((incoming, ocean, ocn_edges))

    temp, flux_table = call(flux_kernel, "temp_scatter", 9, (shape(AR * AT, LANES), jax.ShapeDtypeStruct((128, SPLITS * 48), BF16)), incoming, cols, surface, coef, scratch=[pltpu.VMEM((24, LANES), F32)])

    def atm_step(share, low, high, up, down, beside, *more):
        rows = shape(ASIZE + OSIZE * share, LANES)
        outs = (rows, rows, shape(AL + OL * share, LANES))
        return call(lambda *refs: atm_kernel(share, *refs), "atm_step", 2.5, outs, low, high, up, down, beside, atm_diff, coef, temp, *more)

    low, high, edges = atm_step(True, low, high, up, down, beside, ocean, ocn_edges)
    up, down = row_halos(low, high)
    beside = partner(edges)
    flux_table, low, high = lax.optimization_barrier((flux_table, low, high))

    outgoing = call(send_kernel, "flux_gather", 9, shape(group_size, 8, LANES), flux_table, cols, a2o_weights[0, 0])
    outgoing, up, down, beside = lax.optimization_barrier((outgoing, up, down, beside))
    ocean = call(ocn_kernel, "ocn_step", 3, shape(OR * OSIZE, LANES), ocean, up, down, beside, ocn_diff, frac)
    ocean = from_rows(ocean.reshape(OR, 2, OT, OL, LANES))
    low, high, edges = atm_step(False, low, high, up, down, beside)
    outgoing, ocean, low, high, edges = lax.optimization_barrier((outgoing, ocean, low, high, edges))
    up, down = row_halos(low, high)
    beside = partner(edges)
    incoming = exchange(outgoing)
    low, high, edges = atm_step(False, low, high, up, down, beside)
    up, down = row_halos(low, high)
    beside = partner(edges)
    incoming, low, high = lax.optimization_barrier((incoming, low, high))

    every = shape(2, OR * OT, LANES)
    forcing, gained, first, last = call(forcing_kernel, "forcing_scatter", 15, (every, every, shape(2, OT, LANES), shape(2, OT, LANES)), incoming, cells, frac)
    forcing, gained, first, last, up, down, beside = lax.optimization_barrier((forcing, gained, first, last, up, down, beside))
    above, below = row_halos(first, last)
    side = partner(gained)

    low, high, _ = atm_step(False, low, high, up, down, beside)
    atm_next = from_rows(jnp.stack([low, high]).reshape(AR, 2, AT, AL, LANES))

    line = pltpu.VMEM((OR * OT, LANES), F32)
    ocean_next = call(
        last_kernel,
        "ocn_last",
        1,
        jax.ShapeDtypeStruct(ocean.shape, F32),
        ocean,
        ocean[:, :2],
        forcing,
        gained,
        above,
        below,
        side,
        frac,
        ocn_diff,
        in_specs=[ANY] + [VM] * 8,
        out_specs=ANY,
        scratch=[pltpu.VMEM((6 * OT, LANES), F32), line, line, pltpu.VMEM((2, 2, OR, OT * LANES), F32), pltpu.SemaphoreType.DMA],
        input_output_aliases={0: 0},
    )
    return atm_next, ocean_next


def solution(mesh):
    across = P(None, None, GROUP, "lev")
    pairs = P("lev", GROUP, None, None)
    placed = (across, P(), P(None, GROUP, "lev"), across, P(), P(GROUP, "lev"), pairs, pairs, pairs, pairs)
    return jax.shard_map(shards, mesh=mesh, in_specs=placed, out_specs=(across, across), check_vma=False)
```

```python
import jax
import jax.numpy as jnp
from jax import lax
from jax.experimental import pallas as pl
from jax.experimental.pallas import tpu as pltpu
from jax.sharding import PartitionSpec as P

ASTEPS = 4
OSTEPS = 2
VERT_MIX = 0.1
OCEAN_MIX = 0.15
HEAT_GAIN = 2.0
SALT_GAIN = 1.0
MOIST_RATIO = 0.8
LANES = 128
GROUP = ("comp", "tile")
F32, BF16 = jnp.float32, jnp.bfloat16


SPLITS = 3


def parts_of(v):
    out = []
    for _ in range(SPLITS):
        p = v.astype(BF16)
        out.append(p)
        v = v - p.astype(F32)
    return out


def spread(row):
    return jnp.broadcast_to(row.astype(F32), (16, row.shape[1])).astype(BF16)


def hits(row, size):
    b = spread(row)
    base = lax.broadcasted_iota(jnp.int32, b.shape, 0).astype(F32)
    return [b == (base + 16.0 * j).astype(BF16) for j in range(size // 16)]


def one_hot(row, size):
    masks = hits(row, size)
    one, zero = jnp.ones(masks[0].shape, BF16), jnp.zeros(masks[0].shape, BF16)
    return jnp.concatenate([jnp.where(m, one, zero) for m in masks], axis=0)


def gather_loop(t_ref, index_ref, w_ref, out_ref, split, H, L, F):
    def group(g, c):
        base = pl.multiple_of(g * 8, 8)
        hi, lo = split(index_ref[pl.ds(base, 8), :])
        w = w_ref[pl.ds(base, 8), :]
        for r in range(8):
            hot = jnp.concatenate([one_hot(hi[r : r + 1], H)] * SPLITS, axis=0)
            o = jnp.dot(t_ref[...], hot, preferred_element_type=F32)
            rows = lax.broadcasted_iota(jnp.int32, (L, o.shape[1]), 0)
            mine = rows == lo[r : r + 1]
            for f in range(F):
                picked = jnp.where(mine, o[f * L : (f + 1) * L], 0.0)
                value = jnp.sum(picked, axis=0, keepdims=True) * w[r : r + 1]
                for q in range(4):
                    out_ref[base + r, 4 * f + q : 4 * f + q + 1, :] = value[:, q * 128 : (q + 1) * 128]
        return c
    lax.fori_loop(0, index_ref.shape[0] // 8, group, 0)


def scatter_loop(val_ref, index_ref, H, L, F, start=0, stop=None):
    shift = L.bit_length() - 1
    def group(g, acc):
        base = pl.multiple_of(g * 8, 8)
        index = index_ref[pl.ds(base, 8), :]
        hi, lo = index >> shift, index & (L - 1)
        for r in range(8):
            masks = hits(hi[r : r + 1], H)
            a = []
            for f in range(F):
                v = jnp.concatenate([val_ref[base + r, 4 * f + q : 4 * f + q + 1, :] for q in range(4)], axis=1)
                for p in parts_of(jnp.broadcast_to(v, (16, v.shape[1]))):
                    a += [jnp.where(m, p, jnp.zeros_like(p)) for m in masks]
            a = jnp.concatenate(a, axis=0)
            acc = acc + lax.dot_general(a, one_hot(lo[r : r + 1], L), (((1,), (1,)), ((), ())), preferred_element_type=F32)
        return acc
    stop = stop or index_ref.shape[0]
    acc = lax.fori_loop(start // 8, stop // 8, group, jnp.zeros((F * SPLITS * H, L), F32))
    return [sum(acc[(f * SPLITS + i) * H : (f * SPLITS + i + 1) * H] for i in range(SPLITS)) for f in range(F)]


def temp_kernel(table_ref, cell_ref, w_ref, out_ref, t_ref):
    t_ref[...] = jnp.concatenate(parts_of(table_ref[...].T), axis=1)
    gather_loop(t_ref, cell_ref, w_ref, out_ref, lambda i: (i >> 7, i & 127), 64, 128, 1)


AT, AL, AR = 9, 48, 2
OT, OL, OR = 14, 24, 4
ASIZE, OSIZE = 2 * AT * AL, 2 * OT * OL


def flux_kernel(val_ref, col_ref, state_ref, coef_ref, temp_ref, t_ref, flux_ref):
    temp, = scatter_loop(val_ref, col_ref, 32, 128, 1)
    temp = temp[: AR * AT]
    temp_ref[...] = temp
    flux_ref[...] = jnp.zeros_like(flux_ref)
    tables = []
    for f in range(2):
        flux_ref[: AR * AT, :] = coef_ref[f] * (state_ref[f] - (1.0, MOIST_RATIO)[f] * temp)
        flux = flux_ref[...]
        halves = jnp.concatenate([flux[:, :64], flux[:, 64:]], axis=0)
        tables.append(jnp.concatenate(parts_of(halves.T), axis=1))
    t_ref[...] = jnp.concatenate(tables, axis=0)


def half_split(i):
    return (i >> 7) + 24 * ((i >> 6) & 1), i & 63


def send_kernel(t_ref, col_ref, w_ref, out_ref):
    gather_loop(t_ref, col_ref, w_ref, out_ref, half_split, 48, 64, 2)


def shifted_levels(ref, base, levels, tile):
    side = lax.broadcasted_iota(jnp.int32, (8, LANES), 0)
    first, last = tile[:8], tile[-8:]
    above = jnp.concatenate([ref[base + 1 : base + levels - 7, :], jnp.where(side == 7, last, pltpu.roll(last, 7, 0))], axis=0)
    below = jnp.concatenate([jnp.where(side == 0, first, pltpu.roll(first, 1, 0)), ref[base + 7 : base + levels - 1, :]], axis=0)
    return above, below


def step_row(own, up, down, tiles, levels, left, right, own_gain, side_gain, vertical, finish):
    lane = lax.broadcasted_iota(jnp.int32, (levels, LANES), 1)
    load = lambda place, j: place[0][place[1] + j * levels : place[1] + (j + 1) * levels, :]
    ends = []
    tile = load(own, 0)
    low_side = left
    for j in range(tiles):
        if j < tiles - 1:
            ahead = load(own, j + 1)
            high_side = pltpu.roll(ahead, LANES - 1, 1)
        else:
            ahead, high_side = None, right
        to_right = pltpu.roll(tile, 1, 1)
        before = jnp.where(lane == 0, low_side, to_right)
        after = jnp.where(lane == LANES - 1, high_side, pltpu.roll(tile, LANES - 1, 1))
        above, below = shifted_levels(own[0], own[1] + j * levels, levels, tile)
        around = (load(up, j) + load(down, j)) + (before + after)
        fresh = own_gain * tile + side_gain * around + vertical * (above + below)
        fresh = finish(j, fresh, tile)
        if j in (0, tiles - 1):
            ends.append(fresh)
        tile, low_side = ahead, to_right
    return ends


def edges_of(rows):
    lane = lax.broadcasted_iota(jnp.int32, rows[0][0].shape, 1)
    out = jnp.zeros(rows[0][0].shape, F32)
    for i, (first, last) in enumerate(rows):
        out = jnp.where(lane == 2 * i, pltpu.roll(first, 2 * i, 1) if i else first, out)
        out = jnp.where(lane == 2 * i + 1, pltpu.roll(last, 2 * i + 2, 1), out)
    return out


def edge(edges, i):
    return jnp.broadcast_to(edges[:, i : i + 1], edges.shape)


def prep_kernel(atm_ref, ocn_ref, mask_ref, coef_ref, adiff_ref, odiff_ref, low, high, edges, ocean, frac, table, surface, coef, adiff, odiff):
    adiff[...] = jnp.broadcast_to(adiff_ref[...], (LANES, AL)).T
    odiff[...] = jnp.broadcast_to(odiff_ref[...], (LANES, OL)).T
    ends = []
    for r, out in enumerate((low, high)):
        for f in range(2):
            pair = []
            for j in range(AT):
                tile = atm_ref[f, :, r, j * LANES : (j + 1) * LANES]
                out[(f * AT + j) * AL : (f * AT + j + 1) * AL, :] = tile
                at = r * AT + j
                surface[f, at : at + 1, :] = tile[:1]
                coef[f, at : at + 1, :] = coef_ref[f, r : r + 1, j * LANES : (j + 1) * LANES]
                if j in (0, AT - 1):
                    pair.append(tile)
            ends.append(pair)
    edges[:AL, :] = edges_of(ends)
    table[...] = jnp.zeros_like(table)
    block, count = lax.axis_index(GROUP), lax.axis_size(GROUP)
    ends = []
    for r in range(OR):
        row = block * OR + r
        inner = jnp.where((row > 0) & (row < OR * count - 1), 1.0, 0.0)
        for j in range(OT):
            at = r * OT + j
            frac[at : at + 1, :] = mask_ref[r : r + 1, j * LANES : (j + 1) * LANES].astype(F32) * inner
        for f in range(2):
            pair = []
            for j in range(OT):
                at = r * OT + j
                tile = ocn_ref[f, :, r, j * LANES : (j + 1) * LANES] * frac[at : at + 1, :]
                line = ((r * 2 + f) * OT + j) * OL
                ocean[line : line + OL, :] = tile
                if r in (0, OR - 1):
                    line = ASIZE + (f * OT + j) * OL
                    (high if r else low)[line : line + OL, :] = tile
                if f == 0:
                    table[at : at + 1, :] = tile[:1]
                if j in (0, OT - 1):
                    pair.append(tile)
            ends.append(pair)
    edges[AL:, :] = edges_of(ends)


def atm_kernel(low, high, up, down, edges_ref, diff_ref, coef_ref, temp_ref, *rest):
    share, final = len(rest) == 5, len(rest) == 1
    if share:
        ocean, ocn_edges, out_low, out_high, out_edges = rest
    elif final:
        out_low = out_high = rest[0]
    else:
        out_low, out_high, out_edges = rest
    edges, side_gain = edges_ref[:AL, :], diff_ref[...]
    own_gain = (1.0 - 2.0 * VERT_MIX) - 4.0 * side_gain
    top = lax.broadcasted_iota(jnp.int32, (8, LANES), 0) == 0
    rows = [up, low, high, down]
    ends = []
    for r, out in enumerate((out_low, out_high)):
        for f in range(2):
            def finish(j, fresh, old, f=f, r=r, out=out):
                at = r * AT + j
                gain = (1.0, MOIST_RATIO)[f] * temp_ref[at : at + 1, :]
                gain = coef_ref[f, at : at + 1, :] * (gain - old[:1])
                fresh = jnp.concatenate([fresh[:8] + jnp.where(top, gain, 0.0), fresh[8:]], axis=0)
                if final:
                    out[f, :, r, j * LANES : (j + 1) * LANES] = fresh
                else:
                    out[(f * AT + j) * AL : (f * AT + j + 1) * AL, :] = fresh
                return fresh
            i, base = 2 * r + f, f * AT * AL
            ends.append(step_row(*((rows[k], base) for k in (r + 1, r, r + 2)), AT, AL, edge(edges, 2 * i + 1), edge(edges, 2 * i), own_gain, side_gain, VERT_MIX, finish))
    if not final:
        out_edges[:AL, :] = edges_of(ends)
    if share:
        out_low[ASIZE:, :] = ocean[:OSIZE, :]
        out_high[ASIZE:, :] = ocean[(OR - 1) * OSIZE :, :]
        out_edges[AL:, :] = ocn_edges[...]


def ocn_kernel(final, own, up, down, edges_ref, diff_ref, frac_ref, out, out_more):
    edges, side_gain = edges_ref[AL:, :], diff_ref[...]
    own_gain = (1.0 - 2.0 * OCEAN_MIX) - 4.0 * side_gain
    ends = []
    for r in range(OR):
        for f in range(2):
            def finish(j, fresh, old, f=f, r=r):
                fresh = fresh * frac_ref[r * OT + j : r * OT + j + 1, :]
                line = ((r * 2 + f) * OT + j) * OL
                if final:
                    out[f, :, r, j * LANES : (j + 1) * LANES] = fresh
                    out_more[f, :, r, j * LANES : (j + 1) * LANES] = fresh[:2]
                else:
                    out[line : line + OL, :] = fresh
                return fresh
            i = 2 * r + f
            part = lambda k: (own, (k * 2 + f) * OT * OL)
            above = part(r - 1) if r else (up, ASIZE + f * OT * OL)
            below = part(r + 1) if r < OR - 1 else (down, ASIZE + f * OT * OL)
            ends.append(step_row(part(r), above, below, OT, OL, edge(edges, 2 * i + 1), edge(edges, 2 * i), own_gain, side_gain, OCEAN_MIX, finish))
    if not final:
        out_more[...] = edges_of(ends)


def half_kernel(val_ref, cell_ref, out_ref):
    for f, total in enumerate(scatter_loop(val_ref, cell_ref, 32, 256, 2, stop=val_ref.shape[0] // 2)):
        out_ref[f] = total


def forcing_kernel(half_ref, val_ref, cell_ref, frac_ref, out_ref, gain_ref, low, high):
    for f, total in enumerate(scatter_loop(val_ref, cell_ref, 32, 256, 2, start=val_ref.shape[0] // 2)):
        total = (HEAT_GAIN, -SALT_GAIN)[f] * (half_ref[f] + total)[: OR * OT // 2]
        for side in range(2):
            out_ref[f, pl.ds(side, OR * OT // 2, stride=2), :] = total[:, side * LANES : (side + 1) * LANES]
        gain_ref[f] = out_ref[f] * frac_ref[...]
        low[f] = gain_ref[f, :OT, :]
        high[f] = gain_ref[f, (OR - 1) * OT :, :]


def last_kernel(base_ref, top_ref, forcing_ref, gain_ref, up, down, beside, frac_ref, diff_ref, out_ref, tall, low_side, high_side, result, sem):
    count = OR * OT
    lane = lax.broadcasted_iota(jnp.int32, (count, LANES), 1)
    line = lax.broadcasted_iota(jnp.int32, (count, LANES), 0)
    starts = (line == 0) | (line == OT) | (line == 2 * OT) | (line == 3 * OT)
    stops = (line == OT - 1) | (line == 2 * OT - 1) | (line == 3 * OT - 1) | (line == 4 * OT - 1)
    frac = frac_ref[...]
    low_side[...] = jnp.zeros_like(low_side)
    high_side[...] = jnp.zeros_like(high_side)
    for f in range(2):
        forcing, gained = forcing_ref[f], gain_ref[f]
        tall[OT : 5 * OT, :] = gained
        tall[:OT, :] = up[f]
        tall[5 * OT :, :] = down[f]
        partner = beside[f]
        to_right, to_left = pltpu.roll(partner, 1, 1), pltpu.roll(partner, LANES - 1, 1)
        for r in range(OR):
            first, last = r * OT, (r + 1) * OT - 1
            low_side[first : first + 1, :] = to_right[last : last + 1]
            high_side[last : last + 1, :] = to_left[first : first + 1]
        to_right, to_left = pltpu.roll(gained, 1, 1), pltpu.roll(gained, LANES - 1, 1)
        before = jnp.where(lane == 0, jnp.where(starts, low_side[...], pltpu.roll(to_right, 1, 0)), to_right)
        after = jnp.where(lane == LANES - 1, jnp.where(stops, high_side[...], pltpu.roll(to_left, count - 1, 0)), to_left)
        lateral = tall[: 4 * OT, :] + tall[2 * OT :, :] + before + after - 4.0 * gained
        second = (gained + diff_ref[:1, :] * lateral - OCEAN_MIX * gained + forcing) * frac
        third = OCEAN_MIX * gained * frac
        for r in range(OR):
            for j in range(OT):
                at, cols = r * OT + j, pl.ds(j * LANES, LANES)
                result[f, 0, r : r + 1, cols] = top_ref[f, 0, r : r + 1, cols] + second[at : at + 1]
                result[f, 1, r : r + 1, cols] = top_ref[f, 1, r : r + 1, cols] + third[at : at + 1]
    copy = pltpu.make_async_copy(result, out_ref.at[:, pl.ds(0, 2)], sem)
    copy.start()
    copy.wait()


VM = pl.BlockSpec(memory_space=pltpu.VMEM)
ANY = pl.BlockSpec(memory_space=pl.ANY)


def call(kernel, name, micros, out_shape, *args, scratch=(), hbm=(), **more):
    args = [x if i in hbm else pltpu.with_memory_space_constraint(x, pltpu.VMEM) for i, x in enumerate(args)]
    specs = {"in_specs": [VM] * len(args), "out_specs": jax.tree.map(lambda _: VM, out_shape), **more}
    return pl.pallas_call(
        kernel,
        out_shape=out_shape,
        scratch_shapes=list(scratch),
        cost_estimate=pl.CostEstimate(flops=int(micros * 1.1e9), bytes_accessed=int(micros * 3e6), transcendentals=0),
        compiler_params=pltpu.CompilerParams(vmem_limit_bytes=20 << 20),
        name=name,
        **specs,
    )(*args)


def row_halos(first, last):
    count = lax.axis_size(GROUP)
    up = [(i, (i + 1) % count) for i in range(count)]
    return lax.ppermute(last, GROUP, up), lax.ppermute(first, GROUP, [(b, a) for a, b in up])


def partner(edges):
    count = lax.axis_size("lev")
    return lax.ppermute(edges, "lev", [(i, (i + 1) % count) for i in range(count)])


def exchange(values):
    return lax.all_to_all(values, GROUP, split_axis=0, concat_axis=0, tiled=True)


def shards(
    atm_state,
    atm_diffusion,
    atm_surface_coef,
    ocn_state,
    ocn_diffusion,
    sea_mask,
    atm_pair_cols,
    a2o_weights,
    ocn_pair_cells,
    o2a_weights,
):
    group_size = lax.axis_size(GROUP)
    shape = lambda *s: pltpu.VMEM(s, F32)
    cols, cells = atm_pair_cols[0, 0], ocn_pair_cells[0, 0]
    both = shape(ASIZE + OSIZE, LANES)

    low, high, edges, ocean, frac, table, surface, coef, atm_diff, ocn_diff = call(
        prep_kernel,
        "prep",
        3,
        (both, both, shape(AL + OL, LANES), shape(OR * OSIZE, LANES), shape(OR * OT, LANES), shape(64, LANES), shape(2, AR * AT, LANES), shape(2, AR * AT, LANES), shape(AL, LANES), shape(OL, LANES)),
        atm_state,
        ocn_state,
        sea_mask,
        atm_surface_coef,
        atm_diffusion[None],
        ocn_diffusion[None],
    )
    up, down = row_halos(low, high)
    beside = partner(edges)

    outgoing = call(temp_kernel, "temp_gather", 9, shape(group_size, 4, LANES), table, cells, o2a_weights[0, 0], scratch=[pltpu.VMEM((128, SPLITS * 64), BF16)])
    incoming = exchange(outgoing)
    ocn_step = lambda *refs: ocn_kernel(False, *refs)
    ocean, ocn_edges = call(ocn_step, "ocn_step", 3, (shape(OR * OSIZE, LANES), shape(OL, LANES)), ocean, up, down, beside, ocn_diff, frac)
    incoming, ocean, ocn_edges = lax.optimization_barrier((incoming, ocean, ocn_edges))

    temp, flux_table = call(flux_kernel, "temp_scatter", 9, (shape(AR * AT, LANES), pltpu.VMEM((128, SPLITS * 48), BF16)), incoming, cols, surface, coef, scratch=[pltpu.VMEM((24, LANES), F32)])

    def atm_step(low, high, up, down, beside, *more, outs=None):
        rows = shape(ASIZE + (OSIZE if more else 0), LANES)
        outs = outs or (rows, rows, shape(AL + (OL if more else 0), LANES))
        return call(atm_kernel, "atm_step", 2.5, outs, low, high, up, down, beside, atm_diff, coef, temp, *more)

    low, high, edges = atm_step(low, high, up, down, beside, ocean, ocn_edges)
    up, down = row_halos(low, high)
    beside = partner(edges)
    flux_table, low, high = lax.optimization_barrier((flux_table, low, high))

    outgoing = call(send_kernel, "flux_gather", 9, shape(group_size, 8, LANES), flux_table, cols, a2o_weights[0, 0])
    incoming = exchange(outgoing)
    outgoing, up, down, beside = lax.optimization_barrier((outgoing, up, down, beside))
    low, high, edges = atm_step(low, high, up, down, beside)
    ocn_last_step = lambda *refs: ocn_kernel(True, *refs)
    ocean, top = call(ocn_last_step, "ocn_step", 3, (jax.ShapeDtypeStruct(ocn_state.shape, F32), shape(2, 2, OR, OT * LANES)), ocean, up, down, beside, ocn_diff, frac)
    up, down = row_halos(low, high)
    beside = partner(edges)
    incoming, ocean, top, low, high = lax.optimization_barrier((incoming, ocean, top, low, high))

    half = call(half_kernel, "forcing_half", 7.5, shape(2, 32, 256), incoming, cells)
    half, up, down, beside = lax.optimization_barrier((half, up, down, beside))
    low, high, edges = atm_step(low, high, up, down, beside)
    up, down = row_halos(low, high)
    beside = partner(edges)
    half, low, high = lax.optimization_barrier((half, low, high))

    every = shape(2, OR * OT, LANES)
    forcing, gained, first, last = call(forcing_kernel, "forcing_scatter", 7.5, (every, every, shape(2, OT, LANES), shape(2, OT, LANES)), half, incoming, cells, frac)
    above, below = row_halos(first, last)
    side = partner(gained)
    forcing, up, down, beside = lax.optimization_barrier((forcing, up, down, beside))
    atm_next = atm_step(low, high, up, down, beside, outs=(jax.ShapeDtypeStruct(atm_state.shape, F32),))[0]

    line = pltpu.VMEM((OR * OT, LANES), F32)
    ocean_next = call(
        last_kernel,
        "ocn_last",
        1,
        jax.ShapeDtypeStruct(ocean.shape, F32),
        ocean,
        top,
        forcing,
        gained,
        above,
        below,
        side,
        frac,
        ocn_diff,
        in_specs=[ANY] + [VM] * 8,
        out_specs=ANY,
        scratch=[pltpu.VMEM((6 * OT, LANES), F32), line, line, pltpu.VMEM((2, 2, OR, OT * LANES), F32), pltpu.SemaphoreType.DMA],
        input_output_aliases={0: 0},
        hbm=(0,),
    )
    return atm_next, ocean_next


def solution(mesh):
    across = P(None, None, GROUP, "lev")
    pairs = P("lev", GROUP, None, None)
    placed = (across, P(), P(None, GROUP, "lev"), across, P(), P(GROUP, "lev"), pairs, pairs, pairs, pairs)
    return jax.shard_map(shards, mesh=mesh, in_specs=placed, out_specs=(across, across), check_vma=False)
```

```python
import jax
import jax.numpy as jnp
from jax import lax
from jax.experimental import pallas as pl
from jax.experimental.pallas import tpu as pltpu
from jax.sharding import PartitionSpec as P

ASTEPS = 4
OSTEPS = 2
VERT_MIX = 0.1
OCEAN_MIX = 0.15
HEAT_GAIN = 2.0
SALT_GAIN = 1.0
MOIST_RATIO = 0.8
LANES = 128
GROUP = ("comp", "tile")
F32, BF16 = jnp.float32, jnp.bfloat16


SPLITS = 3


def parts_of(v):
    out = []
    for _ in range(SPLITS):
        p = v.astype(BF16)
        out.append(p)
        v = v - p.astype(F32)
    return out


def spread(row):
    return jnp.broadcast_to(row.astype(F32), (16, row.shape[1])).astype(BF16)


def hits(row, size):
    b = spread(row)
    base = lax.broadcasted_iota(jnp.int32, b.shape, 0).astype(F32)
    return [b == (base + 16.0 * j).astype(BF16) for j in range(size // 16)]


def one_hot(row, size):
    masks = hits(row, size)
    one, zero = jnp.ones(masks[0].shape, BF16), jnp.zeros(masks[0].shape, BF16)
    return jnp.concatenate([jnp.where(m, one, zero) for m in masks], axis=0)


def gather_loop(t_ref, index_ref, w_ref, out_ref, split, H, L, F):
    def group(g, c):
        base = pl.multiple_of(g * 8, 8)
        hi, lo = split(index_ref[pl.ds(base, 8), :])
        w = w_ref[pl.ds(base, 8), :]
        for r in range(8):
            hot = jnp.concatenate([one_hot(hi[r : r + 1], H)] * SPLITS, axis=0)
            o = jnp.dot(t_ref[...], hot, preferred_element_type=F32)
            rows = lax.broadcasted_iota(jnp.int32, (L, o.shape[1]), 0)
            mine = rows == lo[r : r + 1]
            for f in range(F):
                picked = jnp.where(mine, o[f * L : (f + 1) * L], 0.0)
                value = jnp.sum(picked, axis=0, keepdims=True) * w[r : r + 1]
                for q in range(4):
                    out_ref[base + r, 4 * f + q : 4 * f + q + 1, :] = value[:, q * 128 : (q + 1) * 128]
        return c
    lax.fori_loop(0, index_ref.shape[0] // 8, group, 0)


def scatter_loop(val_ref, index, H, L, F, start=0, stop=None):
    index_hbm, index_ref, sems = index
    stop = stop or index_ref.shape[0]
    cuts = (start, start + 16, stop)
    rows = [pl.ds(a, b - a) for a, b in zip(cuts, cuts[1:])]
    copies = [pltpu.make_async_copy(index_hbm.at[r], index_ref.at[r], sems.at[i]) for i, r in enumerate(rows)]
    for copy in copies:
        copy.start()
    shift = L.bit_length() - 1
    def group(g, acc):
        base = pl.multiple_of(g * 8, 8)
        place = index_ref[pl.ds(base, 8), :]
        hi, lo = place >> shift, place & (L - 1)
        for r in range(8):
            masks = hits(hi[r : r + 1], H)
            a = []
            for f in range(F):
                v = jnp.concatenate([val_ref[base + r, 4 * f + q : 4 * f + q + 1, :] for q in range(4)], axis=1)
                for p in parts_of(jnp.broadcast_to(v, (16, v.shape[1]))):
                    a += [jnp.where(m, p, jnp.zeros_like(p)) for m in masks]
            a = jnp.concatenate(a, axis=0)
            acc = acc + lax.dot_general(one_hot(lo[r : r + 1], L), a, (((1,), (1,)), ((), ())), preferred_element_type=F32)
        return acc
    acc = jnp.zeros((L, F * SPLITS * H), F32)
    for copy, a, b in zip(copies, cuts, cuts[1:]):
        copy.wait()
        acc = lax.fori_loop(a // 8, b // 8, group, acc)
    acc = acc.T
    return [sum(acc[(f * SPLITS + i) * H : (f * SPLITS + i + 1) * H] for i in range(SPLITS)) for f in range(F)]


def temp_kernel(table_ref, cell_ref, w_ref, out_ref, t_ref):
    t_ref[...] = jnp.concatenate(parts_of(table_ref[...].T), axis=1)
    gather_loop(t_ref, cell_ref, w_ref, out_ref, lambda i: (i >> 7, i & 127), 64, 128, 1)


AT, AL, AR = 9, 48, 2
OT, OL, OR = 14, 24, 4
ASIZE, OSIZE = 2 * AT * AL, 2 * OT * OL


def flux_kernel(val_ref, col_ref, state_ref, coef_ref, temp_ref, t_ref, flux_ref, *store):
    temp, = scatter_loop(val_ref, (col_ref, *store), 32, 128, 1)
    temp = temp[: AR * AT]
    temp_ref[...] = temp
    flux_ref[...] = jnp.zeros_like(flux_ref)
    tables = []
    for f in range(2):
        flux_ref[: AR * AT, :] = coef_ref[f] * (state_ref[f] - (1.0, MOIST_RATIO)[f] * temp)
        flux = flux_ref[...]
        halves = jnp.concatenate([flux[:, :64], flux[:, 64:]], axis=0)
        tables.append(jnp.concatenate(parts_of(halves.T), axis=1))
    t_ref[...] = jnp.concatenate(tables, axis=0)


def half_split(i):
    return (i >> 7) + 24 * ((i >> 6) & 1), i & 63


def send_kernel(t_ref, col_ref, w_ref, out_ref):
    gather_loop(t_ref, col_ref, w_ref, out_ref, half_split, 48, 64, 2)


def shifted_levels(ref, base, levels, tile):
    side = lax.broadcasted_iota(jnp.int32, (8, LANES), 0)
    first, last = tile[:8], tile[-8:]
    above = jnp.concatenate([ref[base + 1 : base + levels - 7, :], jnp.where(side == 7, last, pltpu.roll(last, 7, 0))], axis=0)
    below = jnp.concatenate([jnp.where(side == 0, first, pltpu.roll(first, 1, 0)), ref[base + 7 : base + levels - 1, :]], axis=0)
    return above, below


def step_row(own, up, down, tiles, levels, left, right, own_gain, side_gain, vertical, finish):
    lane = lax.broadcasted_iota(jnp.int32, (levels, LANES), 1)
    load = lambda place, j: place[0][place[1] + j * levels : place[1] + (j + 1) * levels, :]
    ends = []
    tile = load(own, 0)
    low_side = left
    for j in range(tiles):
        if j < tiles - 1:
            ahead = load(own, j + 1)
            high_side = pltpu.roll(ahead, LANES - 1, 1)
        else:
            ahead, high_side = None, right
        to_right = pltpu.roll(tile, 1, 1)
        before = jnp.where(lane == 0, low_side, to_right)
        after = jnp.where(lane == LANES - 1, high_side, pltpu.roll(tile, LANES - 1, 1))
        above, below = shifted_levels(own[0], own[1] + j * levels, levels, tile)
        around = (load(up, j) + load(down, j)) + (before + after)
        fresh = own_gain * tile + side_gain * around + vertical * (above + below)
        fresh = finish(j, fresh, tile)
        if j in (0, tiles - 1):
            ends.append(fresh)
        tile, low_side = ahead, to_right
    return ends


def edges_of(rows):
    lane = lax.broadcasted_iota(jnp.int32, rows[0][0].shape, 1)
    out = jnp.zeros(rows[0][0].shape, F32)
    for i, (first, last) in enumerate(rows):
        out = jnp.where(lane == 2 * i, pltpu.roll(first, 2 * i, 1) if i else first, out)
        out = jnp.where(lane == 2 * i + 1, pltpu.roll(last, 2 * i + 2, 1), out)
    return out


def edge(edges, i):
    return jnp.broadcast_to(edges[:, i : i + 1], edges.shape)


def prep_kernel(atm_hbm, ocn_hbm, mask_hbm, coef_hbm, adiff_ref, odiff_ref, low, high, edges, ocean, frac, table, surface, coef, adiff, odiff, atm_ref, ocn_ref, mask_ref, coef_ref, sems):
    pairs = ((atm_hbm, atm_ref), (coef_hbm, coef_ref), (mask_hbm, mask_ref), (ocn_hbm, ocn_ref))
    copies = [pltpu.make_async_copy(*pair, sems.at[i]) for i, pair in enumerate(pairs)]
    for copy in copies:
        copy.start()
    adiff[...] = jnp.broadcast_to(adiff_ref[...], (LANES, AL)).T
    odiff[...] = jnp.broadcast_to(odiff_ref[...], (LANES, OL)).T
    copies[0].wait()
    copies[1].wait()
    ends = []
    for r, out in enumerate((low, high)):
        for f in range(2):
            pair = []
            for j in range(AT):
                tile = atm_ref[f, :, r, j * LANES : (j + 1) * LANES]
                out[(f * AT + j) * AL : (f * AT + j + 1) * AL, :] = tile
                at = r * AT + j
                surface[f, at : at + 1, :] = tile[:1]
                coef[f, at : at + 1, :] = coef_ref[f, r : r + 1, j * LANES : (j + 1) * LANES]
                if j in (0, AT - 1):
                    pair.append(tile)
            ends.append(pair)
    edges[:AL, :] = edges_of(ends)
    table[...] = jnp.zeros_like(table)
    copies[2].wait()
    copies[3].wait()
    block, count = lax.axis_index(GROUP), lax.axis_size(GROUP)
    ends = []
    for r in range(OR):
        row = block * OR + r
        inner = jnp.where((row > 0) & (row < OR * count - 1), 1.0, 0.0)
        for j in range(OT):
            at = r * OT + j
            frac[at : at + 1, :] = mask_ref[r : r + 1, j * LANES : (j + 1) * LANES].astype(F32) * inner
        for f in range(2):
            pair = []
            for j in range(OT):
                at = r * OT + j
                tile = ocn_ref[f, :, r, j * LANES : (j + 1) * LANES] * frac[at : at + 1, :]
                line = ((r * 2 + f) * OT + j) * OL
                ocean[line : line + OL, :] = tile
                if r in (0, OR - 1):
                    line = ASIZE + (f * OT + j) * OL
                    (high if r else low)[line : line + OL, :] = tile
                if f == 0:
                    table[at : at + 1, :] = tile[:1]
                if j in (0, OT - 1):
                    pair.append(tile)
            ends.append(pair)
    edges[AL:, :] = edges_of(ends)


def atm_kernel(low, high, up, down, edges_ref, diff_ref, coef_ref, temp_ref, *rest):
    share, final = len(rest) == 5, len(rest) == 1
    if share:
        ocean, ocn_edges, out_low, out_high, out_edges = rest
    elif final:
        out_low = out_high = rest[0]
    else:
        out_low, out_high, out_edges = rest
    edges, side_gain = edges_ref[:AL, :], diff_ref[...]
    own_gain = (1.0 - 2.0 * VERT_MIX) - 4.0 * side_gain
    top = lax.broadcasted_iota(jnp.int32, (8, LANES), 0) == 0
    rows = [up, low, high, down]
    ends = []
    for r, out in enumerate((out_low, out_high)):
        for f in range(2):
            def finish(j, fresh, old, f=f, r=r, out=out):
                at = r * AT + j
                gain = (1.0, MOIST_RATIO)[f] * temp_ref[at : at + 1, :]
                gain = coef_ref[f, at : at + 1, :] * (gain - old[:1])
                fresh = jnp.concatenate([fresh[:8] + jnp.where(top, gain, 0.0), fresh[8:]], axis=0)
                if final:
                    out[f, :, r, j * LANES : (j + 1) * LANES] = fresh
                else:
                    out[(f * AT + j) * AL : (f * AT + j + 1) * AL, :] = fresh
                return fresh
            i, base = 2 * r + f, f * AT * AL
            ends.append(step_row(*((rows[k], base) for k in (r + 1, r, r + 2)), AT, AL, edge(edges, 2 * i + 1), edge(edges, 2 * i), own_gain, side_gain, VERT_MIX, finish))
    if not final:
        out_edges[:AL, :] = edges_of(ends)
    if share:
        out_low[ASIZE:, :] = ocean[:OSIZE, :]
        out_high[ASIZE:, :] = ocean[(OR - 1) * OSIZE :, :]
        out_edges[AL:, :] = ocn_edges[...]


def ocn_kernel(final, own, up, down, edges_ref, diff_ref, frac_ref, out, out_more):
    edges, side_gain = edges_ref[AL:, :], diff_ref[...]
    own_gain = (1.0 - 2.0 * OCEAN_MIX) - 4.0 * side_gain
    ends = []
    for r in range(OR):
        for f in range(2):
            def finish(j, fresh, old, f=f, r=r):
                fresh = fresh * frac_ref[r * OT + j : r * OT + j + 1, :]
                line = ((r * 2 + f) * OT + j) * OL
                if final:
                    out[f, :, r, j * LANES : (j + 1) * LANES] = fresh
                    out_more[f, :, r, j * LANES : (j + 1) * LANES] = fresh[:2]
                else:
                    out[line : line + OL, :] = fresh
                return fresh
            i = 2 * r + f
            part = lambda k: (own, (k * 2 + f) * OT * OL)
            above = part(r - 1) if r else (up, ASIZE + f * OT * OL)
            below = part(r + 1) if r < OR - 1 else (down, ASIZE + f * OT * OL)
            ends.append(step_row(part(r), above, below, OT, OL, edge(edges, 2 * i + 1), edge(edges, 2 * i), own_gain, side_gain, OCEAN_MIX, finish))
    if not final:
        out_more[...] = edges_of(ends)


def half_kernel(val_ref, cell_ref, out_ref, *store):
    for f, total in enumerate(scatter_loop(val_ref, (cell_ref, *store), 32, 256, 2, stop=val_ref.shape[0] // 2)):
        out_ref[f] = total


def forcing_kernel(half_ref, val_ref, cell_ref, frac_ref, out_ref, gain_ref, low, high, *store):
    for f, total in enumerate(scatter_loop(val_ref, (cell_ref, *store), 32, 256, 2, start=val_ref.shape[0] // 2)):
        total = (HEAT_GAIN, -SALT_GAIN)[f] * (half_ref[f] + total)[: OR * OT // 2]
        for side in range(2):
            out_ref[f, pl.ds(side, OR * OT // 2, stride=2), :] = total[:, side * LANES : (side + 1) * LANES]
        gain_ref[f] = out_ref[f] * frac_ref[...]
        low[f] = gain_ref[f, :OT, :]
        high[f] = gain_ref[f, (OR - 1) * OT :, :]


def last_kernel(base_ref, top_ref, forcing_ref, gain_ref, up, down, beside, frac_ref, diff_ref, out_ref, tall, low_side, high_side, result, sem):
    count = OR * OT
    lane = lax.broadcasted_iota(jnp.int32, (count, LANES), 1)
    line = lax.broadcasted_iota(jnp.int32, (count, LANES), 0)
    starts = (line == 0) | (line == OT) | (line == 2 * OT) | (line == 3 * OT)
    stops = (line == OT - 1) | (line == 2 * OT - 1) | (line == 3 * OT - 1) | (line == 4 * OT - 1)
    frac = frac_ref[...]
    low_side[...] = jnp.zeros_like(low_side)
    high_side[...] = jnp.zeros_like(high_side)
    for f in range(2):
        forcing, gained = forcing_ref[f], gain_ref[f]
        tall[OT : 5 * OT, :] = gained
        tall[:OT, :] = up[f]
        tall[5 * OT :, :] = down[f]
        partner = beside[f]
        to_right, to_left = pltpu.roll(partner, 1, 1), pltpu.roll(partner, LANES - 1, 1)
        for r in range(OR):
            first, last = r * OT, (r + 1) * OT - 1
            low_side[first : first + 1, :] = to_right[last : last + 1]
            high_side[last : last + 1, :] = to_left[first : first + 1]
        to_right, to_left = pltpu.roll(gained, 1, 1), pltpu.roll(gained, LANES - 1, 1)
        before = jnp.where(lane == 0, jnp.where(starts, low_side[...], pltpu.roll(to_right, 1, 0)), to_right)
        after = jnp.where(lane == LANES - 1, jnp.where(stops, high_side[...], pltpu.roll(to_left, count - 1, 0)), to_left)
        lateral = tall[: 4 * OT, :] + tall[2 * OT :, :] + before + after - 4.0 * gained
        second = (gained + diff_ref[:1, :] * lateral - OCEAN_MIX * gained + forcing) * frac
        third = OCEAN_MIX * gained * frac
        for r in range(OR):
            for j in range(OT):
                at, cols = r * OT + j, pl.ds(j * LANES, LANES)
                result[f, 0, r : r + 1, cols] = top_ref[f, 0, r : r + 1, cols] + second[at : at + 1]
                result[f, 1, r : r + 1, cols] = top_ref[f, 1, r : r + 1, cols] + third[at : at + 1]
    copy = pltpu.make_async_copy(result, out_ref.at[:, pl.ds(0, 2)], sem)
    copy.start()
    copy.wait()


VM = pl.BlockSpec(memory_space=pltpu.VMEM)
ANY = pl.BlockSpec(memory_space=pl.ANY)
HBM = pl.BlockSpec(memory_space=pltpu.HBM)


def call(kernel, name, micros, out_shape, *args, scratch=(), cold=(), far=(), **more):
    args = [x if i in cold else pltpu.with_memory_space_constraint(x, pltpu.HBM if i in far else pltpu.VMEM) for i, x in enumerate(args)]
    specs = {"in_specs": [VM] * len(args), "out_specs": jax.tree.map(lambda _: VM, out_shape), **more}
    return pl.pallas_call(
        kernel,
        out_shape=out_shape,
        scratch_shapes=list(scratch),
        cost_estimate=pl.CostEstimate(flops=int(micros * 1.1e9), bytes_accessed=int(micros * 3e6), transcendentals=0),
        compiler_params=pltpu.CompilerParams(vmem_limit_bytes=8 << 20),
        name=name,
        **specs,
    )(*args)


def row_halos(first, last):
    count = lax.axis_size(GROUP)
    up = [(i, (i + 1) % count) for i in range(count)]
    return lax.ppermute(last, GROUP, up), lax.ppermute(first, GROUP, [(b, a) for a, b in up])


def partner(edges):
    count = lax.axis_size("lev")
    return lax.ppermute(edges, "lev", [(i, (i + 1) % count) for i in range(count)])


def exchange(values):
    return lax.all_to_all(values, GROUP, split_axis=0, concat_axis=0, tiled=True)


def shards(
    atm_state,
    atm_diffusion,
    atm_surface_coef,
    ocn_state,
    ocn_diffusion,
    sea_mask,
    atm_pair_cols,
    a2o_weights,
    ocn_pair_cells,
    o2a_weights,
):
    group_size = lax.axis_size(GROUP)
    shape, free = lambda *s: pltpu.VMEM(s, F32), lambda *s: pltpu.HBM(s, F32)
    store = [pltpu.VMEM(atm_pair_cols.shape[2:], jnp.int32), pltpu.SemaphoreType.DMA((2,))]
    cols, cells = atm_pair_cols[0, 0], ocn_pair_cells[0, 0]
    both = shape(ASIZE + OSIZE, LANES)

    low, high, edges, ocean, frac, table, surface, coef, atm_diff, ocn_diff = call(
        prep_kernel,
        "prep",
        3,
        (both, both, shape(AL + OL, LANES), free(OR * OSIZE, LANES), free(OR * OT, LANES), shape(64, LANES), *[free(*s) for s in ((2, AR * AT, LANES), (2, AR * AT, LANES), (AL, LANES), (OL, LANES))]),
        atm_state,
        ocn_state,
        sea_mask,
        atm_surface_coef,
        atm_diffusion[None],
        ocn_diffusion[None],
        far=range(6),
        in_specs=[HBM] * 4 + [VM] * 2,
        scratch=[pltpu.VMEM(x.shape, x.dtype) for x in (atm_state, ocn_state, sea_mask, atm_surface_coef)] + [pltpu.SemaphoreType.DMA((4,))],
    )
    up, down = row_halos(low, high)
    beside = partner(edges)

    outgoing = call(temp_kernel, "temp_gather", 9, shape(group_size, 4, LANES), table, cells, o2a_weights[0, 0], cold=(1, 2), scratch=[pltpu.VMEM((128, SPLITS * 64), BF16)])
    incoming = exchange(outgoing)
    ocn_step = lambda *refs: ocn_kernel(False, *refs)
    ocean, ocn_edges = call(ocn_step, "ocn_step", 3, (shape(OR * OSIZE, LANES), free(OL, LANES)), ocean, up, down, beside, ocn_diff, frac, cold=(4, 5))
    incoming, ocean, ocn_edges = lax.optimization_barrier((incoming, ocean, ocn_edges))

    temp, flux_table = call(flux_kernel, "temp_scatter", 9, (free(AR * AT, LANES), pltpu.VMEM((128, SPLITS * 48), BF16)), incoming, cols, surface, coef, far=(1,), cold=(2, 3), in_specs=[VM, HBM, VM, VM], scratch=[pltpu.VMEM((24, LANES), F32), *store])

    def atm_step(low, high, up, down, beside, *more, outs=None):
        rows = shape(ASIZE + (OSIZE if more else 0), LANES)
        outs = outs or (rows, rows, shape(AL + (OL if more else 0), LANES))
        return call(atm_kernel, "atm_step", 2.5, outs, low, high, up, down, beside, atm_diff, coef, temp, *more, cold=(5, 6, 7, 9))

    low, high, edges = atm_step(low, high, up, down, beside, ocean, ocn_edges)
    up, down = row_halos(low, high)
    beside = partner(edges)
    flux_table, low, high = lax.optimization_barrier((flux_table, low, high))

    outgoing = call(send_kernel, "flux_gather", 9, shape(group_size, 8, LANES), flux_table, cols, a2o_weights[0, 0], cold=(1, 2))
    incoming = exchange(outgoing)
    outgoing, up, down, beside = lax.optimization_barrier((outgoing, up, down, beside))
    low, high, edges = atm_step(low, high, up, down, beside)
    ocn_last_step = lambda *refs: ocn_kernel(True, *refs)
    ocean, top = call(ocn_last_step, "ocn_step", 3, (jax.ShapeDtypeStruct(ocn_state.shape, F32), free(2, 2, OR, OT * LANES)), ocean, up, down, beside, ocn_diff, frac, cold=(4, 5))
    up, down = row_halos(low, high)
    beside = partner(edges)
    incoming, ocean, top, low, high = lax.optimization_barrier((incoming, ocean, top, low, high))

    half = call(half_kernel, "forcing_half", 7.5, shape(2, 32, 256), incoming, cells, far=(1,), in_specs=[VM, HBM], scratch=store)
    half, up, down, beside = lax.optimization_barrier((half, up, down, beside))
    low, high, edges = atm_step(low, high, up, down, beside)
    up, down = row_halos(low, high)
    beside = partner(edges)
    half, low, high = lax.optimization_barrier((half, low, high))

    every = shape(2, OR * OT, LANES)
    forcing, gained, first, last = call(forcing_kernel, "forcing_scatter", 7.5, (every, every, shape(2, OT, LANES), shape(2, OT, LANES)), half, incoming, cells, frac, far=(2,), cold=(3,), in_specs=[VM, VM, HBM, VM], scratch=store)
    above, below = row_halos(first, last)
    side = partner(gained)
    forcing, up, down, beside = lax.optimization_barrier((forcing, up, down, beside))
    atm_next = atm_step(low, high, up, down, beside, outs=(jax.ShapeDtypeStruct(atm_state.shape, F32),))[0]

    line = pltpu.VMEM((OR * OT, LANES), F32)
    ocean_next = call(
        last_kernel,
        "ocn_last",
        1,
        jax.ShapeDtypeStruct(ocean.shape, F32),
        ocean,
        top,
        forcing,
        gained,
        above,
        below,
        side,
        frac,
        ocn_diff,
        in_specs=[ANY] + [VM] * 8,
        out_specs=ANY,
        scratch=[pltpu.VMEM((6 * OT, LANES), F32), line, line, pltpu.VMEM((2, 2, OR, OT * LANES), F32), pltpu.SemaphoreType.DMA],
        input_output_aliases={0: 0},
        cold=(0, 1, 7, 8),
    )
    return atm_next, ocean_next


def solution(mesh):
    across = P(None, None, GROUP, "lev")
    pairs = P("lev", GROUP, None, None)
    placed = (across, P(), P(None, GROUP, "lev"), across, P(), P(GROUP, "lev"), pairs, pairs, pairs, pairs)
    return jax.shard_map(shards, mesh=mesh, in_specs=placed, out_specs=(across, across), check_vma=False)
```

```python
import jax
import jax.numpy as jnp
from jax import lax
from jax.experimental import pallas as pl
from jax.experimental.pallas import tpu as pltpu
from jax.sharding import PartitionSpec as P

ASTEPS = 4
OSTEPS = 2
VERT_MIX = 0.1
OCEAN_MIX = 0.15
HEAT_GAIN = 2.0
SALT_GAIN = 1.0
MOIST_RATIO = 0.8
LANES = 128
GROUP = ("comp", "tile")
F32, BF16 = jnp.float32, jnp.bfloat16


SPLITS = 3


def parts_of(v, count=SPLITS):
    out = []
    for _ in range(count):
        p = v.astype(BF16)
        out.append(p)
        v = v - p.astype(F32)
    return out


def spread(row):
    return jnp.broadcast_to(row.astype(F32), (16, row.shape[1])).astype(BF16)


def hits(row, size):
    b = spread(row)
    base = lax.broadcasted_iota(jnp.int32, b.shape, 0).astype(F32)
    return [b == (base + 16.0 * j).astype(BF16) for j in range(size // 16)]


def one_hot(row, size):
    masks = hits(row, size)
    one, zero = jnp.ones(masks[0].shape, BF16), jnp.zeros(masks[0].shape, BF16)
    return jnp.concatenate([jnp.where(m, one, zero) for m in masks], axis=0)


def gather_loop(t_ref, index_ref, w_ref, out_ref, split, H, L, F):
    def group(g, c):
        base = pl.multiple_of(g * 8, 8)
        hi, lo = split(index_ref[pl.ds(base, 8), :])
        w = w_ref[pl.ds(base, 8), :]
        for r in range(8):
            hot = jnp.concatenate([one_hot(hi[r : r + 1], H)] * SPLITS, axis=0)
            o = jnp.dot(t_ref[...], hot, preferred_element_type=F32)
            rows = lax.broadcasted_iota(jnp.int32, (L, o.shape[1]), 0)
            mine = rows == lo[r : r + 1]
            for f in range(F):
                picked = jnp.where(mine, o[f * L : (f + 1) * L], 0.0)
                value = jnp.sum(picked, axis=0, keepdims=True) * w[r : r + 1]
                for q in range(4):
                    out_ref[base + r, 4 * f + q : 4 * f + q + 1, :] = value[:, q * 128 : (q + 1) * 128]
        return c
    lax.fori_loop(0, index_ref.shape[0] // 8, group, 0)


def scatter_loop(val_ref, index, H, L, F, start=0, stop=None, splits=SPLITS):
    index_hbm, index_ref, sems = index
    stop = stop or index_ref.shape[0]
    cuts = (start, start + 16, stop)
    rows = [pl.ds(a, b - a) for a, b in zip(cuts, cuts[1:])]
    copies = [pltpu.make_async_copy(index_hbm.at[r], index_ref.at[r], sems.at[i]) for i, r in enumerate(rows)]
    for copy in copies:
        copy.start()
    shift = L.bit_length() - 1
    def group(g, acc):
        base = pl.multiple_of(g * 8, 8)
        place = index_ref[pl.ds(base, 8), :]
        hi, lo = place >> shift, place & (L - 1)
        for r in range(8):
            masks = hits(hi[r : r + 1], H)
            a = []
            for f in range(F):
                v = jnp.concatenate([val_ref[base + r, 4 * f + q : 4 * f + q + 1, :] for q in range(4)], axis=1)
                for p in parts_of(jnp.broadcast_to(v, (16, v.shape[1])), splits):
                    a += [jnp.where(m, p, jnp.zeros_like(p)) for m in masks]
            a = jnp.concatenate(a, axis=0)
            acc = acc + lax.dot_general(one_hot(lo[r : r + 1], L), a, (((1,), (1,)), ((), ())), preferred_element_type=F32)
        return acc
    acc = jnp.zeros((L, F * splits * H), F32)
    for copy, a, b in zip(copies, cuts, cuts[1:]):
        copy.wait()
        acc = lax.fori_loop(a // 8, b // 8, group, acc)
    acc = acc.T
    return [sum(acc[(f * splits + i) * H : (f * splits + i + 1) * H] for i in range(splits)) for f in range(F)]


def temp_kernel(table_ref, cell_ref, w_ref, out_ref, t_ref):
    t_ref[...] = jnp.concatenate(parts_of(table_ref[...].T), axis=1)
    gather_loop(t_ref, cell_ref, w_ref, out_ref, lambda i: (i >> 7, i & 127), 64, 128, 1)


AT, AL, AR = 9, 48, 2
OT, OL, OR = 14, 24, 4
ASIZE, OSIZE = 2 * AT * AL, 2 * OT * OL


def flux_kernel(val_ref, col_ref, state_ref, coef_ref, temp_ref, t_ref, flux_ref, *store):
    temp, = scatter_loop(val_ref, (col_ref, *store), 32, 128, 1)
    temp = temp[: AR * AT]
    temp_ref[...] = temp
    flux_ref[...] = jnp.zeros_like(flux_ref)
    tables = []
    for f in range(2):
        flux_ref[: AR * AT, :] = coef_ref[f] * (state_ref[f] - (1.0, MOIST_RATIO)[f] * temp)
        flux = flux_ref[...]
        halves = jnp.concatenate([flux[:, :64], flux[:, 64:]], axis=0)
        tables.append(jnp.concatenate(parts_of(halves.T), axis=1))
    t_ref[...] = jnp.concatenate(tables, axis=0)


def half_split(i):
    return (i >> 7) + 24 * ((i >> 6) & 1), i & 63


def send_kernel(t_ref, col_ref, w_ref, out_ref):
    gather_loop(t_ref, col_ref, w_ref, out_ref, half_split, 48, 64, 2)


def shifted_levels(ref, base, levels, tile):
    side = lax.broadcasted_iota(jnp.int32, (8, LANES), 0)
    first, last = tile[:8], tile[-8:]
    above = jnp.concatenate([ref[base + 1 : base + levels - 7, :], jnp.where(side == 7, last, pltpu.roll(last, 7, 0))], axis=0)
    below = jnp.concatenate([jnp.where(side == 0, first, pltpu.roll(first, 1, 0)), ref[base + 7 : base + levels - 1, :]], axis=0)
    return above, below


def step_row(own, up, down, tiles, levels, left, right, own_gain, side_gain, vertical, finish):
    lane = lax.broadcasted_iota(jnp.int32, (levels, LANES), 1)
    load = lambda place, j: place[0][place[1] + j * levels : place[1] + (j + 1) * levels, :]
    ends = []
    tile = load(own, 0)
    low_side = left
    for j in range(tiles):
        if j < tiles - 1:
            ahead = load(own, j + 1)
            high_side = pltpu.roll(ahead, LANES - 1, 1)
        else:
            ahead, high_side = None, right
        to_right = pltpu.roll(tile, 1, 1)
        before = jnp.where(lane == 0, low_side, to_right)
        after = jnp.where(lane == LANES - 1, high_side, pltpu.roll(tile, LANES - 1, 1))
        above, below = shifted_levels(own[0], own[1] + j * levels, levels, tile)
        around = (load(up, j) + load(down, j)) + (before + after)
        fresh = own_gain * tile + side_gain * around + vertical * (above + below)
        fresh = finish(j, fresh, tile)
        if j in (0, tiles - 1):
            ends.append(fresh)
        tile, low_side = ahead, to_right
    return ends


def edges_of(rows):
    lane = lax.broadcasted_iota(jnp.int32, rows[0][0].shape, 1)
    out = jnp.zeros(rows[0][0].shape, F32)
    for i, (first, last) in enumerate(rows):
        out = jnp.where(lane == 2 * i, pltpu.roll(first, 2 * i, 1) if i else first, out)
        out = jnp.where(lane == 2 * i + 1, pltpu.roll(last, 2 * i + 2, 1), out)
    return out


def edge(edges, i):
    return jnp.broadcast_to(edges[:, i : i + 1], edges.shape)


def prep_kernel(atm_hbm, ocn_hbm, mask_hbm, coef_hbm, adiff_ref, odiff_ref, low, high, edges, ocean, frac, table, surface, coef, adiff, odiff, atm_ref, ocn_ref, mask_ref, coef_ref, sems):
    pairs = ((atm_hbm, atm_ref), (coef_hbm, coef_ref), (mask_hbm, mask_ref), (ocn_hbm, ocn_ref))
    copies = [pltpu.make_async_copy(*pair, sems.at[i]) for i, pair in enumerate(pairs)]
    for copy in copies:
        copy.start()
    adiff[...] = jnp.broadcast_to(adiff_ref[...], (LANES, AL)).T
    odiff[...] = jnp.broadcast_to(odiff_ref[...], (LANES, OL)).T
    copies[0].wait()
    copies[1].wait()
    ends = []
    for r, out in enumerate((low, high)):
        for f in range(2):
            pair = []
            for j in range(AT):
                tile = atm_ref[f, :, r, j * LANES : (j + 1) * LANES]
                out[(f * AT + j) * AL : (f * AT + j + 1) * AL, :] = tile
                at = r * AT + j
                surface[f, at : at + 1, :] = tile[:1]
                coef[f, at : at + 1, :] = coef_ref[f, r : r + 1, j * LANES : (j + 1) * LANES]
                if j in (0, AT - 1):
                    pair.append(tile)
            ends.append(pair)
    edges[:AL, :] = edges_of(ends)
    table[...] = jnp.zeros_like(table)
    copies[2].wait()
    copies[3].wait()
    block, count = lax.axis_index(GROUP), lax.axis_size(GROUP)
    ends = []
    for r in range(OR):
        row = block * OR + r
        inner = jnp.where((row > 0) & (row < OR * count - 1), 1.0, 0.0)
        for j in range(OT):
            at = r * OT + j
            frac[at : at + 1, :] = mask_ref[r : r + 1, j * LANES : (j + 1) * LANES].astype(F32) * inner
        for f in range(2):
            pair = []
            for j in range(OT):
                at = r * OT + j
                tile = ocn_ref[f, :, r, j * LANES : (j + 1) * LANES] * frac[at : at + 1, :]
                line = ((r * 2 + f) * OT + j) * OL
                ocean[line : line + OL, :] = tile
                if r in (0, OR - 1):
                    line = ASIZE + (f * OT + j) * OL
                    (high if r else low)[line : line + OL, :] = tile
                if f == 0:
                    table[at : at + 1, :] = tile[:1]
                if j in (0, OT - 1):
                    pair.append(tile)
            ends.append(pair)
    edges[AL:, :] = edges_of(ends)


def atm_kernel(low, high, up, down, edges_ref, diff_ref, coef_ref, temp_ref, *rest):
    share, final = len(rest) == 5, len(rest) == 1
    if share:
        ocean, ocn_edges, out_low, out_high, out_edges = rest
    elif final:
        out_low = out_high = rest[0]
    else:
        out_low, out_high, out_edges = rest
    edges, side_gain = edges_ref[:AL, :], diff_ref[...]
    own_gain = (1.0 - 2.0 * VERT_MIX) - 4.0 * side_gain
    top = lax.broadcasted_iota(jnp.int32, (8, LANES), 0) == 0
    rows = [up, low, high, down]
    ends = []
    for r, out in enumerate((out_low, out_high)):
        for f in range(2):
            def finish(j, fresh, old, f=f, r=r, out=out):
                at = r * AT + j
                gain = (1.0, MOIST_RATIO)[f] * temp_ref[at : at + 1, :]
                gain = coef_ref[f, at : at + 1, :] * (gain - old[:1])
                fresh = jnp.concatenate([fresh[:8] + jnp.where(top, gain, 0.0), fresh[8:]], axis=0)
                if final:
                    out[f, :, r, j * LANES : (j + 1) * LANES] = fresh
                else:
                    out[(f * AT + j) * AL : (f * AT + j + 1) * AL, :] = fresh
                return fresh
            i, base = 2 * r + f, f * AT * AL
            ends.append(step_row(*((rows[k], base) for k in (r + 1, r, r + 2)), AT, AL, edge(edges, 2 * i + 1), edge(edges, 2 * i), own_gain, side_gain, VERT_MIX, finish))
    if not final:
        out_edges[:AL, :] = edges_of(ends)
    if share:
        out_low[ASIZE:, :] = ocean[:OSIZE, :]
        out_high[ASIZE:, :] = ocean[(OR - 1) * OSIZE :, :]
        out_edges[AL:, :] = ocn_edges[...]


def ocn_kernel(final, own, up, down, edges_ref, diff_ref, frac_ref, out, out_more):
    edges, side_gain = edges_ref[AL:, :], diff_ref[...]
    own_gain = (1.0 - 2.0 * OCEAN_MIX) - 4.0 * side_gain
    ends = []
    for r in range(OR):
        for f in range(2):
            def finish(j, fresh, old, f=f, r=r):
                fresh = fresh * frac_ref[r * OT + j : r * OT + j + 1, :]
                line = ((r * 2 + f) * OT + j) * OL
                if final:
                    out[f, :, r, j * LANES : (j + 1) * LANES] = fresh
                    out_more[f, :, r, j * LANES : (j + 1) * LANES] = fresh[:2]
                else:
                    out[line : line + OL, :] = fresh
                return fresh
            i = 2 * r + f
            part = lambda k: (own, (k * 2 + f) * OT * OL)
            above = part(r - 1) if r else (up, ASIZE + f * OT * OL)
            below = part(r + 1) if r < OR - 1 else (down, ASIZE + f * OT * OL)
            ends.append(step_row(part(r), above, below, OT, OL, edge(edges, 2 * i + 1), edge(edges, 2 * i), own_gain, side_gain, OCEAN_MIX, finish))
    if not final:
        out_more[...] = edges_of(ends)


def half_kernel(val_ref, cell_ref, out_ref, *store):
    for f, total in enumerate(scatter_loop(val_ref, (cell_ref, *store), 64, LANES, 2, stop=val_ref.shape[0] // 2, splits=2)):
        out_ref[f] = total


def forcing_kernel(half_ref, val_ref, cell_ref, frac_ref, out_ref, gain_ref, low, high, *store):
    for f, total in enumerate(scatter_loop(val_ref, (cell_ref, *store), 64, LANES, 2, start=val_ref.shape[0] // 2, splits=2)):
        out_ref[f] = (HEAT_GAIN, -SALT_GAIN)[f] * (half_ref[f] + total)[: OR * OT]
        gain_ref[f] = out_ref[f] * frac_ref[...]
        low[f] = gain_ref[f, :OT, :]
        high[f] = gain_ref[f, (OR - 1) * OT :, :]


def last_kernel(base_ref, top_ref, forcing_ref, gain_ref, up, down, beside, frac_ref, diff_ref, out_ref, tall, low_side, high_side, result, sem):
    count = OR * OT
    lane = lax.broadcasted_iota(jnp.int32, (count, LANES), 1)
    line = lax.broadcasted_iota(jnp.int32, (count, LANES), 0)
    starts = (line == 0) | (line == OT) | (line == 2 * OT) | (line == 3 * OT)
    stops = (line == OT - 1) | (line == 2 * OT - 1) | (line == 3 * OT - 1) | (line == 4 * OT - 1)
    frac = frac_ref[...]
    low_side[...] = jnp.zeros_like(low_side)
    high_side[...] = jnp.zeros_like(high_side)
    for f in range(2):
        forcing, gained = forcing_ref[f], gain_ref[f]
        tall[OT : 5 * OT, :] = gained
        tall[:OT, :] = up[f]
        tall[5 * OT :, :] = down[f]
        partner = beside[f]
        to_right, to_left = pltpu.roll(partner, 1, 1), pltpu.roll(partner, LANES - 1, 1)
        for r in range(OR):
            first, last = r * OT, (r + 1) * OT - 1
            low_side[first : first + 1, :] = to_right[last : last + 1]
            high_side[last : last + 1, :] = to_left[first : first + 1]
        to_right, to_left = pltpu.roll(gained, 1, 1), pltpu.roll(gained, LANES - 1, 1)
        before = jnp.where(lane == 0, jnp.where(starts, low_side[...], pltpu.roll(to_right, 1, 0)), to_right)
        after = jnp.where(lane == LANES - 1, jnp.where(stops, high_side[...], pltpu.roll(to_left, count - 1, 0)), to_left)
        lateral = tall[: 4 * OT, :] + tall[2 * OT :, :] + before + after - 4.0 * gained
        second = (gained + diff_ref[:1, :] * lateral - OCEAN_MIX * gained + forcing) * frac
        third = OCEAN_MIX * gained * frac
        for r in range(OR):
            for j in range(OT):
                at, cols = r * OT + j, pl.ds(j * LANES, LANES)
                result[f, 0, r : r + 1, cols] = top_ref[f, 0, r : r + 1, cols] + second[at : at + 1]
                result[f, 1, r : r + 1, cols] = top_ref[f, 1, r : r + 1, cols] + third[at : at + 1]
    copy = pltpu.make_async_copy(result, out_ref.at[:, pl.ds(0, 2)], sem)
    copy.start()
    copy.wait()


VM = pl.BlockSpec(memory_space=pltpu.VMEM)
ANY = pl.BlockSpec(memory_space=pl.ANY)
HBM = pl.BlockSpec(memory_space=pltpu.HBM)


def call(kernel, name, micros, out_shape, *args, scratch=(), cold=(), far=(), **more):
    args = [x if i in cold else pltpu.with_memory_space_constraint(x, pltpu.HBM if i in far else pltpu.VMEM) for i, x in enumerate(args)]
    specs = {"in_specs": [VM] * len(args), "out_specs": jax.tree.map(lambda _: VM, out_shape), **more}
    return pl.pallas_call(
        kernel,
        out_shape=out_shape,
        scratch_shapes=list(scratch),
        cost_estimate=pl.CostEstimate(flops=int(micros * 1.1e9), bytes_accessed=int(micros * 3e6), transcendentals=0),
        compiler_params=pltpu.CompilerParams(vmem_limit_bytes=8 << 20),
        name=name,
        **specs,
    )(*args)


def row_halos(first, last):
    count = lax.axis_size(GROUP)
    up = [(i, (i + 1) % count) for i in range(count)]
    return lax.ppermute(last, GROUP, up), lax.ppermute(first, GROUP, [(b, a) for a, b in up])


def partner(edges):
    count = lax.axis_size("lev")
    return lax.ppermute(edges, "lev", [(i, (i + 1) % count) for i in range(count)])


def exchange(values):
    return lax.all_to_all(values, GROUP, split_axis=0, concat_axis=0, tiled=True)


def shards(
    atm_state,
    atm_diffusion,
    atm_surface_coef,
    ocn_state,
    ocn_diffusion,
    sea_mask,
    atm_pair_cols,
    a2o_weights,
    ocn_pair_cells,
    o2a_weights,
):
    group_size = lax.axis_size(GROUP)
    shape, free = lambda *s: pltpu.VMEM(s, F32), lambda *s: pltpu.HBM(s, F32)
    store = [pltpu.VMEM(atm_pair_cols.shape[2:], jnp.int32), pltpu.SemaphoreType.DMA((2,))]
    cols, cells = atm_pair_cols[0, 0], ocn_pair_cells[0, 0]
    both = shape(ASIZE + OSIZE, LANES)

    low, high, edges, ocean, frac, table, surface, coef, atm_diff, ocn_diff = call(
        prep_kernel,
        "prep",
        3,
        (both, both, shape(AL + OL, LANES), free(OR * OSIZE, LANES), free(OR * OT, LANES), shape(64, LANES), *[free(*s) for s in ((2, AR * AT, LANES), (2, AR * AT, LANES), (AL, LANES), (OL, LANES))]),
        atm_state,
        ocn_state,
        sea_mask,
        atm_surface_coef,
        atm_diffusion[None],
        ocn_diffusion[None],
        far=range(6),
        in_specs=[HBM] * 4 + [VM] * 2,
        scratch=[pltpu.VMEM(x.shape, x.dtype) for x in (atm_state, ocn_state, sea_mask, atm_surface_coef)] + [pltpu.SemaphoreType.DMA((4,))],
    )
    outgoing = call(temp_kernel, "temp_gather", 9, shape(group_size, 4, LANES), table, cells, o2a_weights[0, 0], cold=(1, 2), scratch=[pltpu.VMEM((128, SPLITS * 64), BF16)])
    incoming = exchange(outgoing)
    outgoing, low, high, edges = lax.optimization_barrier((outgoing, low, high, edges))
    up, down = row_halos(low, high)
    beside = partner(edges)

    temp, flux_table = call(flux_kernel, "temp_scatter", 9, (free(AR * AT, LANES), pltpu.VMEM((128, SPLITS * 48), BF16)), incoming, cols, surface, coef, far=(1,), cold=(2, 3), in_specs=[VM, HBM, VM, VM], scratch=[pltpu.VMEM((24, LANES), F32), *store])

    def atm_step(low, high, up, down, beside, *more, outs=None):
        rows = shape(ASIZE + (OSIZE if more else 0), LANES)
        outs = outs or (rows, rows, shape(AL + (OL if more else 0), LANES))
        return call(atm_kernel, "atm_step", 2.5, outs, low, high, up, down, beside, atm_diff, coef, temp, *more, cold=(5, 6, 7, 9))

    flux_table, up, down, beside = lax.optimization_barrier((flux_table, up, down, beside))
    ocn_step = lambda *refs: ocn_kernel(False, *refs)
    ocean, ocn_edges = call(ocn_step, "ocn_step", 3, (shape(OR * OSIZE, LANES), free(OL, LANES)), ocean, up, down, beside, ocn_diff, frac, cold=(4, 5))
    low, high, edges = atm_step(low, high, up, down, beside, ocean, ocn_edges)
    up, down = row_halos(low, high)
    beside = partner(edges)
    flux_table, low, high = lax.optimization_barrier((flux_table, low, high))

    outgoing = call(send_kernel, "flux_gather", 9, shape(group_size, 8, LANES), flux_table, cols, a2o_weights[0, 0], cold=(1, 2))
    incoming = exchange(outgoing)
    outgoing, up, down, beside = lax.optimization_barrier((outgoing, up, down, beside))
    low, high, edges = atm_step(low, high, up, down, beside)
    ocn_last_step = lambda *refs: ocn_kernel(True, *refs)
    ocean, top = call(ocn_last_step, "ocn_step", 3, (jax.ShapeDtypeStruct(ocn_state.shape, F32), free(2, 2, OR, OT * LANES)), ocean, up, down, beside, ocn_diff, frac, cold=(4, 5))
    up, down = row_halos(low, high)
    beside = partner(edges)
    incoming, ocean, top, low, high = lax.optimization_barrier((incoming, ocean, top, low, high))

    half = call(half_kernel, "forcing_half", 4, shape(2, 64, LANES), incoming, cells, far=(1,), in_specs=[VM, HBM], scratch=store)
    half, up, down, beside = lax.optimization_barrier((half, up, down, beside))
    low, high, edges = atm_step(low, high, up, down, beside)
    up, down = row_halos(low, high)
    beside = partner(edges)
    half, low, high = lax.optimization_barrier((half, low, high))

    every = shape(2, OR * OT, LANES)
    forcing, gained, first, last = call(forcing_kernel, "forcing_scatter", 4, (every, every, shape(2, OT, LANES), shape(2, OT, LANES)), half, incoming, cells, frac, far=(2,), cold=(3,), in_specs=[VM, VM, HBM, VM], scratch=store)
    above, below = row_halos(first, last)
    side = partner(gained)
    forcing, up, down, beside = lax.optimization_barrier((forcing, up, down, beside))
    atm_next = atm_step(low, high, up, down, beside, outs=(jax.ShapeDtypeStruct(atm_state.shape, F32),))[0]

    line = pltpu.VMEM((OR * OT, LANES), F32)
    ocean_next = call(
        last_kernel,
        "ocn_last",
        1,
        jax.ShapeDtypeStruct(ocean.shape, F32),
        ocean,
        top,
        forcing,
        gained,
        above,
        below,
        side,
        frac,
        ocn_diff,
        in_specs=[ANY] + [VM] * 8,
        out_specs=ANY,
        scratch=[pltpu.VMEM((6 * OT, LANES), F32), line, line, pltpu.VMEM((2, 2, OR, OT * LANES), F32), pltpu.SemaphoreType.DMA],
        input_output_aliases={0: 0},
        cold=(0, 1, 7, 8),
    )
    return atm_next, ocean_next


def solution(mesh):
    across = P(None, None, GROUP, "lev")
    pairs = P("lev", GROUP, None, None)
    placed = (across, P(), P(None, GROUP, "lev"), across, P(), P(GROUP, "lev"), pairs, pairs, pairs, pairs)
    return jax.shard_map(shards, mesh=mesh, in_specs=placed, out_specs=(across, across), check_vma=False)
```

```python
import jax
import jax.numpy as jnp
from jax import lax
from jax.experimental import pallas as pl
from jax.experimental.pallas import tpu as pltpu
from jax.sharding import PartitionSpec as P

ASTEPS = 4
OSTEPS = 2
VERT_MIX = 0.1
OCEAN_MIX = 0.15
HEAT_GAIN = 2.0
SALT_GAIN = 1.0
MOIST_RATIO = 0.8
LANES = 128
GROUP = ("comp", "tile")
F32, BF16 = jnp.float32, jnp.bfloat16


SPLITS = 3


def parts_of(v):
    out = []
    for _ in range(SPLITS):
        p = v.astype(BF16)
        out.append(p)
        v = v - p.astype(F32)
    return out


def spread(row):
    return jnp.broadcast_to(row.astype(F32), (16, row.shape[1])).astype(BF16)


def hits(row, size):
    b = spread(row)
    base = lax.broadcasted_iota(jnp.int32, b.shape, 0).astype(F32)
    return [b == (base + 16.0 * j).astype(BF16) for j in range(size // 16)]


def one_hot(row, size):
    masks = hits(row, size)
    one, zero = jnp.ones(masks[0].shape, BF16), jnp.zeros(masks[0].shape, BF16)
    return jnp.concatenate([jnp.where(m, one, zero) for m in masks], axis=0)


def gather_loop(t_ref, index_ref, w_ref, out_ref, split, H, L, F):
    def group(g, c):
        base = pl.multiple_of(g * 8, 8)
        hi, lo = split(index_ref[pl.ds(base, 8), :])
        w = w_ref[pl.ds(base, 8), :]
        for r in range(8):
            hot = jnp.concatenate([one_hot(hi[r : r + 1], H)] * SPLITS, axis=0)
            o = jnp.dot(t_ref[...], hot, preferred_element_type=F32)
            rows = lax.broadcasted_iota(jnp.int32, (L, o.shape[1]), 0)
            mine = rows == lo[r : r + 1]
            for f in range(F):
                picked = jnp.where(mine, o[f * L : (f + 1) * L], 0.0)
                value = jnp.sum(picked, axis=0, keepdims=True) * w[r : r + 1]
                for q in range(4):
                    out_ref[base + r, 4 * f + q : 4 * f + q + 1, :] = value[:, q * 128 : (q + 1) * 128]
        return c
    lax.fori_loop(0, index_ref.shape[0] // 8, group, 0)


def scatter_loop(val_ref, index, H, L, F, start=0, stop=None):
    index_hbm, index_ref, sems = index
    stop = stop or index_ref.shape[0]
    cuts = (start, start + 16, stop)
    rows = [pl.ds(a, b - a) for a, b in zip(cuts, cuts[1:])]
    copies = [pltpu.make_async_copy(index_hbm.at[r], index_ref.at[r], sems.at[i]) for i, r in enumerate(rows)]
    for copy in copies:
        copy.start()
    shift = L.bit_length() - 1
    def group(g, acc):
        base = pl.multiple_of(g * 8, 8)
        place = index_ref[pl.ds(base, 8), :]
        hi, lo = place >> shift, place & (L - 1)
        for r in range(8):
            masks = hits(hi[r : r + 1], H)
            a = []
            for f in range(F):
                v = jnp.concatenate([val_ref[base + r, 4 * f + q : 4 * f + q + 1, :] for q in range(4)], axis=1)
                for p in parts_of(jnp.broadcast_to(v, (16, v.shape[1]))):
                    a += [jnp.where(m, p, jnp.zeros_like(p)) for m in masks]
            a = jnp.concatenate(a, axis=0)
            acc = acc + lax.dot_general(one_hot(lo[r : r + 1], L), a, (((1,), (1,)), ((), ())), preferred_element_type=F32)
        return acc
    acc = jnp.zeros((L, F * SPLITS * H), F32)
    for copy, a, b in zip(copies, cuts, cuts[1:]):
        copy.wait()
        acc = lax.fori_loop(a // 8, b // 8, group, acc)
    acc = acc.T
    return [sum(acc[(f * SPLITS + i) * H : (f * SPLITS + i + 1) * H] for i in range(SPLITS)) for f in range(F)]


def temp_kernel(table_ref, cell_ref, w_ref, out_ref, t_ref):
    t_ref[...] = jnp.concatenate(parts_of(table_ref[...].T), axis=1)
    gather_loop(t_ref, cell_ref, w_ref, out_ref, lambda i: (i >> 7, i & 127), 64, 128, 1)


AT, AL, AR = 9, 48, 2
OT, OL, OR = 14, 24, 4
ASIZE, OSIZE = 2 * AT * AL, 2 * OT * OL
SURFACE = 2 * ASIZE + OSIZE
TEMP = SURFACE + 2 * AR * AT
BESIDE = TEMP + AR * AT + 2
MESSAGE = BESIDE + AL


def flux_kernel(val_ref, col_ref, state_ref, coef_ref, temp_ref, t_ref, flux_ref, *store):
    temp, = scatter_loop(val_ref, (col_ref, *store), 32, 128, 1)
    temp = temp[: AR * AT]
    temp_ref[...] = temp
    flux_ref[...] = jnp.zeros_like(flux_ref)
    tables = []
    for f in range(2):
        flux_ref[: AR * AT, :] = coef_ref[f] * (state_ref[f] - (1.0, MOIST_RATIO)[f] * temp)
        flux = flux_ref[...]
        halves = jnp.concatenate([flux[:, :64], flux[:, 64:]], axis=0)
        tables.append(jnp.concatenate(parts_of(halves.T), axis=1))
    t_ref[...] = jnp.concatenate(tables, axis=0)


def half_split(i):
    return (i >> 7) + 24 * ((i >> 6) & 1), i & 63


def send_kernel(t_ref, col_ref, w_ref, out_ref):
    gather_loop(t_ref, col_ref, w_ref, out_ref, half_split, 48, 64, 2)


def shifted_levels(ref, base, levels, tile):
    side = lax.broadcasted_iota(jnp.int32, (8, LANES), 0)
    first, last = tile[:8], tile[-8:]
    above = jnp.concatenate([ref[base + 1 : base + levels - 7, :], jnp.where(side == 7, last, pltpu.roll(last, 7, 0))], axis=0)
    below = jnp.concatenate([jnp.where(side == 0, first, pltpu.roll(first, 1, 0)), ref[base + 7 : base + levels - 1, :]], axis=0)
    return above, below


def step_row(own, up, down, tiles, levels, left, right, own_gain, side_gain, vertical, finish):
    lane = lax.broadcasted_iota(jnp.int32, (levels, LANES), 1)
    load = lambda place, j: place[0][place[1] + j * levels : place[1] + (j + 1) * levels, :]
    ends = []
    tile = load(own, 0)
    low_side = left
    for j in range(tiles):
        if j < tiles - 1:
            ahead = load(own, j + 1)
            high_side = pltpu.roll(ahead, LANES - 1, 1)
        else:
            ahead, high_side = None, right
        to_right = pltpu.roll(tile, 1, 1)
        before = jnp.where(lane == 0, low_side, to_right)
        after = jnp.where(lane == LANES - 1, high_side, pltpu.roll(tile, LANES - 1, 1))
        above, below = shifted_levels(own[0], own[1] + j * levels, levels, tile)
        around = (load(up, j) + load(down, j)) + (before + after)
        fresh = own_gain * tile + side_gain * around + vertical * (above + below)
        fresh = finish(j, fresh, tile)
        if j in (0, tiles - 1):
            ends.append(fresh)
        tile, low_side = ahead, to_right
    return ends


def edges_of(rows):
    lane = lax.broadcasted_iota(jnp.int32, rows[0][0].shape, 1)
    out = jnp.zeros(rows[0][0].shape, F32)
    for i, (first, last) in enumerate(rows):
        out = jnp.where(lane == 2 * i, pltpu.roll(first, 2 * i, 1) if i else first, out)
        out = jnp.where(lane == 2 * i + 1, pltpu.roll(last, 2 * i + 2, 1), out)
    return out


def edge(edges, i):
    return jnp.broadcast_to(edges[:, i : i + 1], edges.shape)


def prep_kernel(atm_hbm, ocn_hbm, mask_hbm, coef_hbm, adiff_ref, odiff_ref, low, high, edges, ocean, frac, table, surface, coef, adiff, odiff, atm_ref, ocn_ref, mask_ref, coef_ref, sems):
    pairs = ((atm_hbm, atm_ref), (coef_hbm, coef_ref), (mask_hbm, mask_ref), (ocn_hbm, ocn_ref))
    copies = [pltpu.make_async_copy(*pair, sems.at[i]) for i, pair in enumerate(pairs)]
    for copy in copies:
        copy.start()
    adiff[...] = jnp.broadcast_to(adiff_ref[...], (LANES, AL)).T
    odiff[...] = jnp.broadcast_to(odiff_ref[...], (LANES, OL)).T
    copies[0].wait()
    copies[1].wait()
    ends = []
    for r, out in enumerate((low, high)):
        for f in range(2):
            pair = []
            for j in range(AT):
                tile = atm_ref[f, :, r, j * LANES : (j + 1) * LANES]
                out[(f * AT + j) * AL : (f * AT + j + 1) * AL, :] = tile
                at = r * AT + j
                surface[f, at : at + 1, :] = tile[:1]
                coef[f, at : at + 1, :] = coef_ref[f, r : r + 1, j * LANES : (j + 1) * LANES]
                if j in (0, AT - 1):
                    pair.append(tile)
            ends.append(pair)
    edges[:AL, :] = edges_of(ends)
    table[...] = jnp.zeros_like(table)
    copies[2].wait()
    copies[3].wait()
    block, count = lax.axis_index(GROUP), lax.axis_size(GROUP)
    ends = []
    for r in range(OR):
        row = block * OR + r
        inner = jnp.where((row > 0) & (row < OR * count - 1), 1.0, 0.0)
        for j in range(OT):
            at = r * OT + j
            frac[at : at + 1, :] = mask_ref[r : r + 1, j * LANES : (j + 1) * LANES].astype(F32) * inner
        for f in range(2):
            pair = []
            for j in range(OT):
                at = r * OT + j
                tile = ocn_ref[f, :, r, j * LANES : (j + 1) * LANES] * frac[at : at + 1, :]
                line = ((r * 2 + f) * OT + j) * OL
                ocean[line : line + OL, :] = tile
                if r in (0, OR - 1):
                    line = ASIZE + (f * OT + j) * OL
                    (high if r else low)[line : line + OL, :] = tile
                if f == 0:
                    table[at : at + 1, :] = tile[:1]
                if j in (0, OT - 1):
                    pair.append(tile)
            ends.append(pair)
    edges[AL:, :] = edges_of(ends)


def atm_row(place, up, down, edges, i, f, side_gain, surface, store):
    own_gain = (1.0 - 2.0 * VERT_MIX) - 4.0 * side_gain
    top = lax.broadcasted_iota(jnp.int32, (8, LANES), 0) == 0
    def finish(j, fresh, old):
        coef, temp = surface(j)
        gain = coef * ((1.0, MOIST_RATIO)[f] * temp - old[:1])
        fresh = jnp.concatenate([fresh[:8] + jnp.where(top, gain, 0.0), fresh[8:]], axis=0)
        store(j, fresh)
        return fresh
    base = f * AT * AL
    shifted = ((ref, line + base) for ref, line in (place, up, down))
    return step_row(*shifted, AT, AL, edge(edges, 2 * i + 1), edge(edges, 2 * i), own_gain, side_gain, VERT_MIX, finish)


def own_surface(coef_ref, temp_ref, r, f):
    return lambda j: (coef_ref[f, r * AT + j : r * AT + j + 1, :], temp_ref[r * AT + j : r * AT + j + 1, :])


def sent_surface(ref, r, f):
    def lines(j):
        coef, temp = SURFACE + (f * AR + r) * AT + j, TEMP + r * AT + j
        return ref[coef : coef + 1, :], ref[temp : temp + 1, :]
    return lines


def atm_kernel(low, high, up, down, edges_ref, diff_ref, coef_ref, temp_ref, *rest):
    share, final = len(rest) == 5, len(rest) == 1
    if share:
        ocean, ocn_edges, out_low, out_high, out_edges = rest
    elif final:
        out_low = out_high = rest[0]
    else:
        out_low, out_high, out_edges = rest
    edges, side_gain = edges_ref[:AL, :], diff_ref[...]
    rows = [(ref, 0) for ref in (up, low, high, down)]
    ends = []
    for r, out in enumerate((out_low, out_high)):
        for f in range(2):
            def store(j, fresh, f=f, r=r, out=out):
                line = (f * AT + j) * AL
                if final:
                    out[f, :, r, j * LANES : (j + 1) * LANES] = fresh
                elif share:
                    out_low[r * ASIZE + line : r * ASIZE + line + AL, :] = fresh
                    out_high[r * ASIZE + line : r * ASIZE + line + AL, :] = fresh
                else:
                    out[line : line + AL, :] = fresh
            ends.append(atm_row(rows[r + 1], rows[r], rows[r + 2], edges, 2 * r + f, f, side_gain, own_surface(coef_ref, temp_ref, r, f), store))
    if not final:
        out_edges[:AL, :] = edges_of(ends)
    if share:
        out_edges[AL:, :] = ocn_edges[...]
        for out, r in ((out_low, 0), (out_high, OR - 1)):
            out[2 * ASIZE : SURFACE, :] = ocean[r * OSIZE : (r + 1) * OSIZE, :]
            for f in range(2):
                out[SURFACE + f * AR * AT : SURFACE + (f + 1) * AR * AT, :] = coef_ref[f]
            out[TEMP : TEMP + AR * AT, :] = temp_ref[...]
            out[TEMP + AR * AT :, :] = jnp.zeros((MESSAGE - TEMP - AR * AT, LANES), F32)


def beside_kernel(low, high, beside, out_low, out_high, sems):
    copies = [pltpu.make_async_copy(beside.at[pl.ds(0, AL)], out.at[pl.ds(BESIDE, AL)], sems.at[i]) for i, out in enumerate((out_low, out_high))]
    for copy in copies:
        copy.start()
    for copy in copies:
        copy.wait()


def wide_kernel(own, up, down, edges_ref, diff_ref, coef_ref, temp_ref, out_low, out_high, out_up, out_down, out_edges):
    rows = [(up, 0), (up, ASIZE), (own, 0), (own, ASIZE), (down, 0), (down, ASIZE)]
    edges, side_gain = edges_ref[:AL, :], diff_ref[...]
    ends = []
    for k, out in ((1, out_up), (2, out_low), (3, out_high), (4, out_down)):
        for f in range(2):
            def store(j, fresh, f=f, out=out):
                out[(f * AT + j) * AL : (f * AT + j + 1) * AL, :] = fresh
            r = k % 2
            if k in (1, 4):
                ref = up if k == 1 else down
                beside, surface = ref[BESIDE : BESIDE + AL, :], sent_surface(ref, r, f)
            else:
                beside, surface = edges, own_surface(coef_ref, temp_ref, r, f)
            pair = atm_row(rows[k], rows[k - 1], rows[k + 1], beside, 2 * r + f, f, side_gain, surface, store)
            if k in (2, 3):
                ends.append(pair)
    out_edges[...] = edges_of(ends)


def ocn_kernel(final, place, own, up, down, edges_ref, diff_ref, frac_ref, out, out_more):
    edges, side_gain = edges_ref[AL:, :], diff_ref[...]
    own_gain = (1.0 - 2.0 * OCEAN_MIX) - 4.0 * side_gain
    ends = []
    for r in range(OR):
        for f in range(2):
            def finish(j, fresh, old, f=f, r=r):
                fresh = fresh * frac_ref[r * OT + j : r * OT + j + 1, :]
                line = ((r * 2 + f) * OT + j) * OL
                if final:
                    out[f, :, r, j * LANES : (j + 1) * LANES] = fresh
                    out_more[f, :, r, j * LANES : (j + 1) * LANES] = fresh[:2]
                else:
                    out[line : line + OL, :] = fresh
                return fresh
            i = 2 * r + f
            part = lambda k: (own, (k * 2 + f) * OT * OL)
            above = part(r - 1) if r else (up, place + f * OT * OL)
            below = part(r + 1) if r < OR - 1 else (down, place + f * OT * OL)
            ends.append(step_row(part(r), above, below, OT, OL, edge(edges, 2 * i + 1), edge(edges, 2 * i), own_gain, side_gain, OCEAN_MIX, finish))
    if not final:
        out_more[...] = edges_of(ends)


def forcing_kernel(val_ref, cell_ref, frac_ref, out_ref, gain_ref, low, high, *store):
    for f, total in enumerate(scatter_loop(val_ref, (cell_ref, *store), 32, 256, 2)):
        total = (HEAT_GAIN, -SALT_GAIN)[f] * total[: OR * OT // 2]
        for side in range(2):
            out_ref[f, pl.ds(side, OR * OT // 2, stride=2), :] = total[:, side * LANES : (side + 1) * LANES]
        gain_ref[f] = out_ref[f] * frac_ref[...]
        low[f] = gain_ref[f, :OT, :]
        high[f] = gain_ref[f, (OR - 1) * OT :, :]


def last_kernel(base_ref, top_ref, forcing_ref, gain_ref, up, down, beside, frac_ref, diff_ref, out_ref, tall, low_side, high_side, result, sem):
    count = OR * OT
    lane = lax.broadcasted_iota(jnp.int32, (count, LANES), 1)
    line = lax.broadcasted_iota(jnp.int32, (count, LANES), 0)
    starts = (line == 0) | (line == OT) | (line == 2 * OT) | (line == 3 * OT)
    stops = (line == OT - 1) | (line == 2 * OT - 1) | (line == 3 * OT - 1) | (line == 4 * OT - 1)
    frac = frac_ref[...]
    low_side[...] = jnp.zeros_like(low_side)
    high_side[...] = jnp.zeros_like(high_side)
    for f in range(2):
        forcing, gained = forcing_ref[f], gain_ref[f]
        tall[OT : 5 * OT, :] = gained
        tall[:OT, :] = up[f]
        tall[5 * OT :, :] = down[f]
        partner = beside[f]
        to_right, to_left = pltpu.roll(partner, 1, 1), pltpu.roll(partner, LANES - 1, 1)
        for r in range(OR):
            first, last = r * OT, (r + 1) * OT - 1
            low_side[first : first + 1, :] = to_right[last : last + 1]
            high_side[last : last + 1, :] = to_left[first : first + 1]
        to_right, to_left = pltpu.roll(gained, 1, 1), pltpu.roll(gained, LANES - 1, 1)
        before = jnp.where(lane == 0, jnp.where(starts, low_side[...], pltpu.roll(to_right, 1, 0)), to_right)
        after = jnp.where(lane == LANES - 1, jnp.where(stops, high_side[...], pltpu.roll(to_left, count - 1, 0)), to_left)
        lateral = tall[: 4 * OT, :] + tall[2 * OT :, :] + before + after - 4.0 * gained
        second = (gained + diff_ref[:1, :] * lateral - OCEAN_MIX * gained + forcing) * frac
        third = OCEAN_MIX * gained * frac
        for r in range(OR):
            for j in range(OT):
                at, cols = r * OT + j, pl.ds(j * LANES, LANES)
                result[f, 0, r : r + 1, cols] = top_ref[f, 0, r : r + 1, cols] + second[at : at + 1]
                result[f, 1, r : r + 1, cols] = top_ref[f, 1, r : r + 1, cols] + third[at : at + 1]
    copy = pltpu.make_async_copy(result, out_ref.at[:, pl.ds(0, 2)], sem)
    copy.start()
    copy.wait()


VM = pl.BlockSpec(memory_space=pltpu.VMEM)
ANY = pl.BlockSpec(memory_space=pl.ANY)
HBM = pl.BlockSpec(memory_space=pltpu.HBM)


def call(kernel, name, micros, out_shape, *args, scratch=(), cold=(), far=(), **more):
    args = [x if i in cold else pltpu.with_memory_space_constraint(x, pltpu.HBM if i in far else pltpu.VMEM) for i, x in enumerate(args)]
    specs = {"in_specs": [VM] * len(args), "out_specs": jax.tree.map(lambda _: VM, out_shape), **more}
    return pl.pallas_call(
        kernel,
        out_shape=out_shape,
        scratch_shapes=list(scratch),
        cost_estimate=pl.CostEstimate(flops=int(micros * 1.1e9), bytes_accessed=int(micros * 3e6), transcendentals=0),
        compiler_params=pltpu.CompilerParams(vmem_limit_bytes=8 << 20),
        name=name,
        **specs,
    )(*args)


def row_halos(first, last):
    count = lax.axis_size(GROUP)
    up = [(i, (i + 1) % count) for i in range(count)]
    return lax.ppermute(last, GROUP, up), lax.ppermute(first, GROUP, [(b, a) for a, b in up])


def partner(edges):
    count = lax.axis_size("lev")
    return lax.ppermute(edges, "lev", [(i, (i + 1) % count) for i in range(count)])


def exchange(values):
    return lax.all_to_all(values, GROUP, split_axis=0, concat_axis=0, tiled=True)


def shards(
    atm_state,
    atm_diffusion,
    atm_surface_coef,
    ocn_state,
    ocn_diffusion,
    sea_mask,
    atm_pair_cols,
    a2o_weights,
    ocn_pair_cells,
    o2a_weights,
):
    group_size = lax.axis_size(GROUP)
    shape, free = lambda *s: pltpu.VMEM(s, F32), lambda *s: pltpu.HBM(s, F32)
    store = [pltpu.VMEM(atm_pair_cols.shape[2:], jnp.int32), pltpu.SemaphoreType.DMA((2,))]
    cols, cells = atm_pair_cols[0, 0], ocn_pair_cells[0, 0]
    both = shape(ASIZE + OSIZE, LANES)

    low, high, edges, ocean, frac, table, surface, coef, atm_diff, ocn_diff = call(
        prep_kernel,
        "prep",
        3,
        (both, both, shape(AL + OL, LANES), free(OR * OSIZE, LANES), free(OR * OT, LANES), shape(64, LANES), *[free(*s) for s in ((2, AR * AT, LANES), (2, AR * AT, LANES), (AL, LANES), (OL, LANES))]),
        atm_state,
        ocn_state,
        sea_mask,
        atm_surface_coef,
        atm_diffusion[None],
        ocn_diffusion[None],
        far=range(6),
        in_specs=[HBM] * 4 + [VM] * 2,
        scratch=[pltpu.VMEM(x.shape, x.dtype) for x in (atm_state, ocn_state, sea_mask, atm_surface_coef)] + [pltpu.SemaphoreType.DMA((4,))],
    )
    up, down = row_halos(low, high)
    beside = partner(edges)

    outgoing = call(temp_kernel, "temp_gather", 9, shape(group_size, 4, LANES), table, cells, o2a_weights[0, 0], cold=(1, 2), scratch=[pltpu.VMEM((128, SPLITS * 64), BF16)])
    incoming = exchange(outgoing)
    ocn_step = lambda *refs: ocn_kernel(False, ASIZE, *refs)
    ocean, ocn_edges = call(ocn_step, "ocn_step", 3, (shape(OR * OSIZE, LANES), free(OL, LANES)), ocean, up, down, beside, ocn_diff, frac, cold=(4, 5))
    incoming, ocean, ocn_edges = lax.optimization_barrier((incoming, ocean, ocn_edges))

    temp, flux_table = call(flux_kernel, "temp_scatter", 9, (free(AR * AT, LANES), pltpu.VMEM((128, SPLITS * 48), BF16)), incoming, cols, surface, coef, far=(1,), cold=(2, 3), in_specs=[VM, HBM, VM, VM], scratch=[pltpu.VMEM((24, LANES), F32), *store])

    def atm_step(low, high, up, down, beside, *more, outs=None):
        rows = shape(MESSAGE if more else ASIZE, LANES)
        outs = outs or (rows, rows, shape(AL + (OL if more else 0), LANES))
        return call(atm_kernel, "atm_step", 2, outs, low, high, up, down, beside, atm_diff, coef, temp, *more, cold=(5, 6, 7, 9))

    low, high, edges = atm_step(low, high, up, down, beside, ocean, ocn_edges)
    beside = partner(edges)
    message = shape(MESSAGE, LANES)
    low, high = call(beside_kernel, "beside", 1, (message, message), low, high, beside, in_specs=[ANY] * 3, out_specs=(ANY, ANY), scratch=[pltpu.SemaphoreType.DMA((2,))], input_output_aliases={0: 0, 1: 1})
    up, down = row_halos(low, high)
    flux_table, low, high = lax.optimization_barrier((flux_table, low, high))

    outgoing = call(send_kernel, "flux_gather", 9, shape(group_size, 8, LANES), flux_table, cols, a2o_weights[0, 0], cold=(1, 2))
    incoming = exchange(outgoing)
    outgoing, up, down = lax.optimization_barrier((outgoing, up, down))
    row = shape(ASIZE, LANES)
    low, high, near, far, edges = call(wide_kernel, "atm_wide", 3, (row, row, row, row, shape(AL, LANES)), low, up, down, beside, atm_diff, coef, temp, cold=(4, 5, 6))
    side = partner(edges)
    ocn_last_step = lambda *refs: ocn_kernel(True, 2 * ASIZE, *refs)
    ocean, top = call(ocn_last_step, "ocn_step", 3, (jax.ShapeDtypeStruct(ocn_state.shape, F32), free(2, 2, OR, OT * LANES)), ocean, up, down, beside, ocn_diff, frac, cold=(4, 5))
    low, high, edges = atm_step(low, high, near, far, side)
    up, down = row_halos(low, high)
    beside = partner(edges)
    incoming, ocean, top, low, high = lax.optimization_barrier((incoming, ocean, top, low, high))

    every = shape(2, OR * OT, LANES)
    forcing, gained, first, last = call(forcing_kernel, "forcing_scatter", 13, (every, every, shape(2, OT, LANES), shape(2, OT, LANES)), incoming, cells, frac, far=(1,), cold=(2,), in_specs=[VM, HBM, VM], scratch=store)
    above, below = row_halos(first, last)
    side = partner(gained)
    forcing, up, down, beside = lax.optimization_barrier((forcing, up, down, beside))
    atm_next = atm_step(low, high, up, down, beside, outs=(jax.ShapeDtypeStruct(atm_state.shape, F32),))[0]

    line = pltpu.VMEM((OR * OT, LANES), F32)
    ocean_next = call(
        last_kernel,
        "ocn_last",
        1,
        jax.ShapeDtypeStruct(ocean.shape, F32),
        ocean,
        top,
        forcing,
        gained,
        above,
        below,
        side,
        frac,
        ocn_diff,
        in_specs=[ANY] + [VM] * 8,
        out_specs=ANY,
        scratch=[pltpu.VMEM((6 * OT, LANES), F32), line, line, pltpu.VMEM((2, 2, OR, OT * LANES), F32), pltpu.SemaphoreType.DMA],
        input_output_aliases={0: 0},
        cold=(0, 1, 7, 8),
    )
    return atm_next, ocean_next


def solution(mesh):
    across = P(None, None, GROUP, "lev")
    pairs = P("lev", GROUP, None, None)
    placed = (across, P(), P(None, GROUP, "lev"), across, P(), P(GROUP, "lev"), pairs, pairs, pairs, pairs)
    return jax.shard_map(shards, mesh=mesh, in_specs=placed, out_specs=(across, across), check_vma=False)
```

```python
import jax
import jax.numpy as jnp
from jax import lax
from jax.experimental import pallas as pl
from jax.experimental.pallas import tpu as pltpu
from jax.sharding import PartitionSpec as P

ASTEPS = 4
OSTEPS = 2
VERT_MIX = 0.1
OCEAN_MIX = 0.15
HEAT_GAIN = 2.0
SALT_GAIN = 1.0
MOIST_RATIO = 0.8
LANES = 128
GROUP = ("comp", "tile")
F32, BF16 = jnp.float32, jnp.bfloat16


SPLITS = 3


def parts_of(v):
    out = []
    for _ in range(SPLITS):
        p = v.astype(BF16)
        out.append(p)
        v = v - p.astype(F32)
    return out


def spread(row):
    return jnp.broadcast_to(row.astype(F32), (16, row.shape[1])).astype(BF16)


def hits(row, size):
    b = spread(row)
    base = lax.broadcasted_iota(jnp.int32, b.shape, 0).astype(F32)
    return [b == (base + 16.0 * j).astype(BF16) for j in range(size // 16)]


def one_hot(row, size):
    masks = hits(row, size)
    one, zero = jnp.ones(masks[0].shape, BF16), jnp.zeros(masks[0].shape, BF16)
    return jnp.concatenate([jnp.where(m, one, zero) for m in masks], axis=0)


def gather_loop(t_ref, index_ref, w_ref, out_ref, split, H, L, F):
    def group(g, c):
        base = pl.multiple_of(g * 8, 8)
        hi, lo = split(index_ref[pl.ds(base, 8), :])
        w = w_ref[pl.ds(base, 8), :]
        for r in range(8):
            hot = jnp.concatenate([one_hot(hi[r : r + 1], H)] * SPLITS, axis=0)
            o = jnp.dot(t_ref[...], hot, preferred_element_type=F32)
            rows = lax.broadcasted_iota(jnp.int32, (L, o.shape[1]), 0)
            mine = rows == lo[r : r + 1]
            for f in range(F):
                picked = jnp.where(mine, o[f * L : (f + 1) * L], 0.0)
                value = jnp.sum(picked, axis=0, keepdims=True) * w[r : r + 1]
                for q in range(4):
                    out_ref[base + r, 4 * f + q : 4 * f + q + 1, :] = value[:, q * 128 : (q + 1) * 128]
        return c
    lax.fori_loop(0, index_ref.shape[0] // 8, group, 0)


def scatter_loop(val_ref, index, H, L, F, start=0, stop=None):
    index_hbm, index_ref, sems = index
    stop = stop or index_ref.shape[0]
    cuts = (start, start + 16, stop)
    rows = [pl.ds(a, b - a) for a, b in zip(cuts, cuts[1:])]
    copies = [pltpu.make_async_copy(index_hbm.at[r], index_ref.at[r], sems.at[i]) for i, r in enumerate(rows)]
    for copy in copies:
        copy.start()
    shift = L.bit_length() - 1
    def group(g, acc):
        base = pl.multiple_of(g * 8, 8)
        place = index_ref[pl.ds(base, 8), :]
        hi, lo = place >> shift, place & (L - 1)
        for r in range(8):
            masks = hits(hi[r : r + 1], H)
            a = []
            for f in range(F):
                v = jnp.concatenate([val_ref[base + r, 4 * f + q : 4 * f + q + 1, :] for q in range(4)], axis=1)
                for p in parts_of(jnp.broadcast_to(v, (16, v.shape[1]))):
                    a += [jnp.where(m, p, jnp.zeros_like(p)) for m in masks]
            a = jnp.concatenate(a, axis=0)
            acc = acc + lax.dot_general(one_hot(lo[r : r + 1], L), a, (((1,), (1,)), ((), ())), preferred_element_type=F32)
        return acc
    acc = jnp.zeros((L, F * SPLITS * H), F32)
    for copy, a, b in zip(copies, cuts, cuts[1:]):
        copy.wait()
        acc = lax.fori_loop(a // 8, b // 8, group, acc)
    acc = acc.T
    return [sum(acc[(f * SPLITS + i) * H : (f * SPLITS + i + 1) * H] for i in range(SPLITS)) for f in range(F)]


def temp_kernel(table_ref, cell_ref, w_ref, out_ref, t_ref):
    t_ref[...] = jnp.concatenate(parts_of(table_ref[...].T), axis=1)
    gather_loop(t_ref, cell_ref, w_ref, out_ref, lambda i: (i >> 7, i & 127), 64, 128, 1)


AT, AL, AR = 9, 48, 2
OT, OL, OR = 14, 24, 4
ASIZE, OSIZE = 2 * AT * AL, 2 * OT * OL


def flux_kernel(val_ref, col_ref, state_ref, coef_ref, temp_ref, t_ref, flux_ref, *store):
    temp, = scatter_loop(val_ref, (col_ref, *store), 32, 128, 1)
    temp = temp[: AR * AT]
    temp_ref[...] = temp
    flux_ref[...] = jnp.zeros_like(flux_ref)
    blank = jnp.zeros((64, 40), F32)
    for f in range(2):
        flux = coef_ref[f] * (state_ref[f] - (1.0, MOIST_RATIO)[f] * temp)
        flux_ref[: AR * AT, :] = flux
        flux_ref[AR * AT : 2 * AR * AT, :] = pltpu.roll(flux, 64, 1)
        parts = [p.astype(F32) for p in parts_of(flux_ref[:, :64].T)]
        for e in range(2):
            pieces = [x for p in parts for x in ((p, blank), (blank, p))[e]]
            line = 128 * e + 64 * f
            t_ref[line : line + 64, :] = jnp.concatenate(pieces, axis=1).astype(BF16)


def pair_hot(a, b):
    a, b = spread(a), spread(b)
    line = lax.broadcasted_iota(jnp.int32, a.shape, 0).astype(F32)
    early = line < 8.0
    mixed = jnp.where(early, a.astype(F32), b.astype(F32)).astype(BF16)
    targets = (line, line + 16.0, jnp.where(early, line + 32.0, line - 8.0), line + 8.0, line + 24.0)
    one, zero = jnp.ones(a.shape, BF16), jnp.zeros(a.shape, BF16)
    return jnp.concatenate([jnp.where(v == t.astype(BF16), one, zero) for v, t in zip((a, a, mixed, b, b), targets)], axis=0)


def send_kernel(t_ref, col_ref, w_ref, out_ref):
    def group(g, c):
        base = pl.multiple_of(g * 8, 8)
        place = col_ref[pl.ds(base, 8), :]
        hi, lo = (place >> 7) + 18 * ((place >> 6) & 1), place & 63
        w = w_ref[pl.ds(base, 8), :]
        for r in range(0, 8, 2):
            hot = jnp.concatenate([pair_hot(hi[r : r + 1], hi[r + 1 : r + 2])] * SPLITS, axis=0)
            o = jnp.dot(t_ref[...], hot, preferred_element_type=F32)
            lines = lax.broadcasted_iota(jnp.int32, (64, o.shape[1]), 0)
            for e in range(2):
                at = r + e
                mine = lines == lo[at : at + 1]
                for f in range(2):
                    block = 128 * e + 64 * f
                    value = jnp.sum(jnp.where(mine, o[block : block + 64], 0.0), axis=0, keepdims=True) * w[at : at + 1]
                    for q in range(4):
                        out_ref[base + at, 4 * f + q : 4 * f + q + 1, :] = value[:, q * 128 : (q + 1) * 128]
        return c
    lax.fori_loop(0, col_ref.shape[0] // 8, group, 0)


def shifted_levels(ref, base, levels, tile):
    side = lax.broadcasted_iota(jnp.int32, (8, LANES), 0)
    first, last = tile[:8], tile[-8:]
    above = jnp.concatenate([ref[base + 1 : base + levels - 7, :], jnp.where(side == 7, last, pltpu.roll(last, 7, 0))], axis=0)
    below = jnp.concatenate([jnp.where(side == 0, first, pltpu.roll(first, 1, 0)), ref[base + 7 : base + levels - 1, :]], axis=0)
    return above, below


def step_row(own, up, down, tiles, levels, left, right, own_gain, side_gain, vertical, finish):
    lane = lax.broadcasted_iota(jnp.int32, (levels, LANES), 1)
    load = lambda place, j: place[0][place[1] + j * levels : place[1] + (j + 1) * levels, :]
    ends = []
    tile = load(own, 0)
    low_side = left
    for j in range(tiles):
        if j < tiles - 1:
            ahead = load(own, j + 1)
            high_side = pltpu.roll(ahead, LANES - 1, 1)
        else:
            ahead, high_side = None, right
        to_right = pltpu.roll(tile, 1, 1)
        before = jnp.where(lane == 0, low_side, to_right)
        after = jnp.where(lane == LANES - 1, high_side, pltpu.roll(tile, LANES - 1, 1))
        above, below = shifted_levels(own[0], own[1] + j * levels, levels, tile)
        around = (load(up, j) + load(down, j)) + (before + after)
        fresh = own_gain * tile + side_gain * around + vertical * (above + below)
        fresh = finish(j, fresh, tile)
        if j in (0, tiles - 1):
            ends.append(fresh)
        tile, low_side = ahead, to_right
    return ends


def edges_of(rows):
    lane = lax.broadcasted_iota(jnp.int32, rows[0][0].shape, 1)
    out = jnp.zeros(rows[0][0].shape, F32)
    for i, (first, last) in enumerate(rows):
        out = jnp.where(lane == 2 * i, pltpu.roll(first, 2 * i, 1) if i else first, out)
        out = jnp.where(lane == 2 * i + 1, pltpu.roll(last, 2 * i + 2, 1), out)
    return out


def edge(edges, i):
    return jnp.broadcast_to(edges[:, i : i + 1], edges.shape)


def prep_kernel(atm_hbm, ocn_hbm, mask_hbm, coef_hbm, adiff_ref, odiff_ref, low, high, edges, ocean, frac, table, surface, coef, adiff, odiff, atm_ref, ocn_ref, mask_ref, coef_ref, sems):
    pairs = ((atm_hbm, atm_ref), (coef_hbm, coef_ref), (mask_hbm, mask_ref), (ocn_hbm, ocn_ref))
    copies = [pltpu.make_async_copy(*pair, sems.at[i]) for i, pair in enumerate(pairs)]
    for copy in copies:
        copy.start()
    adiff[...] = jnp.broadcast_to(adiff_ref[...], (LANES, AL)).T
    odiff[...] = jnp.broadcast_to(odiff_ref[...], (LANES, OL)).T
    copies[0].wait()
    copies[1].wait()
    ends = []
    for r, out in enumerate((low, high)):
        for f in range(2):
            pair = []
            for j in range(AT):
                tile = atm_ref[f, :, r, j * LANES : (j + 1) * LANES]
                out[(f * AT + j) * AL : (f * AT + j + 1) * AL, :] = tile
                at = r * AT + j
                surface[f, at : at + 1, :] = tile[:1]
                coef[f, at : at + 1, :] = coef_ref[f, r : r + 1, j * LANES : (j + 1) * LANES]
                if j in (0, AT - 1):
                    pair.append(tile)
            ends.append(pair)
    edges[:AL, :] = edges_of(ends)
    table[...] = jnp.zeros_like(table)
    copies[2].wait()
    copies[3].wait()
    block, count = lax.axis_index(GROUP), lax.axis_size(GROUP)
    ends = []
    for r in range(OR):
        row = block * OR + r
        inner = jnp.where((row > 0) & (row < OR * count - 1), 1.0, 0.0)
        for j in range(OT):
            at = r * OT + j
            frac[at : at + 1, :] = mask_ref[r : r + 1, j * LANES : (j + 1) * LANES].astype(F32) * inner
        for f in range(2):
            pair = []
            for j in range(OT):
                at = r * OT + j
                tile = ocn_ref[f, :, r, j * LANES : (j + 1) * LANES] * frac[at : at + 1, :]
                line = ((r * 2 + f) * OT + j) * OL
                ocean[line : line + OL, :] = tile
                if r in (0, OR - 1):
                    line = ASIZE + (f * OT + j) * OL
                    (high if r else low)[line : line + OL, :] = tile
                if f == 0:
                    table[at : at + 1, :] = tile[:1]
                if j in (0, OT - 1):
                    pair.append(tile)
            ends.append(pair)
    edges[AL:, :] = edges_of(ends)


def atm_kernel(low, high, up, down, edges_ref, diff_ref, coef_ref, temp_ref, *rest):
    share, final = len(rest) == 5, len(rest) == 1
    if share:
        ocean, ocn_edges, out_low, out_high, out_edges = rest
    elif final:
        out_low = out_high = rest[0]
    else:
        out_low, out_high, out_edges = rest
    edges, side_gain = edges_ref[:AL, :], diff_ref[...]
    own_gain = (1.0 - 2.0 * VERT_MIX) - 4.0 * side_gain
    top = lax.broadcasted_iota(jnp.int32, (8, LANES), 0) == 0
    rows = [up, low, high, down]
    ends = []
    for r, out in enumerate((out_low, out_high)):
        for f in range(2):
            def finish(j, fresh, old, f=f, r=r, out=out):
                at = r * AT + j
                gain = (1.0, MOIST_RATIO)[f] * temp_ref[at : at + 1, :]
                gain = coef_ref[f, at : at + 1, :] * (gain - old[:1])
                fresh = jnp.concatenate([fresh[:8] + jnp.where(top, gain, 0.0), fresh[8:]], axis=0)
                if final:
                    out[f, :, r, j * LANES : (j + 1) * LANES] = fresh
                else:
                    out[(f * AT + j) * AL : (f * AT + j + 1) * AL, :] = fresh
                return fresh
            i, base = 2 * r + f, f * AT * AL
            ends.append(step_row(*((rows[k], base) for k in (r + 1, r, r + 2)), AT, AL, edge(edges, 2 * i + 1), edge(edges, 2 * i), own_gain, side_gain, VERT_MIX, finish))
    if not final:
        out_edges[:AL, :] = edges_of(ends)
    if share:
        out_low[ASIZE:, :] = ocean[:OSIZE, :]
        out_high[ASIZE:, :] = ocean[(OR - 1) * OSIZE :, :]
        out_edges[AL:, :] = ocn_edges[...]


def ocn_kernel(final, own, up, down, edges_ref, diff_ref, frac_ref, out, out_more):
    edges, side_gain = edges_ref[AL:, :], diff_ref[...]
    own_gain = (1.0 - 2.0 * OCEAN_MIX) - 4.0 * side_gain
    ends = []
    for r in range(OR):
        for f in range(2):
            def finish(j, fresh, old, f=f, r=r):
                fresh = fresh * frac_ref[r * OT + j : r * OT + j + 1, :]
                line = ((r * 2 + f) * OT + j) * OL
                if final:
                    out[f, :, r, j * LANES : (j + 1) * LANES] = fresh
                    out_more[f, :, r, j * LANES : (j + 1) * LANES] = fresh[:2]
                else:
                    out[line : line + OL, :] = fresh
                return fresh
            i = 2 * r + f
            part = lambda k: (own, (k * 2 + f) * OT * OL)
            above = part(r - 1) if r else (up, ASIZE + f * OT * OL)
            below = part(r + 1) if r < OR - 1 else (down, ASIZE + f * OT * OL)
            ends.append(step_row(part(r), above, below, OT, OL, edge(edges, 2 * i + 1), edge(edges, 2 * i), own_gain, side_gain, OCEAN_MIX, finish))
    if not final:
        out_more[...] = edges_of(ends)


def half_kernel(val_ref, cell_ref, out_ref, *store):
    for f, total in enumerate(scatter_loop(val_ref, (cell_ref, *store), 32, 256, 2, stop=88)):
        out_ref[f] = total


def forcing_kernel(half_ref, val_ref, cell_ref, frac_ref, out_ref, gain_ref, low, high, *store):
    for f, total in enumerate(scatter_loop(val_ref, (cell_ref, *store), 32, 256, 2, start=88)):
        total = (HEAT_GAIN, -SALT_GAIN)[f] * (half_ref[f] + total)[: OR * OT // 2]
        for side in range(2):
            out_ref[f, pl.ds(side, OR * OT // 2, stride=2), :] = total[:, side * LANES : (side + 1) * LANES]
        gain_ref[f] = out_ref[f] * frac_ref[...]
        low[f] = gain_ref[f, :OT, :]
        high[f] = gain_ref[f, (OR - 1) * OT :, :]


def last_kernel(base_ref, top_ref, forcing_ref, gain_ref, up, down, beside, frac_ref, diff_ref, out_ref, tall, low_side, high_side, result, sem):
    count = OR * OT
    lane = lax.broadcasted_iota(jnp.int32, (count, LANES), 1)
    line = lax.broadcasted_iota(jnp.int32, (count, LANES), 0)
    starts = (line == 0) | (line == OT) | (line == 2 * OT) | (line == 3 * OT)
    stops = (line == OT - 1) | (line == 2 * OT - 1) | (line == 3 * OT - 1) | (line == 4 * OT - 1)
    frac = frac_ref[...]
    low_side[...] = jnp.zeros_like(low_side)
    high_side[...] = jnp.zeros_like(high_side)
    for f in range(2):
        forcing, gained = forcing_ref[f], gain_ref[f]
        tall[OT : 5 * OT, :] = gained
        tall[:OT, :] = up[f]
        tall[5 * OT :, :] = down[f]
        partner = beside[f]
        to_right, to_left = pltpu.roll(partner, 1, 1), pltpu.roll(partner, LANES - 1, 1)
        for r in range(OR):
            first, last = r * OT, (r + 1) * OT - 1
            low_side[first : first + 1, :] = to_right[last : last + 1]
            high_side[last : last + 1, :] = to_left[first : first + 1]
        to_right, to_left = pltpu.roll(gained, 1, 1), pltpu.roll(gained, LANES - 1, 1)
        before = jnp.where(lane == 0, jnp.where(starts, low_side[...], pltpu.roll(to_right, 1, 0)), to_right)
        after = jnp.where(lane == LANES - 1, jnp.where(stops, high_side[...], pltpu.roll(to_left, count - 1, 0)), to_left)
        lateral = tall[: 4 * OT, :] + tall[2 * OT :, :] + before + after - 4.0 * gained
        second = (gained + diff_ref[:1, :] * lateral - OCEAN_MIX * gained + forcing) * frac
        third = OCEAN_MIX * gained * frac
        for r in range(OR):
            for j in range(OT):
                at, cols = r * OT + j, pl.ds(j * LANES, LANES)
                result[f, 0, r : r + 1, cols] = top_ref[f, 0, r : r + 1, cols] + second[at : at + 1]
                result[f, 1, r : r + 1, cols] = top_ref[f, 1, r : r + 1, cols] + third[at : at + 1]
    copy = pltpu.make_async_copy(result, out_ref.at[:, pl.ds(0, 2)], sem)
    copy.start()
    copy.wait()


VM = pl.BlockSpec(memory_space=pltpu.VMEM)
ANY = pl.BlockSpec(memory_space=pl.ANY)
HBM = pl.BlockSpec(memory_space=pltpu.HBM)


def call(kernel, name, micros, out_shape, *args, scratch=(), cold=(), far=(), **more):
    args = [x if i in cold else pltpu.with_memory_space_constraint(x, pltpu.HBM if i in far else pltpu.VMEM) for i, x in enumerate(args)]
    specs = {"in_specs": [VM] * len(args), "out_specs": jax.tree.map(lambda _: VM, out_shape), **more}
    return pl.pallas_call(
        kernel,
        out_shape=out_shape,
        scratch_shapes=list(scratch),
        cost_estimate=pl.CostEstimate(flops=int(micros * 1.1e9), bytes_accessed=int(micros * 3e6), transcendentals=0),
        compiler_params=pltpu.CompilerParams(vmem_limit_bytes=8 << 20),
        name=name,
        **specs,
    )(*args)


def row_halos(first, last):
    count = lax.axis_size(GROUP)
    up = [(i, (i + 1) % count) for i in range(count)]
    return lax.ppermute(last, GROUP, up), lax.ppermute(first, GROUP, [(b, a) for a, b in up])


def partner(edges):
    count = lax.axis_size("lev")
    return lax.ppermute(edges, "lev", [(i, (i + 1) % count) for i in range(count)])


def exchange(values):
    return lax.all_to_all(values, GROUP, split_axis=0, concat_axis=0, tiled=True)


def shards(
    atm_state,
    atm_diffusion,
    atm_surface_coef,
    ocn_state,
    ocn_diffusion,
    sea_mask,
    atm_pair_cols,
    a2o_weights,
    ocn_pair_cells,
    o2a_weights,
):
    group_size = lax.axis_size(GROUP)
    shape, free = lambda *s: pltpu.VMEM(s, F32), lambda *s: pltpu.HBM(s, F32)
    store = [pltpu.VMEM(atm_pair_cols.shape[2:], jnp.int32), pltpu.SemaphoreType.DMA((2,))]
    cols, cells = atm_pair_cols[0, 0], ocn_pair_cells[0, 0]
    both = shape(ASIZE + OSIZE, LANES)

    low, high, edges, ocean, frac, table, surface, coef, atm_diff, ocn_diff = call(
        prep_kernel,
        "prep",
        3,
        (both, both, shape(AL + OL, LANES), free(OR * OSIZE, LANES), free(OR * OT, LANES), shape(64, LANES), *[free(*s) for s in ((2, AR * AT, LANES), (2, AR * AT, LANES), (AL, LANES), (OL, LANES))]),
        atm_state,
        ocn_state,
        sea_mask,
        atm_surface_coef,
        atm_diffusion[None],
        ocn_diffusion[None],
        far=range(6),
        in_specs=[HBM] * 4 + [VM] * 2,
        scratch=[pltpu.VMEM(x.shape, x.dtype) for x in (atm_state, ocn_state, sea_mask, atm_surface_coef)] + [pltpu.SemaphoreType.DMA((4,))],
    )
    up, down = row_halos(low, high)
    beside = partner(edges)

    outgoing = call(temp_kernel, "temp_gather", 9, shape(group_size, 4, LANES), table, cells, o2a_weights[0, 0], cold=(1, 2), scratch=[pltpu.VMEM((128, SPLITS * 64), BF16)])
    incoming = exchange(outgoing)
    ocn_step = lambda *refs: ocn_kernel(False, *refs)
    ocean, ocn_edges = call(ocn_step, "ocn_step", 3, (shape(OR * OSIZE, LANES), free(OL, LANES)), ocean, up, down, beside, ocn_diff, frac, cold=(4, 5))
    incoming, ocean, ocn_edges = lax.optimization_barrier((incoming, ocean, ocn_edges))

    temp, flux_table = call(flux_kernel, "temp_scatter", 9, (free(AR * AT, LANES), pltpu.VMEM((256, SPLITS * 80), BF16)), incoming, cols, surface, coef, far=(1,), cold=(2, 3), in_specs=[VM, HBM, VM, VM], scratch=[pltpu.VMEM((40, LANES), F32), *store])

    def atm_step(low, high, up, down, beside, *more, outs=None):
        rows = shape(ASIZE + (OSIZE if more else 0), LANES)
        outs = outs or (rows, rows, shape(AL + (OL if more else 0), LANES))
        return call(atm_kernel, "atm_step", 2.5, outs, low, high, up, down, beside, atm_diff, coef, temp, *more, cold=(5, 6, 7, 9))

    low, high, edges = atm_step(low, high, up, down, beside, ocean, ocn_edges)
    up, down = row_halos(low, high)
    beside = partner(edges)
    flux_table, low, high = lax.optimization_barrier((flux_table, low, high))

    outgoing = call(send_kernel, "flux_gather", 9, shape(group_size, 8, LANES), flux_table, cols, a2o_weights[0, 0], cold=(1, 2))
    incoming = exchange(outgoing)
    outgoing, up, down, beside = lax.optimization_barrier((outgoing, up, down, beside))
    low, high, edges = atm_step(low, high, up, down, beside)
    ocn_last_step = lambda *refs: ocn_kernel(True, *refs)
    ocean, top = call(ocn_last_step, "ocn_step", 3, (jax.ShapeDtypeStruct(ocn_state.shape, F32), free(2, 2, OR, OT * LANES)), ocean, up, down, beside, ocn_diff, frac, cold=(4, 5))
    up, down = row_halos(low, high)
    beside = partner(edges)
    incoming, ocean, top, low, high = lax.optimization_barrier((incoming, ocean, top, low, high))

    half = call(half_kernel, "forcing_half", 7.5, shape(2, 32, 256), incoming, cells, far=(1,), in_specs=[VM, HBM], scratch=store)
    half, up, down, beside = lax.optimization_barrier((half, up, down, beside))
    low, high, edges = atm_step(low, high, up, down, beside)
    up, down = row_halos(low, high)
    beside = partner(edges)
    half, low, high = lax.optimization_barrier((half, low, high))

    every = shape(2, OR * OT, LANES)
    forcing, gained, first, last = call(forcing_kernel, "forcing_scatter", 7.5, (every, every, shape(2, OT, LANES), shape(2, OT, LANES)), half, incoming, cells, frac, far=(2,), cold=(3,), in_specs=[VM, VM, HBM, VM], scratch=store)
    above, below = row_halos(first, last)
    side = partner(gained)
    forcing, up, down, beside = lax.optimization_barrier((forcing, up, down, beside))
    atm_next = atm_step(low, high, up, down, beside, outs=(jax.ShapeDtypeStruct(atm_state.shape, F32),))[0]

    line = pltpu.VMEM((OR * OT, LANES), F32)
    ocean_next = call(
        last_kernel,
        "ocn_last",
        1,
        jax.ShapeDtypeStruct(ocean.shape, F32),
        ocean,
        top,
        forcing,
        gained,
        above,
        below,
        side,
        frac,
        ocn_diff,
        in_specs=[ANY] + [VM] * 8,
        out_specs=ANY,
        scratch=[pltpu.VMEM((6 * OT, LANES), F32), line, line, pltpu.VMEM((2, 2, OR, OT * LANES), F32), pltpu.SemaphoreType.DMA],
        input_output_aliases={0: 0},
        cold=(0, 1, 7, 8),
    )
    return atm_next, ocean_next


def solution(mesh):
    across = P(None, None, GROUP, "lev")
    pairs = P("lev", GROUP, None, None)
    placed = (across, P(), P(None, GROUP, "lev"), across, P(), P(GROUP, "lev"), pairs, pairs, pairs, pairs)
    return jax.shard_map(shards, mesh=mesh, in_specs=placed, out_specs=(across, across), check_vma=False)
```

```python
import jax
import jax.numpy as jnp
from jax import lax
from jax.experimental import pallas as pl
from jax.experimental.pallas import tpu as pltpu
from jax.sharding import PartitionSpec as P

ASTEPS = 4
OSTEPS = 2
VERT_MIX = 0.1
OCEAN_MIX = 0.15
HEAT_GAIN = 2.0
SALT_GAIN = 1.0
MOIST_RATIO = 0.8
LANES = 128
GROUP = ("comp", "tile")
F32, BF16 = jnp.float32, jnp.bfloat16


SPLITS = 3


def parts_of(v):
    out = []
    for _ in range(SPLITS):
        p = v.astype(BF16)
        out.append(p)
        v = v - p.astype(F32)
    return out


def spread(row):
    return jnp.broadcast_to(row.astype(F32), (16, row.shape[1])).astype(BF16)


def hits(row, size):
    b = spread(row)
    base = lax.broadcasted_iota(jnp.int32, b.shape, 0).astype(F32)
    return [b == (base + 16.0 * j).astype(BF16) for j in range(size // 16)]


def one_hot(row, size):
    masks = hits(row, size)
    one, zero = jnp.ones(masks[0].shape, BF16), jnp.zeros(masks[0].shape, BF16)
    return jnp.concatenate([jnp.where(m, one, zero) for m in masks], axis=0)


def gather_loop(t_ref, index_ref, w_ref, out_ref, split, H, L, F):
    def group(g, c):
        base = pl.multiple_of(g * 8, 8)
        hi, lo = split(index_ref[pl.ds(base, 8), :])
        w = w_ref[pl.ds(base, 8), :]
        for r in range(8):
            hot = jnp.concatenate([one_hot(hi[r : r + 1], H)] * SPLITS, axis=0)
            o = jnp.dot(t_ref[...], hot, preferred_element_type=F32)
            rows = lax.broadcasted_iota(jnp.int32, (L, o.shape[1]), 0)
            mine = rows == lo[r : r + 1]
            for f in range(F):
                picked = jnp.where(mine, o[f * L : (f + 1) * L], 0.0)
                value = jnp.sum(picked, axis=0, keepdims=True) * w[r : r + 1]
                for q in range(4):
                    out_ref[base + r, 4 * f + q : 4 * f + q + 1, :] = value[:, q * 128 : (q + 1) * 128]
        return c
    lax.fori_loop(0, index_ref.shape[0] // 8, group, 0)


def scatter_loop(val_ref, index, H, L, F, start=0, stop=None):
    index_hbm, index_ref, sems = index
    stop = stop or index_ref.shape[0]
    cuts = (start, start + 16, stop)
    rows = [pl.ds(a, b - a) for a, b in zip(cuts, cuts[1:])]
    copies = [pltpu.make_async_copy(index_hbm.at[r], index_ref.at[r], sems.at[i]) for i, r in enumerate(rows)]
    for copy in copies:
        copy.start()
    shift = L.bit_length() - 1
    def group(g, acc):
        base = pl.multiple_of(g * 8, 8)
        place = index_ref[pl.ds(base, 8), :]
        hi, lo = place >> shift, place & (L - 1)
        for r in range(8):
            masks = hits(hi[r : r + 1], H)
            a = []
            for f in range(F):
                v = jnp.concatenate([val_ref[base + r, 4 * f + q : 4 * f + q + 1, :] for q in range(4)], axis=1)
                for p in parts_of(jnp.broadcast_to(v, (16, v.shape[1]))):
                    a += [jnp.where(m, p, jnp.zeros_like(p)) for m in masks]
            a = jnp.concatenate(a, axis=0)
            acc = acc + lax.dot_general(one_hot(lo[r : r + 1], L), a, (((1,), (1,)), ((), ())), preferred_element_type=F32)
        return acc
    acc = jnp.zeros((L, F * SPLITS * H), F32)
    for copy, a, b in zip(copies, cuts, cuts[1:]):
        copy.wait()
        acc = lax.fori_loop(a // 8, b // 8, group, acc)
    acc = acc.T
    return [sum(acc[(f * SPLITS + i) * H : (f * SPLITS + i + 1) * H] for i in range(SPLITS)) for f in range(F)]


def temp_kernel(table_ref, cell_ref, w_ref, out_ref, t_ref):
    t_ref[...] = jnp.concatenate(parts_of(table_ref[...].T), axis=1)
    gather_loop(t_ref, cell_ref, w_ref, out_ref, lambda i: (i >> 7, i & 127), 64, 128, 1)


AT, AL, AR = 9, 48, 2
OT, OL, OR = 14, 24, 4
ASIZE, OSIZE = 2 * AT * AL, 2 * OT * OL


def flux_kernel(val_ref, col_ref, state_ref, coef_ref, temp_ref, t_ref, flux_ref, *store):
    temp, = scatter_loop(val_ref, (col_ref, *store), 32, 128, 1)
    temp = temp[: AR * AT]
    temp_ref[...] = temp
    flux_ref[...] = jnp.zeros_like(flux_ref)
    tables = []
    for f in range(2):
        flux_ref[: AR * AT, :] = coef_ref[f] * (state_ref[f] - (1.0, MOIST_RATIO)[f] * temp)
        flux = flux_ref[...]
        halves = jnp.concatenate([flux[:, :64], flux[:, 64:]], axis=0)
        tables.append(jnp.concatenate(parts_of(halves.T), axis=1))
    t_ref[...] = jnp.concatenate(tables, axis=0)


def half_split(i):
    return (i >> 7) + 24 * ((i >> 6) & 1), i & 63


def send_kernel(t_ref, col_ref, w_ref, out_ref):
    gather_loop(t_ref, col_ref, w_ref, out_ref, half_split, 48, 64, 2)


def shifted_levels(ref, base, levels, tile):
    side = lax.broadcasted_iota(jnp.int32, (8, LANES), 0)
    first, last = tile[:8], tile[-8:]
    above = jnp.concatenate([ref[base + 1 : base + levels - 7, :], jnp.where(side == 7, last, pltpu.roll(last, 7, 0))], axis=0)
    below = jnp.concatenate([jnp.where(side == 0, first, pltpu.roll(first, 1, 0)), ref[base + 7 : base + levels - 1, :]], axis=0)
    return above, below


def step_row(own, up, down, tiles, levels, left, right, own_gain, side_gain, vertical, finish):
    lane = lax.broadcasted_iota(jnp.int32, (levels, LANES), 1)
    load = lambda place, j: place[0][place[1] + j * levels : place[1] + (j + 1) * levels, :]
    ends = []
    tile = load(own, 0)
    low_side = left
    for j in range(tiles):
        if j < tiles - 1:
            ahead = load(own, j + 1)
            high_side = pltpu.roll(ahead, LANES - 1, 1)
        else:
            ahead, high_side = None, right
        to_right = pltpu.roll(tile, 1, 1)
        before = jnp.where(lane == 0, low_side, to_right)
        after = jnp.where(lane == LANES - 1, high_side, pltpu.roll(tile, LANES - 1, 1))
        above, below = shifted_levels(own[0], own[1] + j * levels, levels, tile)
        around = (load(up, j) + load(down, j)) + (before + after)
        fresh = own_gain * tile + side_gain * around + vertical * (above + below)
        fresh = finish(j, fresh, tile)
        if j in (0, tiles - 1):
            ends.append(fresh)
        tile, low_side = ahead, to_right
    return ends


def edges_of(rows):
    lane = lax.broadcasted_iota(jnp.int32, rows[0][0].shape, 1)
    out = jnp.zeros(rows[0][0].shape, F32)
    for i, (first, last) in enumerate(rows):
        out = jnp.where(lane == 2 * i, pltpu.roll(first, 2 * i, 1) if i else first, out)
        out = jnp.where(lane == 2 * i + 1, pltpu.roll(last, 2 * i + 2, 1), out)
    return out


def edge(edges, i):
    return jnp.broadcast_to(edges[:, i : i + 1], edges.shape)


def prep_kernel(atm_hbm, ocn_hbm, mask_hbm, coef_hbm, adiff_ref, odiff_ref, low, high, edges, ocean, frac, table, surface, coef, adiff, odiff, atm_ref, ocn_ref, mask_ref, coef_ref, sems):
    pairs = ((atm_hbm, atm_ref), (coef_hbm, coef_ref), (mask_hbm, mask_ref), (ocn_hbm, ocn_ref))
    copies = [pltpu.make_async_copy(*pair, sems.at[i]) for i, pair in enumerate(pairs)]
    for copy in copies:
        copy.start()
    adiff[...] = jnp.broadcast_to(adiff_ref[...], (LANES, AL)).T
    odiff[...] = jnp.broadcast_to(odiff_ref[...], (LANES, OL)).T
    copies[0].wait()
    copies[1].wait()
    ends = []
    for r, out in enumerate((low, high)):
        for f in range(2):
            pair = []
            for j in range(AT):
                tile = atm_ref[f, :, r, j * LANES : (j + 1) * LANES]
                out[(f * AT + j) * AL : (f * AT + j + 1) * AL, :] = tile
                at = r * AT + j
                surface[f, at : at + 1, :] = tile[:1]
                coef[f, at : at + 1, :] = coef_ref[f, r : r + 1, j * LANES : (j + 1) * LANES]
                if j in (0, AT - 1):
                    pair.append(tile)
            ends.append(pair)
    edges[:AL, :] = edges_of(ends)
    table[...] = jnp.zeros_like(table)
    copies[2].wait()
    copies[3].wait()
    block, count = lax.axis_index(GROUP), lax.axis_size(GROUP)
    ends = []
    for r in range(OR):
        row = block * OR + r
        inner = jnp.where((row > 0) & (row < OR * count - 1), 1.0, 0.0)
        for j in range(OT):
            at = r * OT + j
            frac[at : at + 1, :] = mask_ref[r : r + 1, j * LANES : (j + 1) * LANES].astype(F32) * inner
        for f in range(2):
            pair = []
            for j in range(OT):
                at = r * OT + j
                tile = ocn_ref[f, :, r, j * LANES : (j + 1) * LANES] * frac[at : at + 1, :]
                line = ((r * 2 + f) * OT + j) * OL
                ocean[line : line + OL, :] = tile
                if r in (0, OR - 1):
                    line = ASIZE + (f * OT + j) * OL
                    (high if r else low)[line : line + OL, :] = tile
                if f == 0:
                    table[at : at + 1, :] = tile[:1]
                if j in (0, OT - 1):
                    pair.append(tile)
            ends.append(pair)
    edges[AL:, :] = edges_of(ends)


def atm_kernel(low, high, up, down, edges_ref, diff_ref, coef_ref, temp_ref, *rest):
    share, final = len(rest) == 5, len(rest) == 1
    if share:
        ocean, ocn_edges, out_low, out_high, out_edges = rest
    elif final:
        out_low = out_high = rest[0]
    else:
        out_low, out_high, out_edges = rest
    edges, side_gain = edges_ref[:AL, :], diff_ref[...]
    own_gain = (1.0 - 2.0 * VERT_MIX) - 4.0 * side_gain
    top = lax.broadcasted_iota(jnp.int32, (8, LANES), 0) == 0
    rows = [up, low, high, down]
    ends = []
    for r, out in enumerate((out_low, out_high)):
        for f in range(2):
            def finish(j, fresh, old, f=f, r=r, out=out):
                at = r * AT + j
                gain = (1.0, MOIST_RATIO)[f] * temp_ref[at : at + 1, :]
                gain = coef_ref[f, at : at + 1, :] * (gain - old[:1])
                fresh = jnp.concatenate([fresh[:8] + jnp.where(top, gain, 0.0), fresh[8:]], axis=0)
                if final:
                    out[f, :, r, j * LANES : (j + 1) * LANES] = fresh
                else:
                    out[(f * AT + j) * AL : (f * AT + j + 1) * AL, :] = fresh
                return fresh
            i, base = 2 * r + f, f * AT * AL
            ends.append(step_row(*((rows[k], base) for k in (r + 1, r, r + 2)), AT, AL, edge(edges, 2 * i + 1), edge(edges, 2 * i), own_gain, side_gain, VERT_MIX, finish))
    if not final:
        out_edges[:AL, :] = edges_of(ends)
    if share:
        out_low[ASIZE:, :] = ocean[:OSIZE, :]
        out_high[ASIZE:, :] = ocean[(OR - 1) * OSIZE :, :]
        out_edges[AL:, :] = ocn_edges[...]


def ocn_kernel(final, own, up, down, edges_ref, diff_ref, frac_ref, out, out_more):
    edges, side_gain = edges_ref[AL:, :], diff_ref[...]
    own_gain = (1.0 - 2.0 * OCEAN_MIX) - 4.0 * side_gain
    ends = []
    for r in range(OR):
        for f in range(2):
            def finish(j, fresh, old, f=f, r=r):
                fresh = fresh * frac_ref[r * OT + j : r * OT + j + 1, :]
                line = ((r * 2 + f) * OT + j) * OL
                if final:
                    out[f, :, r, j * LANES : (j + 1) * LANES] = fresh
                    out_more[f, :, r, j * LANES : (j + 1) * LANES] = fresh[:2]
                else:
                    out[line : line + OL, :] = fresh
                return fresh
            i = 2 * r + f
            part = lambda k: (own, (k * 2 + f) * OT * OL)
            above = part(r - 1) if r else (up, ASIZE + f * OT * OL)
            below = part(r + 1) if r < OR - 1 else (down, ASIZE + f * OT * OL)
            ends.append(step_row(part(r), above, below, OT, OL, edge(edges, 2 * i + 1), edge(edges, 2 * i), own_gain, side_gain, OCEAN_MIX, finish))
    if not final:
        out_more[...] = edges_of(ends)


def half_kernel(val_ref, cell_ref, out_ref, *store):
    for f, total in enumerate(scatter_loop(val_ref, (cell_ref, *store), 32, 256, 2, stop=val_ref.shape[0] // 2)):
        out_ref[f] = total


def forcing_kernel(half_ref, val_ref, cell_ref, frac_ref, out_ref, gain_ref, low, high, *store):
    for f, total in enumerate(scatter_loop(val_ref, (cell_ref, *store), 32, 256, 2, start=val_ref.shape[0] // 2)):
        total = (HEAT_GAIN, -SALT_GAIN)[f] * (half_ref[f] + total)[: OR * OT // 2]
        for side in range(2):
            out_ref[f, pl.ds(side, OR * OT // 2, stride=2), :] = total[:, side * LANES : (side + 1) * LANES]
        gain_ref[f] = out_ref[f] * frac_ref[...]
        low[f] = gain_ref[f, :OT, :]
        high[f] = gain_ref[f, (OR - 1) * OT :, :]


def last_kernel(base_ref, top_ref, forcing_ref, gain_ref, up, down, beside, frac_ref, diff_ref, out_ref, tall, low_side, high_side, result, sem):
    count = OR * OT
    lane = lax.broadcasted_iota(jnp.int32, (count, LANES), 1)
    line = lax.broadcasted_iota(jnp.int32, (count, LANES), 0)
    starts = (line == 0) | (line == OT) | (line == 2 * OT) | (line == 3 * OT)
    stops = (line == OT - 1) | (line == 2 * OT - 1) | (line == 3 * OT - 1) | (line == 4 * OT - 1)
    frac = frac_ref[...]
    low_side[...] = jnp.zeros_like(low_side)
    high_side[...] = jnp.zeros_like(high_side)
    for f in range(2):
        forcing, gained = forcing_ref[f], gain_ref[f]
        tall[OT : 5 * OT, :] = gained
        tall[:OT, :] = up[f]
        tall[5 * OT :, :] = down[f]
        partner = beside[f]
        to_right, to_left = pltpu.roll(partner, 1, 1), pltpu.roll(partner, LANES - 1, 1)
        for r in range(OR):
            first, last = r * OT, (r + 1) * OT - 1
            low_side[first : first + 1, :] = to_right[last : last + 1]
            high_side[last : last + 1, :] = to_left[first : first + 1]
        to_right, to_left = pltpu.roll(gained, 1, 1), pltpu.roll(gained, LANES - 1, 1)
        before = jnp.where(lane == 0, jnp.where(starts, low_side[...], pltpu.roll(to_right, 1, 0)), to_right)
        after = jnp.where(lane == LANES - 1, jnp.where(stops, high_side[...], pltpu.roll(to_left, count - 1, 0)), to_left)
        lateral = tall[: 4 * OT, :] + tall[2 * OT :, :] + before + after - 4.0 * gained
        second = (gained + diff_ref[:1, :] * lateral - OCEAN_MIX * gained + forcing) * frac
        third = OCEAN_MIX * gained * frac
        for r in range(OR):
            for j in range(OT):
                at, cols = r * OT + j, pl.ds(j * LANES, LANES)
                result[f, 0, r : r + 1, cols] = top_ref[f, 0, r : r + 1, cols] + second[at : at + 1]
                result[f, 1, r : r + 1, cols] = top_ref[f, 1, r : r + 1, cols] + third[at : at + 1]
    copy = pltpu.make_async_copy(result, out_ref.at[:, pl.ds(0, 2)], sem)
    copy.start()
    copy.wait()


VM = pl.BlockSpec(memory_space=pltpu.VMEM)
ANY = pl.BlockSpec(memory_space=pl.ANY)
HBM = pl.BlockSpec(memory_space=pltpu.HBM)


def call(kernel, name, micros, out_shape, *args, scratch=(), cold=(), far=(), **more):
    args = [x if i in cold else pltpu.with_memory_space_constraint(x, pltpu.HBM if i in far else pltpu.VMEM) for i, x in enumerate(args)]
    specs = {"in_specs": [VM] * len(args), "out_specs": jax.tree.map(lambda _: VM, out_shape), **more}
    return pl.pallas_call(
        kernel,
        out_shape=out_shape,
        scratch_shapes=list(scratch),
        cost_estimate=pl.CostEstimate(flops=int(micros * 1.1e9), bytes_accessed=int(micros * 3e6), transcendentals=0),
        compiler_params=pltpu.CompilerParams(vmem_limit_bytes=8 << 20),
        name=name,
        **specs,
    )(*args)


def row_halos(first, last):
    count = lax.axis_size(GROUP)
    up = [(i, (i + 1) % count) for i in range(count)]
    return lax.ppermute(last, GROUP, up), lax.ppermute(first, GROUP, [(b, a) for a, b in up])


def partner(edges):
    count = lax.axis_size("lev")
    return lax.ppermute(edges, "lev", [(i, (i + 1) % count) for i in range(count)])


def exchange(values):
    return lax.all_to_all(values, GROUP, split_axis=0, concat_axis=0, tiled=True)


def shards(
    atm_state,
    atm_diffusion,
    atm_surface_coef,
    ocn_state,
    ocn_diffusion,
    sea_mask,
    atm_pair_cols,
    a2o_weights,
    ocn_pair_cells,
    o2a_weights,
):
    group_size = lax.axis_size(GROUP)
    shape, free = lambda *s: pltpu.VMEM(s, F32), lambda *s: pltpu.HBM(s, F32)
    store = [pltpu.VMEM(atm_pair_cols.shape[2:], jnp.int32), pltpu.SemaphoreType.DMA((2,))]
    cols, cells = atm_pair_cols[0, 0], ocn_pair_cells[0, 0]
    both = shape(ASIZE + OSIZE, LANES)

    low, high, edges, ocean, frac, table, surface, coef, atm_diff, ocn_diff = call(
        prep_kernel,
        "prep",
        3,
        (both, both, shape(AL + OL, LANES), free(OR * OSIZE, LANES), free(OR * OT, LANES), shape(64, LANES), *[free(*s) for s in ((2, AR * AT, LANES), (2, AR * AT, LANES), (AL, LANES), (OL, LANES))]),
        atm_state,
        ocn_state,
        sea_mask,
        atm_surface_coef,
        atm_diffusion[None],
        ocn_diffusion[None],
        far=range(6),
        in_specs=[HBM] * 4 + [VM] * 2,
        scratch=[pltpu.VMEM(x.shape, x.dtype) for x in (atm_state, ocn_state, sea_mask, atm_surface_coef)] + [pltpu.SemaphoreType.DMA((4,))],
    )
    up, down = row_halos(low, high)
    beside = partner(edges)

    outgoing = call(temp_kernel, "temp_gather", 9, shape(group_size, 4, LANES), table, cells, o2a_weights[0, 0], cold=(1, 2), scratch=[pltpu.VMEM((128, SPLITS * 64), BF16)])
    incoming = exchange(outgoing)
    ocn_step = lambda *refs: ocn_kernel(False, *refs)
    ocean, ocn_edges = call(ocn_step, "ocn_step", 3, (shape(OR * OSIZE, LANES), free(OL, LANES)), ocean, up, down, beside, ocn_diff, frac, cold=(4, 5))
    incoming, ocean, ocn_edges = lax.optimization_barrier((incoming, ocean, ocn_edges))

    temp, flux_table = call(flux_kernel, "temp_scatter", 9, (shape(AR * AT, LANES), pltpu.VMEM((128, SPLITS * 48), BF16)), incoming, cols, surface, coef, far=(1,), cold=(2, 3), in_specs=[VM, HBM, VM, VM], scratch=[pltpu.VMEM((24, LANES), F32), *store])

    def atm_step(low, high, up, down, beside, *more, outs=None):
        rows = shape(ASIZE + (OSIZE if more else 0), LANES)
        outs = outs or (rows, rows, shape(AL + (OL if more else 0), LANES))
        return call(atm_kernel, "atm_step", 2.5, outs, low, high, up, down, beside, atm_diff, coef, temp, *more, cold=(5, 6, 7, 9))

    low, high, edges = atm_step(low, high, up, down, beside, ocean, ocn_edges)
    up, down = row_halos(low, high)
    beside = partner(edges)
    flux_table, low, high = lax.optimization_barrier((flux_table, low, high))

    outgoing = call(send_kernel, "flux_gather", 9, shape(group_size, 8, LANES), flux_table, cols, a2o_weights[0, 0], cold=(1, 2))
    incoming = exchange(outgoing)
    outgoing, up, down, beside = lax.optimization_barrier((outgoing, up, down, beside))
    low, high, edges = atm_step(low, high, up, down, beside)
    ocn_last_step = lambda *refs: ocn_kernel(True, *refs)
    ocean, top = call(ocn_last_step, "ocn_step", 3, (jax.ShapeDtypeStruct(ocn_state.shape, F32), free(2, 2, OR, OT * LANES)), ocean, up, down, beside, ocn_diff, frac, cold=(4, 5))
    up, down = row_halos(low, high)
    beside = partner(edges)
    incoming, ocean, top, low, high = lax.optimization_barrier((incoming, ocean, top, low, high))

    half = call(half_kernel, "forcing_half", 7.5, shape(2, 32, 256), incoming, cells, far=(1,), in_specs=[VM, HBM], scratch=store)
    half, up, down, beside = lax.optimization_barrier((half, up, down, beside))
    low, high, edges = atm_step(low, high, up, down, beside)
    up, down = row_halos(low, high)
    beside = partner(edges)
    half, low, high = lax.optimization_barrier((half, low, high))

    every = shape(2, OR * OT, LANES)
    forcing, gained, first, last = call(forcing_kernel, "forcing_scatter", 7.5, (every, every, shape(2, OT, LANES), shape(2, OT, LANES)), half, incoming, cells, frac, far=(2,), cold=(3,), in_specs=[VM, VM, HBM, VM], scratch=store)
    above, below = row_halos(first, last)
    side = partner(gained)
    forcing, up, down, beside = lax.optimization_barrier((forcing, up, down, beside))
    atm_next = atm_step(low, high, up, down, beside, outs=(jax.ShapeDtypeStruct(atm_state.shape, F32),))[0]

    line = pltpu.VMEM((OR * OT, LANES), F32)
    ocean_next = call(
        last_kernel,
        "ocn_last",
        1,
        jax.ShapeDtypeStruct(ocean.shape, F32),
        ocean,
        top,
        forcing,
        gained,
        above,
        below,
        side,
        frac,
        ocn_diff,
        in_specs=[ANY] + [VM] * 8,
        out_specs=ANY,
        scratch=[pltpu.VMEM((6 * OT, LANES), F32), line, line, pltpu.VMEM((2, 2, OR, OT * LANES), F32), pltpu.SemaphoreType.DMA],
        input_output_aliases={0: 0},
        cold=(0, 1, 7, 8),
    )
    return atm_next, ocean_next


def solution(mesh):
    across = P(None, None, GROUP, "lev")
    pairs = P("lev", GROUP, None, None)
    placed = (across, P(), P(None, GROUP, "lev"), across, P(), P(GROUP, "lev"), pairs, pairs, pairs, pairs)
    return jax.shard_map(shards, mesh=mesh, in_specs=placed, out_specs=(across, across), check_vma=False)
```
